256 devices in a mesh: tile: 64 (over x, z, core), aux: 4 (over y).
Axes of the slice: x: 4, y: 4, z: 8, core: 2. Of those that a mesh axis runs over, the one named last changes fastest.
Arguments:
- density: float32 [8192, 8192], P('tile', 'aux'), may hold values from -6 to 6
- factors: float32 [1536, 16, 128, 128], P(('tile', 'aux')), may hold values from -0.125 to 0.125
- orthogonalizers: float32 [8192, 128], replicated, may hold values from -0.5 to 0.5
- slot_pairs: int32 [8192, 2], P(('tile', 'aux')), may hold values from 0 to 5
- density_source: int32 [8192, 1], replicated, may hold values from 0 to 63; in each aligned block of 32 rows (0 to 31, 32 to 63, ...) at most 2 rows name the same one
- density_column: int32 [8192, 1], replicated, may hold values from 0 to 63
- target_row: int32 [8192, 1], replicated, may hold values from 0 to 63; in each aligned block of 32 rows (0 to 31, 32 to 63, ...) at most 2 rows name the same one
- target_column: int32 [8192, 1], replicated, may hold values from 0 to 63
Outputs:
- fock_exchange: float32 [8192, 8192], P('tile', 'aux')
The draws below stay inside these ranges and needn't reach their ends.
Inputs may be any that keep to these rules, and one draw needn't show every extreme that they name: `density_source`: in each aligned block of 32 rows (the tasks of one device) no row tile is named more than 2 times, a bound that some block reaches. `target_row`: in each aligned block of 32 rows (the tasks of one device) no row tile is named more than 2 times, a bound that some block reaches.
All inputs are finite; a program needn't handle non-finite values.
Results may differ from the reference program's by a relative error of at most 0.0001.
Values sent between devices are 32-bit elements; how exact they have to be, the bound alone decides.
A program may use at most 128 MiB of HBM per device.

```python
import math
import jax
import jax.numpy as jnp
import numpy as np
from jax import lax

TILE = 128
AUX_DEV = 16
SLOTS = 6
TASKS_DEV = 32
CAP = 2
NBF = 8192
ROWS = 8192
N_TILE = 64


def place_ends(values, stream_key, low, top_value):
    spot = [jax.random.randint(jax.random.fold_in(stream_key, axis), (), 0, length) for axis, length in enumerate(values.shape)]
    longest = values.shape.index(max(values.shape))
    neighbour = spot[:longest] + [(spot[longest] + 1) % values.shape[longest]] + spot[longest + 1:]
    return values.at[tuple(spot)].set(low).at[tuple(neighbour)].set(top_value)


def block_scale(key, dims, split, smallest, high):
    level = 1.0
    for axis_at, parts in split:
        steps = jax.random.uniform(jax.random.fold_in(jax.random.fold_in(key, 6), axis_at), (parts,), jnp.float32, smallest / len(split), high / len(split))
        level = level * jnp.repeat(jnp.exp(steps), dims[axis_at] // parts).reshape((-1,) + (1,) * (len(dims) - 1 - axis_at))
    return level


def routed_block(rng, own, number, rows, amount, top, bound, slope):
    sequence = jax.random.permutation(rng, amount)
    packed, usual = shares(amount, rows * top, bound, slope, True), shares(amount, rows * top, bound, slope, False)
    places = jnp.arange(amount)

    def named(lengths, turn):
        used = int((lengths > 0).sum())
        fixed = max(1, used // 4)
        shifted = fixed + (places - fixed + turn * (used - fixed)) % max(1, amount - fixed)
        return jnp.zeros((amount,), jnp.int32).at[sequence[jnp.where(places < fixed, places, shifted)]].set(jnp.asarray(lengths, jnp.int32))

    lengths = jnp.where(number % 4 == 0, named(packed, number // 4), named(usual, number - number // 4 - 1))
    mixed = jax.random.permutation(jax.random.fold_in(own, 3), amount)
    source_of, taker = mixed[0:amount // 2 * 2:2], mixed[1:amount // 2 * 2:2]
    margin = jnp.minimum(lengths[source_of] - 1, bound - lengths[taker]) // 2
    margin = jnp.where((source_of == sequence[0]) | (taker == sequence[0]) | (lengths[taker] == 0), 0, jnp.maximum(margin, 0))
    shifted = jax.random.randint(jax.random.fold_in(own, 4), (amount // 2,), 0, 1 << 20) % (margin + 1)
    lengths = lengths.at[source_of].add(-shifted).at[taker].add(shifted)
    labels = jnp.searchsorted(jnp.cumsum(lengths), jnp.arange(rows * top), side="right").astype(jnp.int32)
    grid = labels.reshape(top, rows).T
    grid = grid[jax.random.permutation(jax.random.fold_in(own, 1), rows)]
    turn = jax.random.randint(jax.random.fold_in(own, 2), (rows, 1), 0, top)
    return jnp.take_along_axis(grid, (jnp.arange(top)[None, :] + turn) % top, axis=1)


def shares(count, total, limit, skew, full):
    weights = [(1 << 20) // math.isqrt(standing ** skew) + 1 for standing in range(1, count + 1)]
    largest = limit if full else min(limit, max(-(-total // count), total * weights[0] // sum(weights)))
    least = 1 if total - largest >= count - 1 else 0
    holding, spare = [largest] + [least] * (count - 1), total - largest - least * (count - 1)
    while spare > 0:
        candidates = [i for i in range(1, count) if holding[i] < largest] or [i for i in range(1, count) if holding[i] < limit]
        pool, left = sum([weights[i] for i in candidates]), spare
        for i in candidates:
            extra = min(limit - holding[i], max(1, left * weights[i] // pool), spare)
            holding[i] = holding[i] + extra
            spare = spare - extra
    return np.array(holding)


def bell_draw(rng, dims, scale, bound, split=(), held_as=jnp.bfloat16):
    drawn = scale * jax.random.normal(rng, dims, jnp.float32)
    if split:
        drawn = drawn * block_scale(rng, dims, split, -0.22, 0.18)
    return jnp.clip(drawn, -bound, bound).astype(held_as)


def setup_inputs(seed: int = 0) -> dict:
    splits = jax.random.split(jax.random.key(seed), 9)
    density = bell_draw(splits[0], (NBF, NBF), 1.0, 6.0, ((0, 64), (1, 4)), jnp.float32)
    factors = bell_draw(splits[1], (ROWS // TASKS_DEV * SLOTS, AUX_DEV, TILE, TILE), (TILE * AUX_DEV) ** -0.5, 0.125, ((0, 256),), jnp.float32)
    orthogonalizers = bell_draw(splits[2], (NBF, TILE), TILE ** -0.5, 0.5, (), jnp.float32)
    slot_pairs = place_ends(jax.random.randint(splits[3], (ROWS, 2), 0, SLOTS), jax.random.fold_in(splits[3], 1), 0, SLOTS - 1).astype(jnp.int32)
    density_source_keys = jax.random.split(jax.random.fold_in(splits[4], 1), ROWS // TASKS_DEV)
    density_source_turns = jax.random.permutation(jax.random.fold_in(splits[4], 3), ROWS // TASKS_DEV)
    density_source = jax.vmap(lambda own, number: routed_block(jax.random.fold_in(splits[4], 2), own, number, TASKS_DEV, N_TILE, 1, CAP, 2))(density_source_keys, density_source_turns).reshape((ROWS, 1))
    density_column = place_ends(jax.random.randint(splits[5], (ROWS, 1), 0, N_TILE), jax.random.fold_in(splits[5], 1), 0, N_TILE - 1).astype(jnp.int32)
    target_row_keys = jax.random.split(jax.random.fold_in(splits[6], 1), ROWS // TASKS_DEV)
    target_row_turns = jax.random.permutation(jax.random.fold_in(splits[6], 3), ROWS // TASKS_DEV)
    target_row = jax.vmap(lambda own, number: routed_block(jax.random.fold_in(splits[6], 2), own, number, TASKS_DEV, N_TILE, 1, CAP, 2))(target_row_keys, target_row_turns).reshape((ROWS, 1))
    target_column = place_ends(jax.random.randint(splits[7], (ROWS, 1), 0, N_TILE), jax.random.fold_in(splits[7], 1), 0, N_TILE - 1).astype(jnp.int32)
    return {"density": density, "factors": factors, "orthogonalizers": orthogonalizers, "slot_pairs": slot_pairs, "density_source": density_source, "density_column": density_column, "target_row": target_row, "target_column": target_column}


def reference(density, factors, orthogonalizers, slot_pairs, density_source, density_column, target_row, target_column):
    highest = lax.Precision.HIGHEST
    density_tiles = density.reshape(N_TILE, TILE, N_TILE, TILE)
    rows_all = slot_pairs.shape[0]
    device_of = jnp.arange(rows_all, dtype=jnp.int32) // TASKS_DEV
    left_index = (device_of * SLOTS + slot_pairs[:, 0]).astype(jnp.int32)
    right_index = (device_of * SLOTS + slot_pairs[:, 1]).astype(jnp.int32)
    columns = (left_index, right_index, density_source[:, 0], density_column[:, 0], target_row[:, 0], target_column[:, 0])
    blocks = tuple(value.astype(jnp.int32).reshape(-1, TASKS_DEV) for value in columns)

    def step(exchange_sum, block):
        lefts, rights, rows_c, cols_d, rows_a, cols_b = block
        dens_block = density_tiles[rows_c, :, cols_d, :]
        halfway = jnp.einsum("gpik,gkl->gpil", factors[lefts], dens_block, precision=highest)
        partial_value = jnp.einsum("gpil,gplj->gij", halfway, factors[rights], precision=highest)
        return exchange_sum.at[rows_a, cols_b].add(partial_value), None

    exchange_sum = jnp.zeros((N_TILE, N_TILE, TILE, TILE), jnp.float32)
    exchange_sum, unused = lax.scan(step, exchange_sum, blocks)
    symmetric = exchange_sum + jnp.transpose(exchange_sum, (1, 0, 3, 2))
    blocks_x = orthogonalizers.reshape(N_TILE, TILE, TILE)
    leftward = jnp.einsum("aki,abkl->abil", blocks_x, symmetric, precision=highest)
    fock = jnp.einsum("abil,blj->abij", leftward, blocks_x, precision=highest)
    return jnp.transpose(fock, (0, 2, 1, 3)).reshape(N_TILE * TILE, N_TILE * TILE)
```

```python
import functools
import jax
import jax.numpy as jnp
from jax import lax
from jax.experimental import pallas as pl
from jax.experimental.pallas import tpu as pltpu
from jax.sharding import PartitionSpec as P

MESH = pl.DeviceIdType.MESH
TILE = 128
CAP = 2
VMEM_BYTES = 56 * 1024 * 1024
STRIDE = 27


def halves(x):
    top = x.astype(jnp.bfloat16)
    rest = (x - top.astype(jnp.float32)).astype(jnp.bfloat16)
    return top, rest


def ranks_of(keys):
    count = keys.shape[-1]
    spot = jnp.arange(count)
    earlier = spot[None, :] < spot[:, None]
    return jnp.sum((keys[..., :, None] == keys[..., None, :]) & earlier, axis=-1).astype(jnp.int32)


def slot_columns(keys, columns, wanted):
    ranking = ranks_of(keys)
    picked = []
    for level in range(CAP):
        chosen = (keys == wanted) & (ranking == level)
        picked.append(jnp.sum(jnp.where(chosen, columns + 1, 0), axis=-1) - 1)
    return jnp.stack(picked, axis=-1)


def density_kernel(n_tile, n_aux, cols_ref, dens_ref, out_ref, slab, outgoing, y_send, y_recv, t_send, t_recv, own_sem):
    me = lax.axis_index("tile")
    aux = lax.axis_index("aux")
    up, down = lax.rem(aux + 1, n_aux), lax.rem(aux + n_aux - 1, n_aux)
    per = dens_ref.shape[1] // TILE
    half = per // 2
    barrier = pltpu.get_barrier_semaphore()

    @pl.loop(1, n_tile)
    def _(s):
        pl.semaphore_signal(barrier, inc=1, device_id={"tile": lax.rem(me + s, n_tile), "aux": aux}, device_id_type=MESH)

    for other in (up, down):
        pl.semaphore_signal(barrier, inc=1, device_id={"tile": me, "aux": other}, device_id_type=MESH)
    pl.semaphore_wait(barrier, n_tile + 1)

    def near(src, dst, index, other):
        return pltpu.make_async_remote_copy(
            src_ref=src, dst_ref=dst, send_sem=y_send.at[index], recv_sem=y_recv.at[index],
            device_id={"tile": me, "aux": other}, device_id_type=MESH)

    for j in range(per):
        slab[aux * per + j] = dens_ref[:, j * TILE:(j + 1) * TILE]

    def part(owner, start, length):
        return slab.at[pl.ds(owner * per + start, length)]

    across = lax.rem(aux + 2, n_aux)
    first_up = near(part(aux, 0, per), part(aux, 0, per), 0, up)
    first_down = near(part(aux, 0, per), part(aux, 0, per), 1, down)
    first_up.start()
    first_down.start()
    near(part(down, 0, per), part(down, 0, per), 0, up).wait_recv()
    second_up = near(part(down, 0, half), part(down, 0, half), 2, up)
    second_up.start()
    near(part(up, 0, per), part(up, 0, per), 1, down).wait_recv()
    second_down = near(part(up, half, half), part(up, half, half), 3, down)
    second_down.start()
    near(part(across, 0, half), part(across, 0, half), 2, up).wait_recv()
    near(part(across, half, half), part(across, half, half), 3, down).wait_recv()

    def pick(dest):
        for level in range(CAP):
            outgoing[dest, level] = slab[cols_ref[dest, level]]

    def far(s):
        offset = lax.rem(s * STRIDE, n_tile)
        dest = lax.rem(me + offset, n_tile)
        return dest, pltpu.make_async_remote_copy(
            src_ref=outgoing.at[dest], dst_ref=out_ref.at[me], send_sem=t_send.at[s], recv_sem=t_recv.at[s],
            device_id={"tile": dest, "aux": aux}, device_id_type=MESH)

    @pl.loop(1, n_tile)
    def _(s):
        dest, copy = far(s)
        pick(dest)
        copy.start()

    pick(me)
    own = pltpu.make_async_copy(outgoing.at[me], out_ref.at[me], own_sem)
    own.start()

    @pl.loop(1, n_tile)
    def _(s):
        offset = lax.rem(s * STRIDE, n_tile)
        source = lax.rem(me + n_tile - offset, n_tile)
        pltpu.make_async_remote_copy(
            src_ref=outgoing.at[me], dst_ref=out_ref.at[source], send_sem=t_send.at[s], recv_sem=t_recv.at[s],
            device_id={"tile": source, "aux": aux}, device_id_type=MESH).wait_recv()

    @pl.loop(1, n_tile)
    def _(s):
        far(s)[1].wait_send()

    own.wait()
    for copy in (first_up, first_down, second_up, second_down):
        copy.wait_send()


def fetch_density(density, cols, n_tile, n_aux):
    return pl.pallas_call(
        functools.partial(density_kernel, n_tile, n_aux),
        out_shape=jax.ShapeDtypeStruct((n_tile, CAP, TILE, TILE), jnp.float32),
        in_specs=[pl.BlockSpec(memory_space=pltpu.SMEM), pl.BlockSpec(memory_space=pltpu.VMEM)],
        out_specs=pl.BlockSpec(memory_space=pl.ANY),
        scratch_shapes=[
            pltpu.VMEM((n_tile, TILE, TILE), jnp.float32),
            pltpu.VMEM((n_tile, CAP, TILE, TILE), jnp.float32),
            pltpu.SemaphoreType.DMA((4,)),
            pltpu.SemaphoreType.DMA((4,)),
            pltpu.SemaphoreType.DMA((n_tile,)),
            pltpu.SemaphoreType.DMA((n_tile,)),
            pltpu.SemaphoreType.DMA,
        ],
        compiler_params=pltpu.CompilerParams(collective_id=0, has_side_effects=True, vmem_limit_bytes=VMEM_BYTES),
        name="fetch_density",
    )(cols, density)


def task_kernel(pair_count, table, dens_ref, fact_ref, out_ref, split):
    q = pl.program_id(0)

    @pl.when(q == 0)
    def _():
        @pl.loop(0, fact_ref.shape[0])
        def _(slot):
            @pl.loop(0, pair_count)
            def _(p):
                rows = pl.ds(pl.multiple_of(p * 2 * TILE, 2 * TILE), 2 * TILE)
                top, rest = halves(fact_ref[slot, rows, :])
                split[slot, rows, 0:TILE] = top
                split[slot, rows, TILE:2 * TILE] = rest

    left, right = table[1, q], table[2, q]
    top, rest = halves(dens_ref[0])
    row = jnp.concatenate([top, rest], axis=1)
    weights = jnp.concatenate([row, row], axis=0)
    total = jnp.zeros((2 * TILE, 2 * TILE), jnp.float32)
    for p in range(pair_count):
        rows = slice(p * 2 * TILE, (p + 1) * 2 * TILE)
        wide = jnp.dot(split[left, rows, :], weights, preferred_element_type=jnp.float32)
        top, rest = halves(wide[:, :TILE] + wide[:, TILE:])
        lhs = jnp.concatenate(
            [jnp.concatenate([top[:TILE], top[TILE:]], axis=1), jnp.concatenate([rest[:TILE], rest[TILE:]], axis=1)], axis=0)
        total = total + jnp.dot(lhs, split[right, rows, :], preferred_element_type=jnp.float32)
    tall = total[:, :TILE] + total[:, TILE:]
    out_ref[0] = tall[:TILE] + tall[TILE:]


def run_tasks(table, incoming, factors, slots):
    slot_count, aux_funcs = factors.shape[:2]
    flat = factors.reshape(slot_count, aux_funcs * TILE, TILE)
    task_count = table.shape[1]
    return pl.pallas_call(
        functools.partial(task_kernel, aux_funcs // 2),
        out_shape=jax.ShapeDtypeStruct((slots, TILE, TILE), jnp.float32),
        grid_spec=pltpu.PrefetchScalarGridSpec(
            num_scalar_prefetch=1,
            grid=(task_count,),
            in_specs=[
                pl.BlockSpec((1, TILE, TILE), lambda q, t: (t[0, q], 0, 0)),
                pl.BlockSpec(flat.shape, lambda q, t: (0, 0, 0), pipeline_mode=pl.Buffered(1)),
            ],
            out_specs=pl.BlockSpec((1, TILE, TILE), lambda q, t: (t[3, q], 0, 0)),
            scratch_shapes=[pltpu.VMEM((slot_count, aux_funcs * TILE, 2 * TILE), jnp.bfloat16)],
        ),
        compiler_params=pltpu.CompilerParams(vmem_limit_bytes=VMEM_BYTES),
        name="run_tasks",
    )(table, incoming, flat)


def return_kernel(n_tile, src_ref, out_ref, t_send, t_recv, own_sem):
    me = lax.axis_index("tile")
    aux = lax.axis_index("aux")
    barrier = pltpu.get_barrier_semaphore()

    @pl.loop(1, n_tile)
    def _(s):
        pl.semaphore_signal(barrier, inc=1, device_id={"tile": lax.rem(me + s, n_tile), "aux": aux}, device_id_type=MESH)

    pl.semaphore_wait(barrier, n_tile - 1)

    def far(s):
        dest = lax.rem(me + lax.rem(s * STRIDE, n_tile), n_tile)
        return pltpu.make_async_remote_copy(
            src_ref=src_ref.at[dest], dst_ref=out_ref.at[me], send_sem=t_send.at[s], recv_sem=t_recv.at[s],
            device_id={"tile": dest, "aux": aux}, device_id_type=MESH)

    @pl.loop(1, n_tile)
    def _(s):
        far(s).start()

    own = pltpu.make_async_copy(src_ref.at[me], out_ref.at[me], own_sem)
    own.start()

    @pl.loop(1, n_tile)
    def _(s):
        source = lax.rem(me + n_tile - lax.rem(s * STRIDE, n_tile), n_tile)
        pltpu.make_async_remote_copy(
            src_ref=src_ref.at[me], dst_ref=out_ref.at[source], send_sem=t_send.at[s], recv_sem=t_recv.at[s],
            device_id={"tile": source, "aux": aux}, device_id_type=MESH).wait_recv()

    @pl.loop(1, n_tile)
    def _(s):
        far(s).wait_send()

    own.wait()


def return_partials(outbound, n_tile):
    return pl.pallas_call(
        functools.partial(return_kernel, n_tile),
        out_shape=jax.ShapeDtypeStruct(outbound.shape, jnp.float32),
        in_specs=[pl.BlockSpec(memory_space=pl.ANY)],
        out_specs=pl.BlockSpec(memory_space=pl.ANY),
        scratch_shapes=[
            pltpu.SemaphoreType.DMA((n_tile,)),
            pltpu.SemaphoreType.DMA((n_tile,)),
            pltpu.SemaphoreType.DMA,
        ],
        compiler_params=pltpu.CompilerParams(collective_id=1, has_side_effects=True),
        name="return_partials",
    )(outbound)


def sum_kernel(group, cols, tiles_ref, out_ref):
    step = pl.program_id(0)

    @pl.when(step == 0)
    def _():
        @pl.loop(0, out_ref.shape[0])
        def _(b):
            out_ref[b] = jnp.zeros((TILE, TILE), jnp.float32)

    for i in range(group):
        col = cols[step * group + i]

        @pl.when(col >= 0)
        def _():
            out_ref[col] = out_ref[col] + tiles_ref[i]


def sum_rows(cols, arrived, n_tile):
    group = 16
    count = arrived.shape[0]
    return pl.pallas_call(
        functools.partial(sum_kernel, group),
        out_shape=jax.ShapeDtypeStruct((n_tile, TILE, TILE), jnp.float32),
        grid_spec=pltpu.PrefetchScalarGridSpec(
            num_scalar_prefetch=1,
            grid=(count // group,),
            in_specs=[pl.BlockSpec((group, TILE, TILE), lambda s, t: (s, 0, 0))],
            out_specs=pl.BlockSpec((n_tile, TILE, TILE), lambda s, t: (0, 0, 0)),
        ),
        compiler_params=pltpu.CompilerParams(vmem_limit_bytes=VMEM_BYTES),
        name="sum_rows",
    )(cols, arrived)


def mirror_kernel(n_tile, n_aux, rows_ref, own_ref, mirror_ref, half_up, half_down, full_up, full_down, outgoing,
                  summed, y_send, y_recv, m_send, m_recv, out_sem):
    me = lax.axis_index("tile")
    aux = lax.axis_index("aux")
    up, down = lax.rem(aux + 1, n_aux), lax.rem(aux + n_aux - 1, n_aux)
    across = lax.rem(aux + 2, n_aux)
    per = n_tile // n_aux
    half = per // 2
    block = me // per
    slot = lax.rem(me, per)
    alike = block == aux
    barrier = pltpu.get_barrier_semaphore()
    for other in (up, down):
        pl.semaphore_signal(barrier, inc=1, device_id={"tile": me, "aux": other}, device_id_type=MESH)

    @pl.loop(0, per)
    def _(j):
        @pl.when(jnp.logical_not(alike & (j == slot)))
        def _():
            pl.semaphore_signal(barrier, inc=1, device_id={"tile": aux * per + j, "aux": block}, device_id_type=MESH)

    pl.semaphore_wait(barrier, jnp.where(alike, per + 1, per + 2))

    def near(src, dst, index, other):
        return pltpu.make_async_remote_copy(
            src_ref=src, dst_ref=dst, send_sem=y_send.at[index], recv_sem=y_recv.at[index],
            device_id={"tile": me, "aux": other}, device_id_type=MESH)

    first_up = near(rows_ref.at[pl.ds(across * per, half)], half_up, 0, up)
    first_down = near(rows_ref.at[pl.ds(across * per + half, half)], half_down, 1, down)
    first_up.start()
    first_down.start()

    @pl.loop(0, per)
    def _(j):
        outgoing[0, j] = rows_ref[up * per + j]
        outgoing[1, j] = rows_ref[down * per + j]

    first_up.wait_recv()

    @pl.loop(0, half)
    def _(j):
        outgoing[0, j] = outgoing[0, j] + half_up[j]

    second_up = near(outgoing.at[0], full_up, 2, up)
    second_up.start()
    first_down.wait_recv()

    @pl.loop(0, half)
    def _(j):
        outgoing[1, half + j] = outgoing[1, half + j] + half_down[j]

    second_down = near(outgoing.at[1], full_down, 3, down)
    second_down.start()
    second_up.wait_recv()
    second_down.wait_recv()

    def send(j):
        return pltpu.make_async_remote_copy(
            src_ref=summed.at[j], dst_ref=mirror_ref.at[slot], send_sem=m_send.at[j], recv_sem=m_recv.at[slot],
            device_id={"tile": aux * per + j, "aux": block}, device_id_type=MESH)

    def keep(j):
        return pltpu.make_async_copy(summed.at[j], mirror_ref.at[j], m_send.at[j])

    @pl.loop(0, per)
    def _(j):
        summed[j] = rows_ref[aux * per + j] + (full_up[j] + full_down[j])
        mine = alike & (j == slot)

        @pl.when(jnp.logical_not(mine))
        def _():
            send(j).start()

        @pl.when(mine)
        def _():
            keep(j).start()

    out_copy = pltpu.make_async_copy(summed, own_ref, out_sem)
    out_copy.start()

    @pl.loop(0, per)
    def _(j):
        mine = alike & (j == slot)

        @pl.when(jnp.logical_not(mine))
        def _():
            pltpu.make_async_remote_copy(
                src_ref=summed.at[j], dst_ref=mirror_ref.at[j], send_sem=m_send.at[j], recv_sem=m_recv.at[j],
                device_id={"tile": aux * per + j, "aux": block}, device_id_type=MESH).wait_recv()
            send(j).wait_send()

        @pl.when(mine)
        def _():
            keep(j).wait()

    out_copy.wait()
    for copy in (first_up, first_down, second_up, second_down):
        copy.wait_send()


def exchange_mirror(rows, n_tile, n_aux):
    per = n_tile // n_aux
    tiles = lambda *lead: pltpu.VMEM(lead + (TILE, TILE), jnp.float32)
    shape = jax.ShapeDtypeStruct((per, TILE, TILE), jnp.float32)
    return pl.pallas_call(
        functools.partial(mirror_kernel, n_tile, n_aux),
        out_shape=(shape, shape),
        in_specs=[pl.BlockSpec(memory_space=pltpu.VMEM)],
        out_specs=(pl.BlockSpec(memory_space=pl.ANY), pl.BlockSpec(memory_space=pl.ANY)),
        scratch_shapes=[
            tiles(per // 2), tiles(per // 2), tiles(per), tiles(per), tiles(2, per), tiles(per),
            pltpu.SemaphoreType.DMA((4,)),
            pltpu.SemaphoreType.DMA((4,)),
            pltpu.SemaphoreType.DMA((per,)),
            pltpu.SemaphoreType.DMA((per,)),
            pltpu.SemaphoreType.DMA,
        ],
        compiler_params=pltpu.CompilerParams(collective_id=2, has_side_effects=True, vmem_limit_bytes=VMEM_BYTES),
        name="exchange_mirror",
    )(rows)


def finish_kernel(place, own_ref, mirror_ref, left_ref, right_ref, out_ref):
    symmetric = own_ref[0] + jnp.transpose(mirror_ref[0])
    dims = (((0,), (0,)), ((), ()))
    leftward = lax.dot_general(left_ref[...], symmetric, dims, precision=lax.Precision.HIGHEST,
                               preferred_element_type=jnp.float32)
    out_ref[...] = jnp.dot(leftward, right_ref[...], precision=lax.Precision.HIGHEST,
                           preferred_element_type=jnp.float32)


def finish(place, own, mirror, orthogonalizers):
    per = own.shape[0]
    tile = pl.BlockSpec((1, TILE, TILE), lambda j, t: (j, 0, 0))
    return pl.pallas_call(
        finish_kernel,
        out_shape=jax.ShapeDtypeStruct((TILE, per * TILE), jnp.float32),
        grid_spec=pltpu.PrefetchScalarGridSpec(
            num_scalar_prefetch=1,
            grid=(per,),
            in_specs=[
                tile, tile,
                pl.BlockSpec((TILE, TILE), lambda j, t: (t[0], 0)),
                pl.BlockSpec((TILE, TILE), lambda j, t: (t[1] * per + j, 0)),
            ],
            out_specs=pl.BlockSpec((TILE, TILE), lambda j, t: (0, j)),
        ),
        name="finish",
    )(place, own, mirror, orthogonalizers, orthogonalizers)


def local(density, factors, orthogonalizers, slot_pairs, density_source, density_column, target_row, target_column):
    n_tile, n_aux = lax.axis_size("tile"), lax.axis_size("aux")
    me, aux = lax.axis_index("tile"), lax.axis_index("aux")
    tasks = slot_pairs.shape[0]

    def group(rows):
        grid = rows.reshape(n_tile, n_aux, tasks)
        return lax.dynamic_index_in_dim(grid, aux, 1, False)

    sources, columns = group(density_source), group(density_column)
    targets, target_cols = group(target_row), group(target_column)
    own_source = lax.dynamic_index_in_dim(sources, me, 0, False)
    own_target = lax.dynamic_index_in_dim(targets, me, 0, False)
    send_cols = slot_columns(sources, columns, me)
    sum_cols = slot_columns(targets, target_cols, me).reshape(-1)
    table = jnp.stack([
        own_source * CAP + ranks_of(own_source),
        slot_pairs[:, 0],
        slot_pairs[:, 1],
        own_target * CAP + ranks_of(own_target),
    ])
    slots = n_tile * CAP
    incoming = fetch_density(density, jnp.maximum(send_cols, 0), n_tile, n_aux)
    outbound = run_tasks(table, incoming.reshape(slots, TILE, TILE), factors, slots)
    arrived = return_partials(outbound.reshape(n_tile, CAP, TILE, TILE), n_tile)
    rows = sum_rows(sum_cols, arrived.reshape(slots, TILE, TILE), n_tile)
    own, mirror = exchange_mirror(rows, n_tile, n_aux)
    return finish(jnp.stack([me, aux]).astype(jnp.int32), own, mirror, orthogonalizers)


def solution(mesh):
    return jax.shard_map(
        local,
        mesh=mesh,
        in_specs=(
            P("tile", "aux"),
            P(("tile", "aux"), None, None, None),
            P(),
            P(("tile", "aux"), None),
            P(),
            P(),
            P(),
            P(),
        ),
        out_specs=P("tile", "aux"),
        check_vma=False,
    )
```

```python
import functools
import jax
import jax.numpy as jnp
from jax import lax
from jax.experimental import pallas as pl
from jax.experimental.pallas import tpu as pltpu
from jax.sharding import PartitionSpec as P

MESH = pl.DeviceIdType.MESH
TILE = 128
CAP = 2
VMEM_BYTES = 56 * 1024 * 1024
STRIDE = 27
CHUNKS = 4
STRIP = TILE // CHUNKS
AHEAD = 2


def halves(x):
    top = x.astype(jnp.bfloat16)
    rest = (x - top.astype(jnp.float32)).astype(jnp.bfloat16)
    return top, rest


def ranks_of(keys):
    count = keys.shape[-1]
    spot = jnp.arange(count)
    earlier = spot[None, :] < spot[:, None]
    return jnp.sum((keys[..., :, None] == keys[..., None, :]) & earlier, axis=-1).astype(jnp.int32)


def slot_columns(keys, columns, wanted):
    ranking = ranks_of(keys)
    picked = []
    for level in range(CAP):
        chosen = (keys == wanted) & (ranking == level)
        picked.append(jnp.sum(jnp.where(chosen, columns + 1, 0), axis=-1) - 1)
    return jnp.stack(picked, axis=-1)


def density_kernel(n_tile, n_aux, cols_ref, dens_ref, out_ref, *scratch):
    slabs, outgoing = scratch[:CHUNKS], scratch[CHUNKS]
    y_send, y_recv, t_send, t_recv, own_sem = scratch[CHUNKS + 1:]
    me = lax.axis_index("tile")
    aux = lax.axis_index("aux")
    up, down = lax.rem(aux + 1, n_aux), lax.rem(aux + n_aux - 1, n_aux)
    across = lax.rem(aux + 2, n_aux)
    per = dens_ref.shape[1] // TILE
    half = per // 2
    barrier = pltpu.get_barrier_semaphore()

    @pl.loop(1, n_tile)
    def _(s):
        pl.semaphore_signal(barrier, inc=1, device_id={"tile": lax.rem(me + s, n_tile), "aux": aux}, device_id_type=MESH)

    for other in (up, down):
        pl.semaphore_signal(barrier, inc=1, device_id={"tile": me, "aux": other}, device_id_type=MESH)
    for r in range(CHUNKS):
        for j in range(per):
            slabs[r][aux * per + j] = dens_ref[r * STRIP:(r + 1) * STRIP, j * TILE:(j + 1) * TILE]
    pl.semaphore_wait(barrier, n_tile + 1)

    def near(r, owner, start, length, index, other):
        where = slabs[r].at[pl.ds(owner * per + start, length)]
        return pltpu.make_async_remote_copy(
            src_ref=where, dst_ref=where, send_sem=y_send.at[r, index], recv_sem=y_recv.at[r, index],
            device_id={"tile": me, "aux": other}, device_id_type=MESH)

    def far(r, s):
        dest = lax.rem(me + lax.rem(s * STRIDE, n_tile), n_tile)
        return dest, pltpu.make_async_remote_copy(
            src_ref=outgoing.at[r, dest], dst_ref=out_ref.at[me, :, pl.ds(r * STRIP, STRIP)],
            send_sem=t_send.at[r, s], recv_sem=t_recv.at[r, s],
            device_id={"tile": dest, "aux": aux}, device_id_type=MESH)

    def own(r):
        return pltpu.make_async_copy(outgoing.at[r, me], out_ref.at[me, :, pl.ds(r * STRIP, STRIP)], own_sem.at[r])

    def first(r):
        near(r, aux, 0, per, 0, up).start()
        near(r, aux, 0, per, 1, down).start()

    first(0)
    for r in range(CHUNKS):
        if r + 1 < CHUNKS:
            first(r + 1)
        near(r, down, 0, per, 0, up).wait_recv()
        near(r, down, 0, half, 2, up).start()
        near(r, up, 0, per, 1, down).wait_recv()
        near(r, up, half, half, 3, down).start()
        near(r, across, 0, half, 2, up).wait_recv()
        near(r, across, half, half, 3, down).wait_recv()

        def pick(dest):
            for level in range(CAP):
                outgoing[r, dest, level] = slabs[r][cols_ref[dest, level]]

        @pl.loop(1, n_tile)
        def _(s):
            dest, copy = far(r, s)
            pick(dest)
            copy.start()

        pick(me)
        own(r).start()

    for r in range(CHUNKS):
        @pl.loop(1, n_tile)
        def _(s):
            source = lax.rem(me + n_tile - lax.rem(s * STRIDE, n_tile), n_tile)
            pltpu.make_async_remote_copy(
                src_ref=outgoing.at[r, me], dst_ref=out_ref.at[source, :, pl.ds(r * STRIP, STRIP)],
                send_sem=t_send.at[r, s], recv_sem=t_recv.at[r, s],
                device_id={"tile": source, "aux": aux}, device_id_type=MESH).wait_recv()
            far(r, s)[1].wait_send()

        own(r).wait()
        near(r, aux, 0, per, 0, up).wait_send()
        near(r, aux, 0, per, 1, down).wait_send()
        near(r, down, 0, half, 2, up).wait_send()
        near(r, up, half, half, 3, down).wait_send()


def fetch_density(density, cols, n_tile, n_aux):
    return pl.pallas_call(
        functools.partial(density_kernel, n_tile, n_aux),
        out_shape=jax.ShapeDtypeStruct((n_tile, CAP, TILE, TILE), jnp.float32),
        in_specs=[pl.BlockSpec(memory_space=pltpu.SMEM), pl.BlockSpec(memory_space=pltpu.VMEM)],
        out_specs=pl.BlockSpec(memory_space=pl.ANY),
        scratch_shapes=[pltpu.VMEM((n_tile, STRIP, TILE), jnp.float32)] * CHUNKS + [
            pltpu.VMEM((CHUNKS, n_tile, CAP, STRIP, TILE), jnp.float32),
            pltpu.SemaphoreType.DMA((CHUNKS, 4)),
            pltpu.SemaphoreType.DMA((CHUNKS, 4)),
            pltpu.SemaphoreType.DMA((CHUNKS, n_tile)),
            pltpu.SemaphoreType.DMA((CHUNKS, n_tile)),
            pltpu.SemaphoreType.DMA((CHUNKS,)),
        ],
        compiler_params=pltpu.CompilerParams(collective_id=0, has_side_effects=True, vmem_limit_bytes=VMEM_BYTES),
        name="fetch_density",
    )(cols, density)


def task_kernel(pair_count, table, dens_ref, fact_ref, out_ref, split):
    q = pl.program_id(0)

    @pl.when(q == 0)
    def _():
        @pl.loop(0, fact_ref.shape[0])
        def _(slot):
            @pl.loop(0, pair_count)
            def _(p):
                rows = pl.ds(pl.multiple_of(p * 2 * TILE, 2 * TILE), 2 * TILE)
                top, rest = halves(fact_ref[slot, rows, :])
                split[slot, rows, 0:TILE] = top
                split[slot, rows, TILE:2 * TILE] = rest

    left, right = table[1, q], table[2, q]
    top, rest = halves(dens_ref[0])
    row = jnp.concatenate([top, rest], axis=1)
    weights = jnp.concatenate([row, row], axis=0)
    total = jnp.zeros((2 * TILE, 2 * TILE), jnp.float32)
    for p in range(pair_count):
        rows = slice(p * 2 * TILE, (p + 1) * 2 * TILE)
        wide = jnp.dot(split[left, rows, :], weights, preferred_element_type=jnp.float32)
        top, rest = halves(wide[:, :TILE] + wide[:, TILE:])
        lhs = jnp.concatenate(
            [jnp.concatenate([top[:TILE], top[TILE:]], axis=1), jnp.concatenate([rest[:TILE], rest[TILE:]], axis=1)], axis=0)
        total = total + jnp.dot(lhs, split[right, rows, :], preferred_element_type=jnp.float32)
    tall = total[:, :TILE] + total[:, TILE:]
    out_ref[0] = tall[:TILE] + tall[TILE:]


def run_tasks(table, incoming, factors, slots):
    slot_count, aux_funcs = factors.shape[:2]
    flat = factors.reshape(slot_count, aux_funcs * TILE, TILE)
    task_count = table.shape[1]
    return pl.pallas_call(
        functools.partial(task_kernel, aux_funcs // 2),
        out_shape=jax.ShapeDtypeStruct((slots, TILE, TILE), jnp.float32),
        grid_spec=pltpu.PrefetchScalarGridSpec(
            num_scalar_prefetch=1,
            grid=(task_count,),
            in_specs=[
                pl.BlockSpec((1, TILE, TILE), lambda q, t: (t[0, q], 0, 0)),
                pl.BlockSpec(flat.shape, lambda q, t: (0, 0, 0), pipeline_mode=pl.Buffered(1)),
            ],
            out_specs=pl.BlockSpec((1, TILE, TILE), lambda q, t: (t[3, q], 0, 0)),
            scratch_shapes=[pltpu.VMEM((slot_count, aux_funcs * TILE, 2 * TILE), jnp.bfloat16)],
        ),
        compiler_params=pltpu.CompilerParams(vmem_limit_bytes=VMEM_BYTES),
        name="run_tasks",
    )(table, incoming, flat)


def return_kernel(n_tile, n_aux, order_ref, src_ref, own_ref, mirror_ref, *scratch):
    arrived = scratch[:CHUNKS]
    (running, rows, half_up, half_down, full_up, full_down, outgoing, summed,
     t_send, t_recv, y_send, y_recv, m_send, m_recv, own_sem, out_sem) = scratch[CHUNKS:]
    me = lax.axis_index("tile")
    aux = lax.axis_index("aux")
    up, down = lax.rem(aux + 1, n_aux), lax.rem(aux + n_aux - 1, n_aux)
    across = lax.rem(aux + 2, n_aux)
    per = n_tile // n_aux
    half = per // 2
    block = me // per
    slot = lax.rem(me, per)
    alike = block == aux
    slots = n_tile * CAP
    barrier = pltpu.get_barrier_semaphore()

    @pl.loop(1, n_tile)
    def _(s):
        pl.semaphore_signal(barrier, inc=1, device_id={"tile": lax.rem(me + s, n_tile), "aux": aux}, device_id_type=MESH)

    for other in (up, down):
        pl.semaphore_signal(barrier, inc=1, device_id={"tile": me, "aux": other}, device_id_type=MESH)

    @pl.loop(0, per)
    def _(j):
        @pl.when(jnp.logical_not(alike & (j == slot)))
        def _():
            pl.semaphore_signal(barrier, inc=1, device_id={"tile": aux * per + j, "aux": block}, device_id_type=MESH)

    pl.semaphore_wait(barrier, n_tile + jnp.where(alike, per, per + 1))

    def far(r, s):
        dest = lax.rem(me + lax.rem(s * STRIDE, n_tile), n_tile)
        return pltpu.make_async_remote_copy(
            src_ref=src_ref.at[dest, :, pl.ds(r * STRIP, STRIP)], dst_ref=arrived[r].at[pl.ds(me * CAP, CAP)],
            send_sem=t_send.at[r, s], recv_sem=t_recv.at[r, s],
            device_id={"tile": dest, "aux": aux}, device_id_type=MESH)

    def own(r):
        return pltpu.make_async_copy(
            src_ref.at[me, :, pl.ds(r * STRIP, STRIP)], arrived[r].at[pl.ds(me * CAP, CAP)], own_sem.at[r])

    def begin(r):
        @pl.loop(1, n_tile)
        def _(s):
            far(r, s).start()

        own(r).start()

    def near(src, dst, r, index, other):
        return pltpu.make_async_remote_copy(
            src_ref=src, dst_ref=dst, send_sem=y_send.at[r, index], recv_sem=y_recv.at[r, index],
            device_id={"tile": me, "aux": other}, device_id_type=MESH)

    def steps(r):
        return (
            near(rows.at[r, pl.ds(across * per, half)], half_up.at[r], r, 0, up),
            near(rows.at[r, pl.ds(across * per + half, half)], half_down.at[r], r, 1, down),
            near(outgoing.at[r, 0], full_up.at[r], r, 2, up),
            near(outgoing.at[r, 1], full_down.at[r], r, 3, down),
        )

    def send(r, j):
        return pltpu.make_async_remote_copy(
            src_ref=summed.at[r, j], dst_ref=mirror_ref.at[slot, pl.ds(r * STRIP, STRIP)],
            send_sem=m_send.at[r, j], recv_sem=m_recv.at[r, slot],
            device_id={"tile": aux * per + j, "aux": block}, device_id_type=MESH)

    def keep(r, j):
        return pltpu.make_async_copy(summed.at[r, j], mirror_ref.at[j, pl.ds(r * STRIP, STRIP)], m_send.at[r, j])

    def settle(r):
        return pltpu.make_async_copy(summed.at[r], own_ref.at[:, pl.ds(r * STRIP, STRIP)], out_sem.at[r])

    for r in range(AHEAD):
        begin(r)
    for r in range(CHUNKS):
        @pl.loop(1, n_tile)
        def _(s):
            source = lax.rem(me + n_tile - lax.rem(s * STRIDE, n_tile), n_tile)
            pltpu.make_async_remote_copy(
                src_ref=src_ref.at[me, :, pl.ds(r * STRIP, STRIP)], dst_ref=arrived[r].at[pl.ds(source * CAP, CAP)],
                send_sem=t_send.at[r, s], recv_sem=t_recv.at[r, s],
                device_id={"tile": source, "aux": aux}, device_id_type=MESH).wait_recv()

        own(r).wait()

        def add(i, carry):
            for u in range(4):
                k = i * 4 + u
                carry = jnp.where(order_ref[1, k] > 0, 0.0, carry) + arrived[r][order_ref[0, k]]
                running[k] = carry
            return carry

        lax.fori_loop(0, slots // 4, add, jnp.zeros((STRIP, TILE), jnp.float32))

        @pl.loop(0, n_tile)
        def _(b):
            rows[r, b] = jnp.where(order_ref[3, b] > 0, running[order_ref[2, b]], 0.0)

        first_up, first_down, second_up, second_down = steps(r)
        first_up.start()
        first_down.start()
        if r + AHEAD < CHUNKS:
            begin(r + AHEAD)

        @pl.loop(0, half)
        def _(j):
            outgoing[r, 0, half + j] = rows[r, up * per + half + j]
            outgoing[r, 1, j] = rows[r, down * per + j]

        first_up.wait_recv()

        @pl.loop(0, half)
        def _(j):
            outgoing[r, 0, j] = rows[r, up * per + j] + half_up[r, j]

        second_up.start()
        first_down.wait_recv()

        @pl.loop(0, half)
        def _(j):
            outgoing[r, 1, half + j] = rows[r, down * per + half + j] + half_down[r, j]

        second_down.start()
        second_up.wait_recv()
        second_down.wait_recv()

        @pl.loop(0, per)
        def _(j):
            summed[r, j] = rows[r, aux * per + j] + (full_up[r, j] + full_down[r, j])
            mine = alike & (j == slot)

            @pl.when(jnp.logical_not(mine))
            def _():
                send(r, j).start()

            @pl.when(mine)
            def _():
                keep(r, j).start()

        settle(r).start()

    for r in range(CHUNKS):
        @pl.loop(1, n_tile)
        def _(s):
            far(r, s).wait_send()

        @pl.loop(0, per)
        def _(j):
            mine = alike & (j == slot)

            @pl.when(jnp.logical_not(mine))
            def _():
                pltpu.make_async_remote_copy(
                    src_ref=summed.at[r, j], dst_ref=mirror_ref.at[j, pl.ds(r * STRIP, STRIP)],
                    send_sem=m_send.at[r, j], recv_sem=m_recv.at[r, j],
                    device_id={"tile": aux * per + j, "aux": block}, device_id_type=MESH).wait_recv()
                send(r, j).wait_send()

            @pl.when(mine)
            def _():
                keep(r, j).wait()

        settle(r).wait()
        for copy in steps(r):
            copy.wait_send()


def return_partials(order, outbound, n_tile, n_aux):
    per = n_tile // n_aux
    strips = lambda *lead: pltpu.VMEM(lead + (STRIP, TILE), jnp.float32)
    shape = jax.ShapeDtypeStruct((per, TILE, TILE), jnp.float32)
    return pl.pallas_call(
        functools.partial(return_kernel, n_tile, n_aux),
        out_shape=(shape, shape),
        in_specs=[pl.BlockSpec(memory_space=pltpu.SMEM), pl.BlockSpec(memory_space=pl.ANY)],
        out_specs=(pl.BlockSpec(memory_space=pl.ANY), pl.BlockSpec(memory_space=pl.ANY)),
        scratch_shapes=[strips(n_tile * CAP)] * CHUNKS + [
            strips(n_tile * CAP), strips(CHUNKS, n_tile),
            strips(CHUNKS, per // 2), strips(CHUNKS, per // 2), strips(CHUNKS, per), strips(CHUNKS, per),
            strips(CHUNKS, 2, per), strips(CHUNKS, per),
            pltpu.SemaphoreType.DMA((CHUNKS, n_tile)),
            pltpu.SemaphoreType.DMA((CHUNKS, n_tile)),
            pltpu.SemaphoreType.DMA((CHUNKS, 4)),
            pltpu.SemaphoreType.DMA((CHUNKS, 4)),
            pltpu.SemaphoreType.DMA((CHUNKS, per)),
            pltpu.SemaphoreType.DMA((CHUNKS, per)),
            pltpu.SemaphoreType.DMA((CHUNKS,)),
            pltpu.SemaphoreType.DMA((CHUNKS,)),
        ],
        compiler_params=pltpu.CompilerParams(collective_id=1, has_side_effects=True, vmem_limit_bytes=VMEM_BYTES),
        name="return_partials",
    )(order, outbound)


def stacked(x, axis):
    return jnp.concatenate(halves(x), axis=axis)


def folded(x):
    tall = x[:, :TILE] + x[:, TILE:]
    return tall[:TILE] + tall[TILE:]


def finish_kernel(group, place, own_ref, mirror_ref, left_ref, right_ref, out_ref):
    left = stacked(jnp.transpose(left_ref[...]), 0)
    for i in range(group):
        symmetric = own_ref[i] + jnp.transpose(mirror_ref[i])
        leftward = folded(jnp.dot(left, stacked(symmetric, 1), preferred_element_type=jnp.float32))
        right = stacked(right_ref[i * TILE:(i + 1) * TILE, :], 1)
        out_ref[:, i * TILE:(i + 1) * TILE] = folded(
            jnp.dot(stacked(leftward, 0), right, preferred_element_type=jnp.float32))


def finish(place, own, mirror, orthogonalizers):
    per = own.shape[0]
    group = 4
    steps = per // group
    tile = pl.BlockSpec((group, TILE, TILE), lambda j, t: (j, 0, 0))
    return pl.pallas_call(
        functools.partial(finish_kernel, group),
        out_shape=jax.ShapeDtypeStruct((TILE, per * TILE), jnp.float32),
        grid_spec=pltpu.PrefetchScalarGridSpec(
            num_scalar_prefetch=1,
            grid=(steps,),
            in_specs=[
                tile, tile,
                pl.BlockSpec((TILE, TILE), lambda j, t: (t[0], 0)),
                pl.BlockSpec((group * TILE, TILE), lambda j, t: (t[1] * steps + j, 0)),
            ],
            out_specs=pl.BlockSpec((TILE, group * TILE), lambda j, t: (0, j)),
        ),
        name="finish",
    )(place, own, mirror, orthogonalizers, orthogonalizers)


def column_order(cols, n_tile):
    count = cols.shape[0]
    spot = jnp.arange(count, dtype=jnp.int32)
    key = jnp.where(cols < 0, n_tile, cols)
    before = (key[None, :] < key[:, None]) | ((key[None, :] == key[:, None]) & (spot[None, :] < spot[:, None]))
    place = jnp.sum(before, axis=1)
    at = place[None, :] == spot[:, None]
    order = jnp.sum(jnp.where(at, spot[None, :], 0), axis=1)
    starts = jnp.any(at & (~jnp.any(before & (key[None, :] == key[:, None]), axis=1))[None, :], axis=1)
    ends = jnp.sum(key[None, :] <= spot[:, None], axis=1) - 1
    held = jnp.any(key[None, :] == spot[:, None], axis=1) & (spot < n_tile)
    return jnp.stack([order, starts.astype(jnp.int32), jnp.maximum(ends, 0), held.astype(jnp.int32)]).astype(jnp.int32)


def local(density, factors, orthogonalizers, slot_pairs, density_source, density_column, target_row, target_column):
    n_tile, n_aux = lax.axis_size("tile"), lax.axis_size("aux")
    me, aux = lax.axis_index("tile"), lax.axis_index("aux")
    tasks = slot_pairs.shape[0]

    def group(rows):
        grid = rows.reshape(n_tile, n_aux, tasks)
        return lax.dynamic_index_in_dim(grid, aux, 1, False)

    sources, columns = group(density_source), group(density_column)
    targets, target_cols = group(target_row), group(target_column)
    own_source = lax.dynamic_index_in_dim(sources, me, 0, False)
    own_target = lax.dynamic_index_in_dim(targets, me, 0, False)
    send_cols = slot_columns(sources, columns, me)
    sum_cols = slot_columns(targets, target_cols, me).reshape(-1)
    table = jnp.stack([
        own_source * CAP + ranks_of(own_source),
        slot_pairs[:, 0],
        slot_pairs[:, 1],
        own_target * CAP + ranks_of(own_target),
    ])
    slots = n_tile * CAP
    incoming = fetch_density(density, jnp.maximum(send_cols, 0), n_tile, n_aux)
    outbound = run_tasks(table, incoming.reshape(slots, TILE, TILE), factors, slots)
    own, mirror = return_partials(
        column_order(sum_cols, n_tile), outbound.reshape(n_tile, CAP, TILE, TILE), n_tile, n_aux)
    return finish(jnp.stack([me, aux]).astype(jnp.int32), own, mirror, orthogonalizers)


def solution(mesh):
    return jax.shard_map(
        local,
        mesh=mesh,
        in_specs=(
            P("tile", "aux"),
            P(("tile", "aux"), None, None, None),
            P(),
            P(("tile", "aux"), None),
            P(),
            P(),
            P(),
            P(),
        ),
        out_specs=P("tile", "aux"),
        check_vma=False,
    )
```

```python
import functools
import jax
import jax.numpy as jnp
from jax import lax
from jax.experimental import pallas as pl
from jax.experimental.pallas import tpu as pltpu
from jax.sharding import PartitionSpec as P

MESH = pl.DeviceIdType.MESH
TILE = 128
CAP = 2
VMEM_BYTES = 56 * 1024 * 1024
STRIDE = 27
CHUNKS = 4
STRIP = TILE // CHUNKS
AHEAD = 2
RING = 8
CORES = 2
ORDER = 13
ROWS = (48, 80)
SPANS = [(sum(ROWS[:r]), n) for r, n in enumerate(ROWS)]


def halves(x):
    top = x.astype(jnp.bfloat16)
    rest = (x - top.astype(jnp.float32)).astype(jnp.bfloat16)
    return top, rest


def ranks_of(keys):
    count = keys.shape[-1]
    spot = jnp.arange(count)
    earlier = spot[None, :] < spot[:, None]
    return jnp.sum((keys[..., :, None] == keys[..., None, :]) & earlier, axis=-1).astype(jnp.int32)


def slot_columns(keys, columns, wanted):
    ranking = ranks_of(keys)
    picked = []
    for level in range(CAP):
        chosen = (keys == wanted) & (ranking == level)
        picked.append(jnp.sum(jnp.where(chosen, columns + 1, 0), axis=-1) - 1)
    return jnp.stack(picked, axis=-1)


def spot_of(tile):
    return tile // (RING * CORES), lax.rem(tile // CORES, RING), lax.rem(tile, CORES)


def tile_of(x, z, core):
    return (x * RING + z) * CORES + core


def opposite(tile):
    x, z, core = spot_of(tile)
    return tile_of(x, lax.rem(z + RING // 2, RING), core)


def reach(turn, core):
    far = jnp.where(core == 0, 2, RING - 2)
    return jnp.where(turn == 3, far, jnp.where(turn == 2, RING - 1, turn))


def served(tile, k, n_tile):
    x, z, core = spot_of(tile)
    across = n_tile // (RING * CORES)
    to_core = lax.rem(core + lax.rem(k, CORES), CORES)
    turn = lax.rem(k // CORES, 4)
    return tile_of(lax.rem(x + k // (4 * CORES), across), lax.rem(z + reach(turn, core), RING), to_core)


def holder(tile, k, n_tile):
    x, z, core = spot_of(tile)
    across = n_tile // (RING * CORES)
    from_core = lax.rem(core + CORES - lax.rem(k, CORES), CORES)
    turn = lax.rem(k // CORES, 4)
    return tile_of(lax.rem(x + across - k // (4 * CORES), across), lax.rem(z + RING - reach(turn, from_core), RING), from_core)


def density_kernel(n_tile, n_aux, cols_ref, dens_ref, out_ref, *scratch):
    parts = len(ROWS)
    slabs, outgoing = scratch[:2 * parts], scratch[2 * parts:4 * parts]
    y_send, y_recv, z_send, z_recv, t_send, t_recv, own_sem = scratch[4 * parts:]
    me = lax.axis_index("tile")
    aux = lax.axis_index("aux")
    far_side = opposite(me)
    homes = [me] * parts + [far_side] * parts
    spans = SPANS * 2
    up, down = lax.rem(aux + 1, n_aux), lax.rem(aux + n_aux - 1, n_aux)
    across = lax.rem(aux + 2, n_aux)
    per = dens_ref.shape[1] // TILE
    half = per // 2
    peers = n_tile // 2
    barrier = pltpu.get_barrier_semaphore()

    @pl.loop(1, n_tile)
    def _(s):
        pl.semaphore_signal(barrier, inc=1, device_id={"tile": lax.rem(me + s, n_tile), "aux": aux}, device_id_type=MESH)

    for other in (up, down):
        pl.semaphore_signal(barrier, inc=1, device_id={"tile": me, "aux": other}, device_id_type=MESH)
    for r, (start, length) in enumerate(SPANS):
        for j in range(per):
            slabs[r][aux * per + j] = dens_ref[start:start + length, j * TILE:(j + 1) * TILE]
    pl.semaphore_wait(barrier, n_tile + 1)

    def near(r, owner, start, length, index, other):
        where = slabs[r].at[pl.ds(owner * per + start, length)]
        return pltpu.make_async_remote_copy(
            src_ref=where, dst_ref=where, send_sem=y_send.at[r, index], recv_sem=y_recv.at[r, index],
            device_id={"tile": me, "aux": other}, device_id_type=MESH)

    def swap(r):
        mine = pl.ds(aux * per, per)
        return pltpu.make_async_remote_copy(
            src_ref=slabs[r].at[mine], dst_ref=slabs[parts + r].at[mine], send_sem=z_send.at[r], recv_sem=z_recv.at[r],
            device_id={"tile": far_side, "aux": aux}, device_id_type=MESH)

    def home_rows(tile, r):
        return out_ref.at[tile, :, pl.ds(*spans[r])]

    def ship(r, k):
        return pltpu.make_async_remote_copy(
            src_ref=outgoing[r].at[k], dst_ref=home_rows(homes[r], r),
            send_sem=t_send.at[r, k], recv_sem=t_recv.at[r, k],
            device_id={"tile": served(me, k, n_tile), "aux": aux}, device_id_type=MESH)

    def own(r):
        return pltpu.make_async_copy(outgoing[r].at[0], home_rows(homes[r], r), own_sem.at[r])

    def first(r):
        near(r, aux, 0, per, 0, up).start()
        near(r, aux, 0, per, 1, down).start()

    def second(r):
        near(r, down, 0, per, 0, up).wait_recv()
        near(r, down, 0, half, 2, up).start()
        near(r, up, 0, per, 1, down).wait_recv()
        near(r, up, half, half, 3, down).start()

    def gathered(r):
        near(r, across, 0, half, 2, up).wait_recv()
        near(r, across, half, half, 3, down).wait_recv()

    def send_all(r):
        base = 0 if r < parts else n_tile

        @pl.loop(0, peers)
        def _(s):
            k = lax.rem(s * ORDER, peers)
            dest = base + served(me, k, n_tile)
            for level in range(CAP):
                outgoing[r][k, level] = slabs[r][cols_ref[dest, level]]

            @pl.when(s > 0)
            def _():
                ship(r, k).start()

        own(r).start()

    def step_copy(r):
        swap(r).wait_recv()
        first(parts + r)

    first(0)
    swap(0).start()
    first(1)
    swap(1).start()
    second(0)
    gathered(0)
    send_all(0)
    second(1)
    step_copy(0)
    gathered(1)
    second(2)
    send_all(1)
    gathered(2)
    step_copy(1)
    send_all(2)
    second(3)
    gathered(3)
    send_all(3)

    for r in range(2 * parts):
        @pl.loop(1, peers)
        def _(k):
            source = holder(me, k, n_tile)
            home = source if r < parts else opposite(source)
            pltpu.make_async_remote_copy(
                src_ref=outgoing[r].at[k], dst_ref=home_rows(home, r),
                send_sem=t_send.at[r, k], recv_sem=t_recv.at[r, k],
                device_id={"tile": source, "aux": aux}, device_id_type=MESH).wait_recv()
            ship(r, k).wait_send()

        own(r).wait()
        near(r, aux, 0, per, 0, up).wait_send()
        near(r, aux, 0, per, 1, down).wait_send()
        near(r, down, 0, half, 2, up).wait_send()
        near(r, up, half, half, 3, down).wait_send()
        if r < parts:
            swap(r).wait_send()


def fetch_density(density, cols, n_tile, n_aux):
    units = 2 * len(ROWS)
    return pl.pallas_call(
        functools.partial(density_kernel, n_tile, n_aux),
        out_shape=jax.ShapeDtypeStruct((n_tile, CAP, TILE, TILE), jnp.float32),
        in_specs=[pl.BlockSpec(memory_space=pltpu.SMEM), pl.BlockSpec(memory_space=pltpu.VMEM)],
        out_specs=pl.BlockSpec(memory_space=pl.ANY),
        scratch_shapes=[pltpu.VMEM((n_tile, n, TILE), jnp.float32) for n in ROWS * 2]
        + [pltpu.VMEM((n_tile // 2, CAP, n, TILE), jnp.float32) for n in ROWS * 2]
        + [
            pltpu.SemaphoreType.DMA((units, 4)),
            pltpu.SemaphoreType.DMA((units, 4)),
            pltpu.SemaphoreType.DMA((len(ROWS),)),
            pltpu.SemaphoreType.DMA((len(ROWS),)),
            pltpu.SemaphoreType.DMA((units, n_tile // 2)),
            pltpu.SemaphoreType.DMA((units, n_tile // 2)),
            pltpu.SemaphoreType.DMA((units,)),
        ],
        compiler_params=pltpu.CompilerParams(collective_id=0, has_side_effects=True, vmem_limit_bytes=VMEM_BYTES),
        name="fetch_density",
    )(cols, density)


def task_kernel(pair_count, table, dens_ref, fact_ref, out_ref, split):
    q = pl.program_id(0)

    @pl.when(q == 0)
    def _():
        @pl.loop(0, fact_ref.shape[0])
        def _(slot):
            @pl.loop(0, pair_count)
            def _(p):
                rows = pl.ds(pl.multiple_of(p * 2 * TILE, 2 * TILE), 2 * TILE)
                top, rest = halves(fact_ref[slot, rows, :])
                split[slot, rows, 0:TILE] = top
                split[slot, rows, TILE:2 * TILE] = rest

    left, right = table[1, q], table[2, q]
    top, rest = halves(dens_ref[0])
    row = jnp.concatenate([top, rest], axis=1)
    weights = jnp.concatenate([row, row], axis=0)
    total = jnp.zeros((2 * TILE, 2 * TILE), jnp.float32)
    for p in range(pair_count):
        rows = slice(p * 2 * TILE, (p + 1) * 2 * TILE)
        wide = jnp.dot(split[left, rows, :], weights, preferred_element_type=jnp.float32)
        top, rest = halves(wide[:, :TILE] + wide[:, TILE:])
        lhs = jnp.concatenate(
            [jnp.concatenate([top[:TILE], top[TILE:]], axis=1), jnp.concatenate([rest[:TILE], rest[TILE:]], axis=1)], axis=0)
        total = total + jnp.dot(lhs, split[right, rows, :], preferred_element_type=jnp.float32)
    tall = total[:, :TILE] + total[:, TILE:]
    out_ref[0] = tall[:TILE] + tall[TILE:]


def run_tasks(table, incoming, factors, slots):
    slot_count, aux_funcs = factors.shape[:2]
    flat = factors.reshape(slot_count, aux_funcs * TILE, TILE)
    task_count = table.shape[1]
    return pl.pallas_call(
        functools.partial(task_kernel, aux_funcs // 2),
        out_shape=jax.ShapeDtypeStruct((slots, TILE, TILE), jnp.float32),
        grid_spec=pltpu.PrefetchScalarGridSpec(
            num_scalar_prefetch=1,
            grid=(task_count,),
            in_specs=[
                pl.BlockSpec((1, TILE, TILE), lambda q, t: (t[0, q], 0, 0)),
                pl.BlockSpec(flat.shape, lambda q, t: (0, 0, 0), pipeline_mode=pl.Buffered(1)),
            ],
            out_specs=pl.BlockSpec((1, TILE, TILE), lambda q, t: (t[3, q], 0, 0)),
            scratch_shapes=[pltpu.VMEM((slot_count, aux_funcs * TILE, 2 * TILE), jnp.bfloat16)],
        ),
        compiler_params=pltpu.CompilerParams(vmem_limit_bytes=VMEM_BYTES),
        name="run_tasks",
    )(table, incoming, flat)


def return_kernel(n_tile, n_aux, order_ref, src_ref, own_ref, mirror_ref, *scratch):
    arrived = scratch[:CHUNKS]
    (running, rows, half_up, half_down, full_up, full_down, outgoing, summed,
     t_send, t_recv, y_send, y_recv, m_send, m_recv, own_sem, out_sem) = scratch[CHUNKS:]
    me = lax.axis_index("tile")
    aux = lax.axis_index("aux")
    up, down = lax.rem(aux + 1, n_aux), lax.rem(aux + n_aux - 1, n_aux)
    across = lax.rem(aux + 2, n_aux)
    per = n_tile // n_aux
    half = per // 2
    block = me // per
    slot = lax.rem(me, per)
    alike = block == aux
    slots = n_tile * CAP
    barrier = pltpu.get_barrier_semaphore()

    @pl.loop(1, n_tile)
    def _(s):
        pl.semaphore_signal(barrier, inc=1, device_id={"tile": lax.rem(me + s, n_tile), "aux": aux}, device_id_type=MESH)

    for other in (up, down):
        pl.semaphore_signal(barrier, inc=1, device_id={"tile": me, "aux": other}, device_id_type=MESH)

    @pl.loop(0, per)
    def _(j):
        @pl.when(jnp.logical_not(alike & (j == slot)))
        def _():
            pl.semaphore_signal(barrier, inc=1, device_id={"tile": aux * per + j, "aux": block}, device_id_type=MESH)

    pl.semaphore_wait(barrier, n_tile + jnp.where(alike, per, per + 1))

    def far(r, s):
        dest = lax.rem(me + lax.rem(s * STRIDE, n_tile), n_tile)
        return pltpu.make_async_remote_copy(
            src_ref=src_ref.at[dest, :, pl.ds(r * STRIP, STRIP)], dst_ref=arrived[r].at[pl.ds(me * CAP, CAP)],
            send_sem=t_send.at[r, s], recv_sem=t_recv.at[r, s],
            device_id={"tile": dest, "aux": aux}, device_id_type=MESH)

    def own(r):
        return pltpu.make_async_copy(
            src_ref.at[me, :, pl.ds(r * STRIP, STRIP)], arrived[r].at[pl.ds(me * CAP, CAP)], own_sem.at[r])

    def begin(r):
        @pl.loop(1, n_tile)
        def _(s):
            far(r, s).start()

        own(r).start()

    def near(src, dst, r, index, other):
        return pltpu.make_async_remote_copy(
            src_ref=src, dst_ref=dst, send_sem=y_send.at[r, index], recv_sem=y_recv.at[r, index],
            device_id={"tile": me, "aux": other}, device_id_type=MESH)

    def steps(r):
        return (
            near(rows.at[r, pl.ds(across * per, half)], half_up.at[r], r, 0, up),
            near(rows.at[r, pl.ds(across * per + half, half)], half_down.at[r], r, 1, down),
            near(outgoing.at[r, 0], full_up.at[r], r, 2, up),
            near(outgoing.at[r, 1], full_down.at[r], r, 3, down),
        )

    def send(r, j):
        return pltpu.make_async_remote_copy(
            src_ref=summed.at[r, j], dst_ref=mirror_ref.at[slot, pl.ds(r * STRIP, STRIP)],
            send_sem=m_send.at[r, j], recv_sem=m_recv.at[r, slot],
            device_id={"tile": aux * per + j, "aux": block}, device_id_type=MESH)

    def keep(r, j):
        return pltpu.make_async_copy(summed.at[r, j], mirror_ref.at[j, pl.ds(r * STRIP, STRIP)], m_send.at[r, j])

    def settle(r):
        return pltpu.make_async_copy(summed.at[r], own_ref.at[:, pl.ds(r * STRIP, STRIP)], out_sem.at[r])

    for r in range(AHEAD):
        begin(r)
    for r in range(CHUNKS):
        @pl.loop(1, n_tile)
        def _(s):
            source = lax.rem(me + n_tile - lax.rem(s * STRIDE, n_tile), n_tile)
            pltpu.make_async_remote_copy(
                src_ref=src_ref.at[me, :, pl.ds(r * STRIP, STRIP)], dst_ref=arrived[r].at[pl.ds(source * CAP, CAP)],
                send_sem=t_send.at[r, s], recv_sem=t_recv.at[r, s],
                device_id={"tile": source, "aux": aux}, device_id_type=MESH).wait_recv()

        own(r).wait()

        def add(i, carry):
            for u in range(4):
                k = i * 4 + u
                carry = jnp.where(order_ref[1, k] > 0, 0.0, carry) + arrived[r][order_ref[0, k]]
                running[k] = carry
            return carry

        lax.fori_loop(0, slots // 4, add, jnp.zeros((STRIP, TILE), jnp.float32))

        @pl.loop(0, n_tile)
        def _(b):
            rows[r, b] = jnp.where(order_ref[3, b] > 0, running[order_ref[2, b]], 0.0)

        first_up, first_down, second_up, second_down = steps(r)
        first_up.start()
        first_down.start()
        if r + AHEAD < CHUNKS:
            begin(r + AHEAD)

        @pl.loop(0, half)
        def _(j):
            outgoing[r, 0, half + j] = rows[r, up * per + half + j]
            outgoing[r, 1, j] = rows[r, down * per + j]

        first_up.wait_recv()

        @pl.loop(0, half)
        def _(j):
            outgoing[r, 0, j] = rows[r, up * per + j] + half_up[r, j]

        second_up.start()
        first_down.wait_recv()

        @pl.loop(0, half)
        def _(j):
            outgoing[r, 1, half + j] = rows[r, down * per + half + j] + half_down[r, j]

        second_down.start()
        second_up.wait_recv()
        second_down.wait_recv()

        @pl.loop(0, per)
        def _(j):
            summed[r, j] = rows[r, aux * per + j] + (full_up[r, j] + full_down[r, j])
            mine = alike & (j == slot)

            @pl.when(jnp.logical_not(mine))
            def _():
                send(r, j).start()

            @pl.when(mine)
            def _():
                keep(r, j).start()

        settle(r).start()

    for r in range(CHUNKS):
        @pl.loop(1, n_tile)
        def _(s):
            far(r, s).wait_send()

        @pl.loop(0, per)
        def _(j):
            mine = alike & (j == slot)

            @pl.when(jnp.logical_not(mine))
            def _():
                pltpu.make_async_remote_copy(
                    src_ref=summed.at[r, j], dst_ref=mirror_ref.at[j, pl.ds(r * STRIP, STRIP)],
                    send_sem=m_send.at[r, j], recv_sem=m_recv.at[r, j],
                    device_id={"tile": aux * per + j, "aux": block}, device_id_type=MESH).wait_recv()
                send(r, j).wait_send()

            @pl.when(mine)
            def _():
                keep(r, j).wait()

        settle(r).wait()
        for copy in steps(r):
            copy.wait_send()


def return_partials(order, outbound, n_tile, n_aux):
    per = n_tile // n_aux
    strips = lambda *lead: pltpu.VMEM(lead + (STRIP, TILE), jnp.float32)
    shape = jax.ShapeDtypeStruct((per, TILE, TILE), jnp.float32)
    return pl.pallas_call(
        functools.partial(return_kernel, n_tile, n_aux),
        out_shape=(shape, shape),
        in_specs=[pl.BlockSpec(memory_space=pltpu.SMEM), pl.BlockSpec(memory_space=pl.ANY)],
        out_specs=(pl.BlockSpec(memory_space=pl.ANY), pl.BlockSpec(memory_space=pl.ANY)),
        scratch_shapes=[strips(n_tile * CAP)] * CHUNKS + [
            strips(n_tile * CAP), strips(CHUNKS, n_tile),
            strips(CHUNKS, per // 2), strips(CHUNKS, per // 2), strips(CHUNKS, per), strips(CHUNKS, per),
            strips(CHUNKS, 2, per), strips(CHUNKS, per),
            pltpu.SemaphoreType.DMA((CHUNKS, n_tile)),
            pltpu.SemaphoreType.DMA((CHUNKS, n_tile)),
            pltpu.SemaphoreType.DMA((CHUNKS, 4)),
            pltpu.SemaphoreType.DMA((CHUNKS, 4)),
            pltpu.SemaphoreType.DMA((CHUNKS, per)),
            pltpu.SemaphoreType.DMA((CHUNKS, per)),
            pltpu.SemaphoreType.DMA((CHUNKS,)),
            pltpu.SemaphoreType.DMA((CHUNKS,)),
        ],
        compiler_params=pltpu.CompilerParams(collective_id=1, has_side_effects=True, vmem_limit_bytes=VMEM_BYTES),
        name="return_partials",
    )(order, outbound)


def stacked(x, axis):
    return jnp.concatenate(halves(x), axis=axis)


def folded(x):
    tall = x[:, :TILE] + x[:, TILE:]
    return tall[:TILE] + tall[TILE:]


def finish_kernel(group, place, own_ref, mirror_ref, left_ref, right_ref, out_ref):
    left = stacked(jnp.transpose(left_ref[...]), 0)
    for i in range(group):
        symmetric = own_ref[i] + jnp.transpose(mirror_ref[i])
        leftward = folded(jnp.dot(left, stacked(symmetric, 1), preferred_element_type=jnp.float32))
        right = stacked(right_ref[i * TILE:(i + 1) * TILE, :], 1)
        out_ref[:, i * TILE:(i + 1) * TILE] = folded(
            jnp.dot(stacked(leftward, 0), right, preferred_element_type=jnp.float32))


def finish(place, own, mirror, orthogonalizers):
    per = own.shape[0]
    group = 4
    steps = per // group
    tile = pl.BlockSpec((group, TILE, TILE), lambda j, t: (j, 0, 0))
    return pl.pallas_call(
        functools.partial(finish_kernel, group),
        out_shape=jax.ShapeDtypeStruct((TILE, per * TILE), jnp.float32),
        grid_spec=pltpu.PrefetchScalarGridSpec(
            num_scalar_prefetch=1,
            grid=(steps,),
            in_specs=[
                tile, tile,
                pl.BlockSpec((TILE, TILE), lambda j, t: (t[0], 0)),
                pl.BlockSpec((group * TILE, TILE), lambda j, t: (t[1] * steps + j, 0)),
            ],
            out_specs=pl.BlockSpec((TILE, group * TILE), lambda j, t: (0, j)),
        ),
        name="finish",
    )(place, own, mirror, orthogonalizers, orthogonalizers)


def column_order(cols, n_tile):
    count = cols.shape[0]
    spot = jnp.arange(count, dtype=jnp.int32)
    key = jnp.where(cols < 0, n_tile, cols)
    before = (key[None, :] < key[:, None]) | ((key[None, :] == key[:, None]) & (spot[None, :] < spot[:, None]))
    place = jnp.sum(before, axis=1)
    at = place[None, :] == spot[:, None]
    order = jnp.sum(jnp.where(at, spot[None, :], 0), axis=1)
    starts = jnp.any(at & (~jnp.any(before & (key[None, :] == key[:, None]), axis=1))[None, :], axis=1)
    ends = jnp.sum(key[None, :] <= spot[:, None], axis=1) - 1
    held = jnp.any(key[None, :] == spot[:, None], axis=1) & (spot < n_tile)
    return jnp.stack([order, starts.astype(jnp.int32), jnp.maximum(ends, 0), held.astype(jnp.int32)]).astype(jnp.int32)


def local(density, factors, orthogonalizers, slot_pairs, density_source, density_column, target_row, target_column):
    n_tile, n_aux = lax.axis_size("tile"), lax.axis_size("aux")
    me, aux = lax.axis_index("tile"), lax.axis_index("aux")
    tasks = slot_pairs.shape[0]

    def group(rows):
        grid = rows.reshape(n_tile, n_aux, tasks)
        return lax.dynamic_index_in_dim(grid, aux, 1, False)

    sources, columns = group(density_source), group(density_column)
    targets, target_cols = group(target_row), group(target_column)
    own_source = lax.dynamic_index_in_dim(sources, me, 0, False)
    own_target = lax.dynamic_index_in_dim(targets, me, 0, False)
    send_cols = jnp.concatenate([slot_columns(sources, columns, me), slot_columns(sources, columns, opposite(me))])
    sum_cols = slot_columns(targets, target_cols, me).reshape(-1)
    table = jnp.stack([
        own_source * CAP + ranks_of(own_source),
        slot_pairs[:, 0],
        slot_pairs[:, 1],
        own_target * CAP + ranks_of(own_target),
    ])
    slots = n_tile * CAP
    incoming = fetch_density(density, jnp.maximum(send_cols, 0), n_tile, n_aux)
    outbound = run_tasks(table, incoming.reshape(slots, TILE, TILE), factors, slots)
    own, mirror = return_partials(
        column_order(sum_cols, n_tile), outbound.reshape(n_tile, CAP, TILE, TILE), n_tile, n_aux)
    return finish(jnp.stack([me, aux]).astype(jnp.int32), own, mirror, orthogonalizers)


def solution(mesh):
    return jax.shard_map(
        local,
        mesh=mesh,
        in_specs=(
            P("tile", "aux"),
            P(("tile", "aux"), None, None, None),
            P(),
            P(("tile", "aux"), None),
            P(),
            P(),
            P(),
            P(),
        ),
        out_specs=P("tile", "aux"),
        check_vma=False,
    )
```

```python
import functools
import jax
import jax.numpy as jnp
from jax import lax
from jax.experimental import pallas as pl
from jax.experimental.pallas import tpu as pltpu
from jax.sharding import PartitionSpec as P

MESH = pl.DeviceIdType.MESH
TILE = 128
CAP = 2
VMEM_BYTES = 56 * 1024 * 1024
RING = 8
CORES = 2
ORDER = 13
ROWS = (48, 80)
SPANS = [(sum(ROWS[:r]), n) for r, n in enumerate(ROWS)]
BACK = (56, 40, 32)
BACK_SPANS = [(sum(BACK[:r]), n) for r, n in enumerate(BACK)]


def halves(x):
    top = x.astype(jnp.bfloat16)
    rest = (x - top.astype(jnp.float32)).astype(jnp.bfloat16)
    return top, rest


def ranks_of(keys):
    count = keys.shape[-1]
    spot = jnp.arange(count)
    earlier = spot[None, :] < spot[:, None]
    return jnp.sum((keys[..., :, None] == keys[..., None, :]) & earlier, axis=-1).astype(jnp.int32)


def slot_columns(keys, columns, wanted):
    ranking = ranks_of(keys)
    picked = []
    for level in range(CAP):
        chosen = (keys == wanted) & (ranking == level)
        picked.append(jnp.sum(jnp.where(chosen, columns + 1, 0), axis=-1) - 1)
    return jnp.stack(picked, axis=-1)


def spot_of(tile):
    return tile // (RING * CORES), lax.rem(tile // CORES, RING), lax.rem(tile, CORES)


def tile_of(x, z, core):
    return (x * RING + z) * CORES + core


def opposite(tile):
    x, z, core = spot_of(tile)
    return tile_of(x, lax.rem(z + RING // 2, RING), core)


def reach(turn, core):
    far = jnp.where(core == 0, 2, RING - 2)
    return jnp.where(turn == 3, far, jnp.where(turn == 2, RING - 1, turn))


def served(tile, k, n_tile):
    x, z, core = spot_of(tile)
    across = n_tile // (RING * CORES)
    to_core = lax.rem(core + lax.rem(k, CORES), CORES)
    turn = lax.rem(k // CORES, 4)
    return tile_of(lax.rem(x + k // (4 * CORES), across), lax.rem(z + reach(turn, core), RING), to_core)


def holder(tile, k, n_tile):
    x, z, core = spot_of(tile)
    across = n_tile // (RING * CORES)
    from_core = lax.rem(core + CORES - lax.rem(k, CORES), CORES)
    turn = lax.rem(k // CORES, 4)
    return tile_of(lax.rem(x + across - k // (4 * CORES), across), lax.rem(z + RING - reach(turn, from_core), RING), from_core)


def density_kernel(n_tile, n_aux, cols_ref, dens_ref, out_ref, *scratch):
    parts = len(ROWS)
    slabs, outgoing = scratch[:2 * parts], scratch[2 * parts:4 * parts]
    y_send, y_recv, z_send, z_recv, t_send, t_recv, own_sem = scratch[4 * parts:]
    me = lax.axis_index("tile")
    aux = lax.axis_index("aux")
    far_side = opposite(me)
    homes = [me] * parts + [far_side] * parts
    spans = SPANS * 2
    up, down = lax.rem(aux + 1, n_aux), lax.rem(aux + n_aux - 1, n_aux)
    across = lax.rem(aux + 2, n_aux)
    per = dens_ref.shape[1] // TILE
    half = per // 2
    peers = n_tile // 2
    barrier = pltpu.get_barrier_semaphore()

    @pl.loop(1, n_tile)
    def _(s):
        pl.semaphore_signal(barrier, inc=1, device_id={"tile": lax.rem(me + s, n_tile), "aux": aux}, device_id_type=MESH)

    for other in (up, down):
        pl.semaphore_signal(barrier, inc=1, device_id={"tile": me, "aux": other}, device_id_type=MESH)
    for r, (start, length) in enumerate(SPANS):
        for j in range(per):
            slabs[r][aux * per + j] = dens_ref[start:start + length, j * TILE:(j + 1) * TILE]
    pl.semaphore_wait(barrier, n_tile + 1)

    def near(r, owner, start, length, index, other):
        where = slabs[r].at[pl.ds(owner * per + start, length)]
        return pltpu.make_async_remote_copy(
            src_ref=where, dst_ref=where, send_sem=y_send.at[r, index], recv_sem=y_recv.at[r, index],
            device_id={"tile": me, "aux": other}, device_id_type=MESH)

    def swap(r):
        mine = pl.ds(aux * per, per)
        return pltpu.make_async_remote_copy(
            src_ref=slabs[r].at[mine], dst_ref=slabs[parts + r].at[mine], send_sem=z_send.at[r], recv_sem=z_recv.at[r],
            device_id={"tile": far_side, "aux": aux}, device_id_type=MESH)

    def home_rows(tile, r):
        return out_ref.at[tile, :, pl.ds(*spans[r])]

    def ship(r, k):
        return pltpu.make_async_remote_copy(
            src_ref=outgoing[r].at[k], dst_ref=home_rows(homes[r], r),
            send_sem=t_send.at[r, k], recv_sem=t_recv.at[r, k],
            device_id={"tile": served(me, k, n_tile), "aux": aux}, device_id_type=MESH)

    def own(r):
        return pltpu.make_async_copy(outgoing[r].at[0], home_rows(homes[r], r), own_sem.at[r])

    def first(r):
        near(r, aux, 0, per, 0, up).start()
        near(r, aux, 0, per, 1, down).start()

    def second(r):
        near(r, down, 0, per, 0, up).wait_recv()
        near(r, down, 0, half, 2, up).start()
        near(r, up, 0, per, 1, down).wait_recv()
        near(r, up, half, half, 3, down).start()

    def gathered(r):
        near(r, across, 0, half, 2, up).wait_recv()
        near(r, across, half, half, 3, down).wait_recv()

    def send_all(r):
        base = 0 if r < parts else n_tile

        @pl.loop(0, peers)
        def _(s):
            k = lax.rem(s * ORDER, peers)
            dest = base + served(me, k, n_tile)
            for level in range(CAP):
                outgoing[r][k, level] = slabs[r][cols_ref[dest, level]]

            @pl.when(s > 0)
            def _():
                ship(r, k).start()

        own(r).start()

    def step_copy(r):
        swap(r).wait_recv()
        first(parts + r)

    first(0)
    swap(0).start()
    first(1)
    swap(1).start()
    second(0)
    gathered(0)
    send_all(0)
    second(1)
    step_copy(0)
    gathered(1)
    second(2)
    send_all(1)
    gathered(2)
    step_copy(1)
    send_all(2)
    second(3)
    gathered(3)
    send_all(3)

    for r in range(2 * parts):
        @pl.loop(1, peers)
        def _(k):
            source = holder(me, k, n_tile)
            home = source if r < parts else opposite(source)
            pltpu.make_async_remote_copy(
                src_ref=outgoing[r].at[k], dst_ref=home_rows(home, r),
                send_sem=t_send.at[r, k], recv_sem=t_recv.at[r, k],
                device_id={"tile": source, "aux": aux}, device_id_type=MESH).wait_recv()
            ship(r, k).wait_send()

        own(r).wait()
        near(r, aux, 0, per, 0, up).wait_send()
        near(r, aux, 0, per, 1, down).wait_send()
        near(r, down, 0, half, 2, up).wait_send()
        near(r, up, half, half, 3, down).wait_send()
        if r < parts:
            swap(r).wait_send()


def fetch_density(density, cols, n_tile, n_aux):
    units = 2 * len(ROWS)
    return pl.pallas_call(
        functools.partial(density_kernel, n_tile, n_aux),
        out_shape=jax.ShapeDtypeStruct((n_tile, CAP, TILE, TILE), jnp.float32),
        in_specs=[pl.BlockSpec(memory_space=pltpu.SMEM), pl.BlockSpec(memory_space=pltpu.VMEM)],
        out_specs=pl.BlockSpec(memory_space=pl.ANY),
        scratch_shapes=[pltpu.VMEM((n_tile, n, TILE), jnp.float32) for n in ROWS * 2]
        + [pltpu.VMEM((n_tile // 2, CAP, n, TILE), jnp.float32) for n in ROWS * 2]
        + [
            pltpu.SemaphoreType.DMA((units, 4)),
            pltpu.SemaphoreType.DMA((units, 4)),
            pltpu.SemaphoreType.DMA((len(ROWS),)),
            pltpu.SemaphoreType.DMA((len(ROWS),)),
            pltpu.SemaphoreType.DMA((units, n_tile // 2)),
            pltpu.SemaphoreType.DMA((units, n_tile // 2)),
            pltpu.SemaphoreType.DMA((units,)),
        ],
        compiler_params=pltpu.CompilerParams(collective_id=0, has_side_effects=True, vmem_limit_bytes=VMEM_BYTES),
        name="fetch_density",
    )(cols, density)


def task_kernel(pair_count, table, dens_ref, fact_ref, out_ref, split):
    q = pl.program_id(0)

    @pl.when(q == 0)
    def _():
        @pl.loop(0, fact_ref.shape[0])
        def _(slot):
            @pl.loop(0, pair_count)
            def _(p):
                rows = pl.ds(pl.multiple_of(p * 2 * TILE, 2 * TILE), 2 * TILE)
                top, rest = halves(fact_ref[slot, rows, :])
                split[slot, rows, 0:TILE] = top
                split[slot, rows, TILE:2 * TILE] = rest

    left, right = table[1, q], table[2, q]
    top, rest = halves(dens_ref[0])
    row = jnp.concatenate([top, rest], axis=1)
    weights = jnp.concatenate([row, row], axis=0)
    total = jnp.zeros((2 * TILE, 2 * TILE), jnp.float32)
    for p in range(pair_count):
        rows = slice(p * 2 * TILE, (p + 1) * 2 * TILE)
        wide = jnp.dot(split[left, rows, :], weights, preferred_element_type=jnp.float32)
        top, rest = halves(wide[:, :TILE] + wide[:, TILE:])
        lhs = jnp.concatenate(
            [jnp.concatenate([top[:TILE], top[TILE:]], axis=1), jnp.concatenate([rest[:TILE], rest[TILE:]], axis=1)], axis=0)
        total = total + jnp.dot(lhs, split[right, rows, :], preferred_element_type=jnp.float32)
    tall = total[:, :TILE] + total[:, TILE:]
    out_ref[0] = tall[:TILE] + tall[TILE:]


def run_tasks(table, incoming, factors, slots):
    slot_count, aux_funcs = factors.shape[:2]
    flat = factors.reshape(slot_count, aux_funcs * TILE, TILE)
    task_count = table.shape[1]
    return pl.pallas_call(
        functools.partial(task_kernel, aux_funcs // 2),
        out_shape=jax.ShapeDtypeStruct((slots, TILE, TILE), jnp.float32),
        grid_spec=pltpu.PrefetchScalarGridSpec(
            num_scalar_prefetch=1,
            grid=(task_count,),
            in_specs=[
                pl.BlockSpec((1, TILE, TILE), lambda q, t: (t[0, q], 0, 0)),
                pl.BlockSpec(flat.shape, lambda q, t: (0, 0, 0), pipeline_mode=pl.Buffered(1)),
            ],
            out_specs=pl.BlockSpec((1, TILE, TILE), lambda q, t: (t[3, q], 0, 0)),
            scratch_shapes=[pltpu.VMEM((slot_count, aux_funcs * TILE, 2 * TILE), jnp.bfloat16)],
        ),
        compiler_params=pltpu.CompilerParams(vmem_limit_bytes=VMEM_BYTES),
        name="run_tasks",
    )(table, incoming, flat)


def return_kernel(n_tile, n_aux, order_ref, src_ref, own_ref, mirror_ref, *scratch):
    parts = len(BACK)
    units = 2 * parts
    groups = [scratch[i * units:(i + 1) * units] for i in range(8)]
    arrived, rows, half_up, half_down, full_up, full_down, outgoing, summed = groups
    swapped = scratch[8 * units:8 * units + parts]
    (running, t_send, t_recv, y_send, y_recv, m_send, m_recv, z_send, z_recv, own_sem, out_sem) = scratch[8 * units + parts:]
    me = lax.axis_index("tile")
    aux = lax.axis_index("aux")
    far_side = opposite(me)
    up, down = lax.rem(aux + 1, n_aux), lax.rem(aux + n_aux - 1, n_aux)
    across = lax.rem(aux + 2, n_aux)
    per = n_tile // n_aux
    half = per // 2
    peers = n_tile // 2
    block = me // per
    slot = lax.rem(me, per)
    alike = block == aux
    barrier = pltpu.get_barrier_semaphore()

    @pl.loop(1, n_tile)
    def _(s):
        pl.semaphore_signal(barrier, inc=1, device_id={"tile": lax.rem(me + s, n_tile), "aux": aux}, device_id_type=MESH)

    for other in (up, down):
        pl.semaphore_signal(barrier, inc=1, device_id={"tile": me, "aux": other}, device_id_type=MESH)

    @pl.loop(0, per)
    def _(j):
        @pl.when(jnp.logical_not(alike & (j == slot)))
        def _():
            pl.semaphore_signal(barrier, inc=1, device_id={"tile": aux * per + j, "aux": block}, device_id_type=MESH)

    pl.semaphore_wait(barrier, n_tile + jnp.where(alike, per, per + 1))

    def span(u):
        return pl.ds(*BACK_SPANS[u // 2])

    def home_of(tile, u):
        return opposite(tile) if u % 2 == 0 else tile

    def far(u, k):
        dest = holder(me, k, n_tile)
        return pltpu.make_async_remote_copy(
            src_ref=src_ref.at[home_of(dest, u), :, span(u)], dst_ref=arrived[u].at[pl.ds(k * CAP, CAP)],
            send_sem=t_send.at[u, k], recv_sem=t_recv.at[u, k],
            device_id={"tile": dest, "aux": aux}, device_id_type=MESH)

    def own(u):
        return pltpu.make_async_copy(src_ref.at[home_of(me, u), :, span(u)], arrived[u].at[pl.ds(0, CAP)], own_sem.at[u])

    def begin(u):
        @pl.loop(1, peers)
        def _(s):
            far(u, lax.rem(s * ORDER, peers)).start()

        own(u).start()

    def near(src, dst, u, index, other):
        return pltpu.make_async_remote_copy(
            src_ref=src, dst_ref=dst, send_sem=y_send.at[u, index], recv_sem=y_recv.at[u, index],
            device_id={"tile": me, "aux": other}, device_id_type=MESH)

    def steps(u):
        return (
            near(rows[u].at[pl.ds(across * per, half)], half_up[u], u, 0, up),
            near(rows[u].at[pl.ds(across * per + half, half)], half_down[u], u, 1, down),
            near(outgoing[u].at[0], full_up[u], u, 2, up),
            near(outgoing[u].at[1], full_down[u], u, 3, down),
        )

    def swap(p):
        return pltpu.make_async_remote_copy(
            src_ref=summed[2 * p], dst_ref=swapped[p], send_sem=z_send.at[p], recv_sem=z_recv.at[p],
            device_id={"tile": far_side, "aux": aux}, device_id_type=MESH)

    def send(u, j):
        return pltpu.make_async_remote_copy(
            src_ref=summed[u].at[j], dst_ref=mirror_ref.at[slot, span(u)],
            send_sem=m_send.at[u, j], recv_sem=m_recv.at[u, slot],
            device_id={"tile": aux * per + j, "aux": block}, device_id_type=MESH)

    def keep(u, j):
        return pltpu.make_async_copy(summed[u].at[j], mirror_ref.at[j, span(u)], m_send.at[u, j])

    def settle(u):
        return pltpu.make_async_copy(summed[u], own_ref.at[:, span(u)], out_sem.at[u // 2])

    begin(0)
    begin(1)
    for u in range(units):
        length = BACK[u // 2]
        table = (u % 2) * 4

        @pl.loop(1, peers)
        def _(k):
            pltpu.make_async_remote_copy(
                src_ref=src_ref.at[me, :, span(u)], dst_ref=arrived[u].at[pl.ds(k * CAP, CAP)],
                send_sem=t_send.at[u, k], recv_sem=t_recv.at[u, k],
                device_id={"tile": served(me, k, n_tile), "aux": aux}, device_id_type=MESH).wait_recv()

        own(u).wait()

        def add(i, carry):
            for v in range(4):
                k = i * 4 + v
                carry = jnp.where(order_ref[table + 1, k] > 0, 0.0, carry) + arrived[u][order_ref[table, k]]
                running[k, 0:length] = carry
            return carry

        lax.fori_loop(0, peers * CAP // 4, add, jnp.zeros((length, TILE), jnp.float32))

        @pl.loop(0, n_tile)
        def _(b):
            rows[u][b] = jnp.where(order_ref[table + 3, b] > 0, running[order_ref[table + 2, b], 0:length], 0.0)

        first_up, first_down, second_up, second_down = steps(u)
        first_up.start()
        first_down.start()
        if u + 2 < units:
            begin(u + 2)

        @pl.loop(0, half)
        def _(j):
            outgoing[u][0, half + j] = rows[u][up * per + half + j]
            outgoing[u][1, j] = rows[u][down * per + j]

        first_up.wait_recv()

        @pl.loop(0, half)
        def _(j):
            outgoing[u][0, j] = rows[u][up * per + j] + half_up[u][j]

        second_up.start()
        first_down.wait_recv()

        @pl.loop(0, half)
        def _(j):
            outgoing[u][1, half + j] = rows[u][down * per + half + j] + half_down[u][j]

        second_down.start()
        second_up.wait_recv()
        second_down.wait_recv()
        if u % 2 == 0:
            @pl.loop(0, per)
            def _(j):
                summed[u][j] = rows[u][aux * per + j] + (full_up[u][j] + full_down[u][j])

            swap(u // 2).start()
        else:
            swap(u // 2).wait_recv()

            @pl.loop(0, per)
            def _(j):
                summed[u][j] = (rows[u][aux * per + j] + swapped[u // 2][j]) + (full_up[u][j] + full_down[u][j])
                mine = alike & (j == slot)

                @pl.when(jnp.logical_not(mine))
                def _():
                    send(u, j).start()

                @pl.when(mine)
                def _():
                    keep(u, j).start()

            settle(u).start()

    for u in range(units):
        @pl.loop(1, peers)
        def _(k):
            far(u, k).wait_send()

        for copy in steps(u):
            copy.wait_send()
        if u % 2 == 0:
            swap(u // 2).wait_send()
        else:
            @pl.loop(0, per)
            def _(j):
                mine = alike & (j == slot)

                @pl.when(jnp.logical_not(mine))
                def _():
                    pltpu.make_async_remote_copy(
                        src_ref=summed[u].at[j], dst_ref=mirror_ref.at[j, span(u)],
                        send_sem=m_send.at[u, j], recv_sem=m_recv.at[u, j],
                        device_id={"tile": aux * per + j, "aux": block}, device_id_type=MESH).wait_recv()
                    send(u, j).wait_send()

                @pl.when(mine)
                def _():
                    keep(u, j).wait()

            settle(u).wait()


def return_partials(order, outbound, n_tile, n_aux):
    per = n_tile // n_aux
    peers = n_tile // 2
    parts = len(BACK)
    units = 2 * parts
    lengths = [n for n in BACK for _ in range(2)]
    shape = jax.ShapeDtypeStruct((per, TILE, TILE), jnp.float32)
    leads = [(peers * CAP,), (n_tile,), (per // 2,), (per // 2,), (per,), (per,), (2, per), (per,)]
    return pl.pallas_call(
        functools.partial(return_kernel, n_tile, n_aux),
        out_shape=(shape, shape),
        in_specs=[pl.BlockSpec(memory_space=pltpu.SMEM), pl.BlockSpec(memory_space=pl.ANY)],
        out_specs=(pl.BlockSpec(memory_space=pl.ANY), pl.BlockSpec(memory_space=pl.ANY)),
        scratch_shapes=[pltpu.VMEM(lead + (n, TILE), jnp.float32) for lead in leads for n in lengths]
        + [pltpu.VMEM((per, n, TILE), jnp.float32) for n in BACK]
        + [
            pltpu.VMEM((peers * CAP, max(BACK), TILE), jnp.float32),
            pltpu.SemaphoreType.DMA((units, peers)),
            pltpu.SemaphoreType.DMA((units, peers)),
            pltpu.SemaphoreType.DMA((units, 4)),
            pltpu.SemaphoreType.DMA((units, 4)),
            pltpu.SemaphoreType.DMA((units, per)),
            pltpu.SemaphoreType.DMA((units, per)),
            pltpu.SemaphoreType.DMA((parts,)),
            pltpu.SemaphoreType.DMA((parts,)),
            pltpu.SemaphoreType.DMA((units,)),
            pltpu.SemaphoreType.DMA((parts,)),
        ],
        compiler_params=pltpu.CompilerParams(collective_id=1, has_side_effects=True, vmem_limit_bytes=VMEM_BYTES),
        name="return_partials",
    )(order, outbound)


def stacked(x, axis):
    return jnp.concatenate(halves(x), axis=axis)


def folded(x):
    tall = x[:, :TILE] + x[:, TILE:]
    return tall[:TILE] + tall[TILE:]


def finish_kernel(group, place, own_ref, mirror_ref, left_ref, right_ref, out_ref):
    left = stacked(jnp.transpose(left_ref[...]), 0)
    for i in range(group):
        symmetric = own_ref[i] + jnp.transpose(mirror_ref[i])
        leftward = folded(jnp.dot(left, stacked(symmetric, 1), preferred_element_type=jnp.float32))
        right = stacked(right_ref[i * TILE:(i + 1) * TILE, :], 1)
        out_ref[:, i * TILE:(i + 1) * TILE] = folded(
            jnp.dot(stacked(leftward, 0), right, preferred_element_type=jnp.float32))


def finish(place, own, mirror, orthogonalizers):
    per = own.shape[0]
    group = 4
    steps = per // group
    tile = pl.BlockSpec((group, TILE, TILE), lambda j, t: (j, 0, 0))
    return pl.pallas_call(
        functools.partial(finish_kernel, group),
        out_shape=jax.ShapeDtypeStruct((TILE, per * TILE), jnp.float32),
        grid_spec=pltpu.PrefetchScalarGridSpec(
            num_scalar_prefetch=1,
            grid=(steps,),
            in_specs=[
                tile, tile,
                pl.BlockSpec((TILE, TILE), lambda j, t: (t[0], 0)),
                pl.BlockSpec((group * TILE, TILE), lambda j, t: (t[1] * steps + j, 0)),
            ],
            out_specs=pl.BlockSpec((TILE, group * TILE), lambda j, t: (0, j)),
        ),
        name="finish",
    )(place, own, mirror, orthogonalizers, orthogonalizers)


def column_order(cols, n_tile):
    count = cols.shape[0]
    spot = jnp.arange(count, dtype=jnp.int32)
    key = jnp.where(cols < 0, n_tile, cols)
    before = (key[None, :] < key[:, None]) | ((key[None, :] == key[:, None]) & (spot[None, :] < spot[:, None]))
    place = jnp.sum(before, axis=1)
    at = place[None, :] == spot[:, None]
    order = jnp.sum(jnp.where(at, spot[None, :], 0), axis=1)
    starts = jnp.any(at & (~jnp.any(before & (key[None, :] == key[:, None]), axis=1))[None, :], axis=1)
    ends = jnp.sum(key[None, :] <= spot[:, None], axis=1) - 1
    held = jnp.any(key[None, :] == spot[:, None], axis=1) & (spot < n_tile)
    return jnp.stack([order, starts.astype(jnp.int32), jnp.maximum(ends, 0), held.astype(jnp.int32)]).astype(jnp.int32)


def local(density, factors, orthogonalizers, slot_pairs, density_source, density_column, target_row, target_column):
    n_tile, n_aux = lax.axis_size("tile"), lax.axis_size("aux")
    me, aux = lax.axis_index("tile"), lax.axis_index("aux")
    tasks = slot_pairs.shape[0]

    def group(rows):
        grid = rows.reshape(n_tile, n_aux, tasks)
        return lax.dynamic_index_in_dim(grid, aux, 1, False)

    sources, columns = group(density_source), group(density_column)
    targets, target_cols = group(target_row), group(target_column)
    own_source = lax.dynamic_index_in_dim(sources, me, 0, False)
    own_target = lax.dynamic_index_in_dim(targets, me, 0, False)
    send_cols = jnp.concatenate([slot_columns(sources, columns, me), slot_columns(sources, columns, opposite(me))])
    sources_k = served(me, jnp.arange(n_tile // 2, dtype=jnp.int32), n_tile)
    pick = sources_k[:, None] == jnp.arange(n_tile, dtype=jnp.int32)[None, :]

    def order_for(row):
        slot_cols = slot_columns(targets, target_cols, row)
        cols = jnp.sum(jnp.where(pick[:, :, None], slot_cols[None] + 1, 0), axis=1) - 1
        return column_order(cols.reshape(-1), n_tile)

    table = jnp.stack([
        own_source * CAP + ranks_of(own_source),
        slot_pairs[:, 0],
        slot_pairs[:, 1],
        own_target * CAP + ranks_of(own_target),
    ])
    slots = n_tile * CAP
    incoming = fetch_density(density, jnp.maximum(send_cols, 0), n_tile, n_aux)
    outbound = run_tasks(table, incoming.reshape(slots, TILE, TILE), factors, slots)
    own, mirror = return_partials(
        jnp.concatenate([order_for(opposite(me)), order_for(me)]), outbound.reshape(n_tile, CAP, TILE, TILE), n_tile, n_aux)
    return finish(jnp.stack([me, aux]).astype(jnp.int32), own, mirror, orthogonalizers)


def solution(mesh):
    return jax.shard_map(
        local,
        mesh=mesh,
        in_specs=(
            P("tile", "aux"),
            P(("tile", "aux"), None, None, None),
            P(),
            P(("tile", "aux"), None),
            P(),
            P(),
            P(),
            P(),
        ),
        out_specs=P("tile", "aux"),
        check_vma=False,
    )
```

```python
import functools
import jax
import jax.numpy as jnp
from jax import lax
from jax.experimental import pallas as pl
from jax.experimental.pallas import tpu as pltpu
from jax.sharding import PartitionSpec as P

MESH = pl.DeviceIdType.MESH
TILE = 128
CAP = 2
VMEM_BYTES = 56 * 1024 * 1024
RING = 8
CORES = 2
ORDER = 13
ROWS = (48, 80)
SPANS = [(sum(ROWS[:r]), n) for r, n in enumerate(ROWS)]
BACK = (48, 40, 24, 16)
AHEAD = 3
BACK_SPANS = [(sum(BACK[:r]), n) for r, n in enumerate(BACK)]


def halves(x):
    top = x.astype(jnp.bfloat16)
    rest = (x - top.astype(jnp.float32)).astype(jnp.bfloat16)
    return top, rest


def ranks_of(keys):
    count = keys.shape[-1]
    spot = jnp.arange(count)
    earlier = spot[None, :] < spot[:, None]
    return jnp.sum((keys[..., :, None] == keys[..., None, :]) & earlier, axis=-1).astype(jnp.int32)


def slot_columns(keys, columns, wanted):
    ranking = ranks_of(keys)
    picked = []
    for level in range(CAP):
        chosen = (keys == wanted) & (ranking == level)
        picked.append(jnp.sum(jnp.where(chosen, columns + 1, 0), axis=-1) - 1)
    return jnp.stack(picked, axis=-1)


def spot_of(tile):
    return tile // (RING * CORES), lax.rem(tile // CORES, RING), lax.rem(tile, CORES)


def tile_of(x, z, core):
    return (x * RING + z) * CORES + core


def opposite(tile):
    x, z, core = spot_of(tile)
    return tile_of(x, lax.rem(z + RING // 2, RING), core)


def reach(turn, core):
    far = jnp.where(core == 0, 2, RING - 2)
    return jnp.where(turn == 3, far, jnp.where(turn == 2, RING - 1, turn))


def served(tile, k, n_tile):
    x, z, core = spot_of(tile)
    across = n_tile // (RING * CORES)
    to_core = lax.rem(core + lax.rem(k, CORES), CORES)
    turn = lax.rem(k // CORES, 4)
    return tile_of(lax.rem(x + k // (4 * CORES), across), lax.rem(z + reach(turn, core), RING), to_core)


def holder(tile, k, n_tile):
    x, z, core = spot_of(tile)
    across = n_tile // (RING * CORES)
    from_core = lax.rem(core + CORES - lax.rem(k, CORES), CORES)
    turn = lax.rem(k // CORES, 4)
    return tile_of(lax.rem(x + across - k // (4 * CORES), across), lax.rem(z + RING - reach(turn, from_core), RING), from_core)


def density_kernel(n_tile, n_aux, cols_ref, dens_ref, out_ref, *scratch):
    parts = len(ROWS)
    slabs, outgoing = scratch[:2 * parts], scratch[2 * parts:4 * parts]
    y_send, y_recv, z_send, z_recv, t_send, t_recv, own_sem = scratch[4 * parts:]
    me = lax.axis_index("tile")
    aux = lax.axis_index("aux")
    far_side = opposite(me)
    homes = [me] * parts + [far_side] * parts
    spans = SPANS * 2
    up, down = lax.rem(aux + 1, n_aux), lax.rem(aux + n_aux - 1, n_aux)
    across = lax.rem(aux + 2, n_aux)
    per = dens_ref.shape[1] // TILE
    half = per // 2
    peers = n_tile // 2
    barrier = pltpu.get_barrier_semaphore()

    @pl.loop(1, n_tile)
    def _(s):
        pl.semaphore_signal(barrier, inc=1, device_id={"tile": lax.rem(me + s, n_tile), "aux": aux}, device_id_type=MESH)

    for other in (up, down):
        pl.semaphore_signal(barrier, inc=1, device_id={"tile": me, "aux": other}, device_id_type=MESH)
    for r, (start, length) in enumerate(SPANS):
        for j in range(per):
            slabs[r][aux * per + j] = dens_ref[start:start + length, j * TILE:(j + 1) * TILE]
    pl.semaphore_wait(barrier, n_tile + 1)

    def near(r, owner, start, length, index, other):
        where = slabs[r].at[pl.ds(owner * per + start, length)]
        return pltpu.make_async_remote_copy(
            src_ref=where, dst_ref=where, send_sem=y_send.at[r, index], recv_sem=y_recv.at[r, index],
            device_id={"tile": me, "aux": other}, device_id_type=MESH)

    def swap(r):
        mine = pl.ds(aux * per, per)
        return pltpu.make_async_remote_copy(
            src_ref=slabs[r].at[mine], dst_ref=slabs[parts + r].at[mine], send_sem=z_send.at[r], recv_sem=z_recv.at[r],
            device_id={"tile": far_side, "aux": aux}, device_id_type=MESH)

    def home_rows(tile, r):
        return out_ref.at[tile, :, pl.ds(*spans[r])]

    def ship(r, k):
        return pltpu.make_async_remote_copy(
            src_ref=outgoing[r].at[k], dst_ref=home_rows(homes[r], r),
            send_sem=t_send.at[r, k], recv_sem=t_recv.at[r, k],
            device_id={"tile": served(me, k, n_tile), "aux": aux}, device_id_type=MESH)

    def own(r):
        return pltpu.make_async_copy(outgoing[r].at[0], home_rows(homes[r], r), own_sem.at[r])

    def first(r):
        near(r, aux, 0, per, 0, up).start()
        near(r, aux, 0, per, 1, down).start()

    def second(r):
        near(r, down, 0, per, 0, up).wait_recv()
        near(r, down, 0, half, 2, up).start()
        near(r, up, 0, per, 1, down).wait_recv()
        near(r, up, half, half, 3, down).start()

    def gathered(r):
        near(r, across, 0, half, 2, up).wait_recv()
        near(r, across, half, half, 3, down).wait_recv()

    def send_all(r):
        base = 0 if r < parts else n_tile

        @pl.loop(0, peers)
        def _(s):
            k = lax.rem(s * ORDER, peers)
            dest = base + served(me, k, n_tile)
            for level in range(CAP):
                outgoing[r][k, level] = slabs[r][cols_ref[dest, level]]

            @pl.when(s > 0)
            def _():
                ship(r, k).start()

        own(r).start()

    def step_copy(r):
        swap(r).wait_recv()
        first(parts + r)

    first(0)
    swap(0).start()
    first(1)
    swap(1).start()
    second(0)
    gathered(0)
    send_all(0)
    second(1)
    step_copy(0)
    gathered(1)
    second(2)
    send_all(1)
    gathered(2)
    step_copy(1)
    send_all(2)
    second(3)
    gathered(3)
    send_all(3)

    for r in range(2 * parts):
        @pl.loop(1, peers)
        def _(k):
            source = holder(me, k, n_tile)
            home = source if r < parts else opposite(source)
            pltpu.make_async_remote_copy(
                src_ref=outgoing[r].at[k], dst_ref=home_rows(home, r),
                send_sem=t_send.at[r, k], recv_sem=t_recv.at[r, k],
                device_id={"tile": source, "aux": aux}, device_id_type=MESH).wait_recv()
            ship(r, k).wait_send()

        own(r).wait()
        near(r, aux, 0, per, 0, up).wait_send()
        near(r, aux, 0, per, 1, down).wait_send()
        near(r, down, 0, half, 2, up).wait_send()
        near(r, up, half, half, 3, down).wait_send()
        if r < parts:
            swap(r).wait_send()


def fetch_density(density, cols, n_tile, n_aux):
    units = 2 * len(ROWS)
    return pl.pallas_call(
        functools.partial(density_kernel, n_tile, n_aux),
        out_shape=jax.ShapeDtypeStruct((n_tile, CAP, TILE, TILE), jnp.float32),
        in_specs=[pl.BlockSpec(memory_space=pltpu.SMEM), pl.BlockSpec(memory_space=pltpu.VMEM)],
        out_specs=pl.BlockSpec(memory_space=pl.ANY),
        scratch_shapes=[pltpu.VMEM((n_tile, n, TILE), jnp.float32) for n in ROWS * 2]
        + [pltpu.VMEM((n_tile // 2, CAP, n, TILE), jnp.float32) for n in ROWS * 2]
        + [
            pltpu.SemaphoreType.DMA((units, 4)),
            pltpu.SemaphoreType.DMA((units, 4)),
            pltpu.SemaphoreType.DMA((len(ROWS),)),
            pltpu.SemaphoreType.DMA((len(ROWS),)),
            pltpu.SemaphoreType.DMA((units, n_tile // 2)),
            pltpu.SemaphoreType.DMA((units, n_tile // 2)),
            pltpu.SemaphoreType.DMA((units,)),
        ],
        compiler_params=pltpu.CompilerParams(collective_id=0, has_side_effects=True, vmem_limit_bytes=VMEM_BYTES),
        name="fetch_density",
    )(cols, density)


def task_kernel(pair_count, table, dens_ref, fact_ref, out_ref, split, lhs):
    q = pl.program_id(0)
    last = pl.num_programs(0) - 2
    now = lax.rem(q, 2)

    @pl.when(q == 0)
    def _():
        lhs[1] = jnp.zeros(lhs.shape[1:], lhs.dtype)

        @pl.loop(0, fact_ref.shape[0])
        def _(slot):
            for p in range(pair_count):
                rows = slice(p * 2 * TILE, (p + 1) * 2 * TILE)
                top, rest = halves(fact_ref[slot, rows, :])
                split[slot, rows, 0:TILE] = top
                split[slot, rows, TILE:2 * TILE] = rest

    left, right = table[1, jnp.minimum(q, last)], table[2, jnp.maximum(q - 1, 0)]
    top, rest = halves(dens_ref[0])
    row = jnp.concatenate([top, rest], axis=1)
    weights = jnp.concatenate([row, row], axis=0)
    total = jnp.dot(lhs[1 - now], split[right], preferred_element_type=jnp.float32)
    for p in range(pair_count):
        rows = slice(p * 2 * TILE, (p + 1) * 2 * TILE)
        wide = jnp.dot(split[left, rows, :], weights, preferred_element_type=jnp.float32)
        top, rest = halves(wide[:, :TILE] + wide[:, TILE:])
        lhs[now, :, rows] = jnp.concatenate(
            [jnp.concatenate([top[:TILE], top[TILE:]], axis=1), jnp.concatenate([rest[:TILE], rest[TILE:]], axis=1)], axis=0)
    tall = total[:, :TILE] + total[:, TILE:]
    out_ref[0] = tall[:TILE] + tall[TILE:]


def run_tasks(table, incoming, factors, slots):
    slot_count, aux_funcs = factors.shape[:2]
    flat = factors.reshape(slot_count, aux_funcs * TILE, TILE)
    task_count = table.shape[1]
    return pl.pallas_call(
        functools.partial(task_kernel, aux_funcs // 2),
        out_shape=jax.ShapeDtypeStruct((slots, TILE, TILE), jnp.float32),
        grid_spec=pltpu.PrefetchScalarGridSpec(
            num_scalar_prefetch=1,
            grid=(task_count + 1,),
            in_specs=[
                pl.BlockSpec((1, TILE, TILE), lambda q, t: (t[0, jnp.minimum(q, task_count - 1)], 0, 0)),
                pl.BlockSpec(flat.shape, lambda q, t: (0, 0, 0), pipeline_mode=pl.Buffered(1)),
            ],
            out_specs=pl.BlockSpec((1, TILE, TILE), lambda q, t: (t[3, jnp.maximum(q - 1, 0)], 0, 0)),
            scratch_shapes=[
                pltpu.VMEM((slot_count, aux_funcs * TILE, 2 * TILE), jnp.bfloat16),
                pltpu.VMEM((2, 2 * TILE, aux_funcs * TILE), jnp.bfloat16),
            ],
        ),
        compiler_params=pltpu.CompilerParams(vmem_limit_bytes=VMEM_BYTES),
        name="run_tasks",
    )(table, incoming, flat)


def return_kernel(n_tile, n_aux, order_ref, src_ref, own_ref, mirror_ref, *scratch):
    parts = len(BACK)
    units = 2 * parts
    groups = [scratch[i * units:(i + 1) * units] for i in range(8)]
    arrived, rows, half_up, half_down, full_up, full_down, outgoing, summed = groups
    swapped = scratch[8 * units:8 * units + parts]
    (running, t_send, t_recv, y_send, y_recv, m_send, m_recv, z_send, z_recv, own_sem, out_sem) = scratch[8 * units + parts:]
    me = lax.axis_index("tile")
    aux = lax.axis_index("aux")
    far_side = opposite(me)
    up, down = lax.rem(aux + 1, n_aux), lax.rem(aux + n_aux - 1, n_aux)
    across = lax.rem(aux + 2, n_aux)
    per = n_tile // n_aux
    half = per // 2
    peers = n_tile // 2
    block = me // per
    slot = lax.rem(me, per)
    alike = block == aux
    barrier = pltpu.get_barrier_semaphore()

    @pl.loop(1, n_tile)
    def _(s):
        pl.semaphore_signal(barrier, inc=1, device_id={"tile": lax.rem(me + s, n_tile), "aux": aux}, device_id_type=MESH)

    for other in (up, down):
        pl.semaphore_signal(barrier, inc=1, device_id={"tile": me, "aux": other}, device_id_type=MESH)

    @pl.loop(0, per)
    def _(j):
        @pl.when(jnp.logical_not(alike & (j == slot)))
        def _():
            pl.semaphore_signal(barrier, inc=1, device_id={"tile": aux * per + j, "aux": block}, device_id_type=MESH)

    pl.semaphore_wait(barrier, n_tile + jnp.where(alike, per, per + 1))

    def span(u):
        return pl.ds(*BACK_SPANS[u // 2])

    def home_of(tile, u):
        return opposite(tile) if u % 2 == 0 else tile

    def far(u, k):
        dest = holder(me, k, n_tile)
        return pltpu.make_async_remote_copy(
            src_ref=src_ref.at[home_of(dest, u), :, span(u)], dst_ref=arrived[u].at[pl.ds(k * CAP, CAP)],
            send_sem=t_send.at[u, k], recv_sem=t_recv.at[u, k],
            device_id={"tile": dest, "aux": aux}, device_id_type=MESH)

    def own(u):
        return pltpu.make_async_copy(src_ref.at[home_of(me, u), :, span(u)], arrived[u].at[pl.ds(0, CAP)], own_sem.at[u])

    def begin(u):
        @pl.loop(1, peers)
        def _(s):
            far(u, lax.rem(s * ORDER, peers)).start()

        own(u).start()

    def near(src, dst, u, index, other):
        return pltpu.make_async_remote_copy(
            src_ref=src, dst_ref=dst, send_sem=y_send.at[u, index], recv_sem=y_recv.at[u, index],
            device_id={"tile": me, "aux": other}, device_id_type=MESH)

    def steps(u):
        return (
            near(rows[u].at[pl.ds(across * per, half)], half_up[u], u, 0, up),
            near(rows[u].at[pl.ds(across * per + half, half)], half_down[u], u, 1, down),
            near(outgoing[u].at[0], full_up[u], u, 2, up),
            near(outgoing[u].at[1], full_down[u], u, 3, down),
        )

    def swap(p):
        return pltpu.make_async_remote_copy(
            src_ref=summed[2 * p], dst_ref=swapped[p], send_sem=z_send.at[p], recv_sem=z_recv.at[p],
            device_id={"tile": far_side, "aux": aux}, device_id_type=MESH)

    def send(u, j):
        return pltpu.make_async_remote_copy(
            src_ref=summed[u].at[j], dst_ref=mirror_ref.at[slot, span(u)],
            send_sem=m_send.at[u, j], recv_sem=m_recv.at[u, slot],
            device_id={"tile": aux * per + j, "aux": block}, device_id_type=MESH)

    def keep(u, j):
        return pltpu.make_async_copy(summed[u].at[j], mirror_ref.at[j, span(u)], m_send.at[u, j])

    def settle(u):
        return pltpu.make_async_copy(summed[u], own_ref.at[:, span(u)], out_sem.at[u // 2])

    def collect(u):
        length = BACK[u // 2]
        table = (u % 2) * 4

        @pl.loop(1, peers)
        def _(k):
            pltpu.make_async_remote_copy(
                src_ref=src_ref.at[me, :, span(u)], dst_ref=arrived[u].at[pl.ds(k * CAP, CAP)],
                send_sem=t_send.at[u, k], recv_sem=t_recv.at[u, k],
                device_id={"tile": served(me, k, n_tile), "aux": aux}, device_id_type=MESH).wait_recv()

        own(u).wait()
        if u + AHEAD < units:
            begin(u + AHEAD)

        def add(i, carry):
            for v in range(4):
                k = i * 4 + v
                carry = jnp.where(order_ref[table + 1, k] > 0, 0.0, carry) + arrived[u][order_ref[table, k]]
                running[k, 0:length] = carry
            return carry

        lax.fori_loop(0, peers * CAP // 4, add, jnp.zeros((length, TILE), jnp.float32))

        @pl.loop(0, n_tile)
        def _(b):
            rows[u][b] = jnp.where(order_ref[table + 3, b] > 0, running[order_ref[table + 2, b], 0:length], 0.0)

        first_up, first_down, _, _ = steps(u)
        first_up.start()
        first_down.start()

        @pl.loop(0, half)
        def _(j):
            outgoing[u][0, half + j] = rows[u][up * per + half + j]
            outgoing[u][1, j] = rows[u][down * per + j]

    def pass_on(u):
        first_up, first_down, second_up, second_down = steps(u)
        first_up.wait_recv()

        @pl.loop(0, half)
        def _(j):
            outgoing[u][0, j] = rows[u][up * per + j] + half_up[u][j]

        second_up.start()
        first_down.wait_recv()

        @pl.loop(0, half)
        def _(j):
            outgoing[u][1, half + j] = rows[u][down * per + half + j] + half_down[u][j]

        second_down.start()

    def conclude(u):
        _, _, second_up, second_down = steps(u)
        second_up.wait_recv()
        second_down.wait_recv()
        if u % 2 == 0:
            @pl.loop(0, per)
            def _(j):
                summed[u][j] = rows[u][aux * per + j] + (full_up[u][j] + full_down[u][j])

            swap(u // 2).start()
        else:
            swap(u // 2).wait_recv()

            @pl.loop(0, per)
            def _(j):
                summed[u][j] = (rows[u][aux * per + j] + swapped[u // 2][j]) + (full_up[u][j] + full_down[u][j])
                mine = alike & (j == slot)

                @pl.when(jnp.logical_not(mine))
                def _():
                    send(u, j).start()

                @pl.when(mine)
                def _():
                    keep(u, j).start()

            settle(u).start()

    for u in range(AHEAD):
        begin(u)
    for u in range(units):
        collect(u)
        if u > 0:
            conclude(u - 1)
        pass_on(u)
    conclude(units - 1)

    for u in range(units):
        @pl.loop(1, peers)
        def _(k):
            far(u, k).wait_send()

        for copy in steps(u):
            copy.wait_send()
        if u % 2 == 0:
            swap(u // 2).wait_send()
        else:
            @pl.loop(0, per)
            def _(j):
                mine = alike & (j == slot)

                @pl.when(jnp.logical_not(mine))
                def _():
                    pltpu.make_async_remote_copy(
                        src_ref=summed[u].at[j], dst_ref=mirror_ref.at[j, span(u)],
                        send_sem=m_send.at[u, j], recv_sem=m_recv.at[u, j],
                        device_id={"tile": aux * per + j, "aux": block}, device_id_type=MESH).wait_recv()
                    send(u, j).wait_send()

                @pl.when(mine)
                def _():
                    keep(u, j).wait()

            settle(u).wait()


def return_partials(order, outbound, n_tile, n_aux):
    per = n_tile // n_aux
    peers = n_tile // 2
    parts = len(BACK)
    units = 2 * parts
    lengths = [n for n in BACK for _ in range(2)]
    shape = jax.ShapeDtypeStruct((per, TILE, TILE), jnp.float32)
    leads = [(peers * CAP,), (n_tile,), (per // 2,), (per // 2,), (per,), (per,), (2, per), (per,)]
    return pl.pallas_call(
        functools.partial(return_kernel, n_tile, n_aux),
        out_shape=(shape, shape),
        in_specs=[pl.BlockSpec(memory_space=pltpu.SMEM), pl.BlockSpec(memory_space=pl.ANY)],
        out_specs=(pl.BlockSpec(memory_space=pl.ANY), pl.BlockSpec(memory_space=pl.ANY)),
        scratch_shapes=[pltpu.VMEM(lead + (n, TILE), jnp.float32) for lead in leads for n in lengths]
        + [pltpu.VMEM((per, n, TILE), jnp.float32) for n in BACK]
        + [
            pltpu.VMEM((peers * CAP, max(BACK), TILE), jnp.float32),
            pltpu.SemaphoreType.DMA((units, peers)),
            pltpu.SemaphoreType.DMA((units, peers)),
            pltpu.SemaphoreType.DMA((units, 4)),
            pltpu.SemaphoreType.DMA((units, 4)),
            pltpu.SemaphoreType.DMA((units, per)),
            pltpu.SemaphoreType.DMA((units, per)),
            pltpu.SemaphoreType.DMA((parts,)),
            pltpu.SemaphoreType.DMA((parts,)),
            pltpu.SemaphoreType.DMA((units,)),
            pltpu.SemaphoreType.DMA((parts,)),
        ],
        compiler_params=pltpu.CompilerParams(collective_id=1, has_side_effects=True, vmem_limit_bytes=VMEM_BYTES),
        name="return_partials",
    )(order, outbound)


def stacked(x, axis):
    return jnp.concatenate(halves(x), axis=axis)


def folded(x):
    tall = x[:, :TILE] + x[:, TILE:]
    return tall[:TILE] + tall[TILE:]


def finish_kernel(group, place, own_ref, mirror_ref, left_ref, right_ref, out_ref):
    left = stacked(jnp.transpose(left_ref[...]), 0)
    for i in range(group):
        symmetric = own_ref[i] + jnp.transpose(mirror_ref[i])
        leftward = folded(jnp.dot(left, stacked(symmetric, 1), preferred_element_type=jnp.float32))
        right = stacked(right_ref[i * TILE:(i + 1) * TILE, :], 1)
        out_ref[:, i * TILE:(i + 1) * TILE] = folded(
            jnp.dot(stacked(leftward, 0), right, preferred_element_type=jnp.float32))


def finish(place, own, mirror, orthogonalizers):
    per = own.shape[0]
    group = 4
    steps = per // group
    tile = pl.BlockSpec((group, TILE, TILE), lambda j, t: (j, 0, 0))
    return pl.pallas_call(
        functools.partial(finish_kernel, group),
        out_shape=jax.ShapeDtypeStruct((TILE, per * TILE), jnp.float32),
        grid_spec=pltpu.PrefetchScalarGridSpec(
            num_scalar_prefetch=1,
            grid=(steps,),
            in_specs=[
                tile, tile,
                pl.BlockSpec((TILE, TILE), lambda j, t: (t[0], 0)),
                pl.BlockSpec((group * TILE, TILE), lambda j, t: (t[1] * steps + j, 0)),
            ],
            out_specs=pl.BlockSpec((TILE, group * TILE), lambda j, t: (0, j)),
        ),
        name="finish",
    )(place, own, mirror, orthogonalizers, orthogonalizers)


def column_order(cols, n_tile):
    count = cols.shape[0]
    spot = jnp.arange(count, dtype=jnp.int32)
    key = jnp.where(cols < 0, n_tile, cols)
    before = (key[None, :] < key[:, None]) | ((key[None, :] == key[:, None]) & (spot[None, :] < spot[:, None]))
    place = jnp.sum(before, axis=1)
    at = place[None, :] == spot[:, None]
    order = jnp.sum(jnp.where(at, spot[None, :], 0), axis=1)
    starts = jnp.any(at & (~jnp.any(before & (key[None, :] == key[:, None]), axis=1))[None, :], axis=1)
    ends = jnp.sum(key[None, :] <= spot[:, None], axis=1) - 1
    held = jnp.any(key[None, :] == spot[:, None], axis=1) & (spot < n_tile)
    return jnp.stack([order, starts.astype(jnp.int32), jnp.maximum(ends, 0), held.astype(jnp.int32)]).astype(jnp.int32)


def local(density, factors, orthogonalizers, slot_pairs, density_source, density_column, target_row, target_column):
    n_tile, n_aux = lax.axis_size("tile"), lax.axis_size("aux")
    me, aux = lax.axis_index("tile"), lax.axis_index("aux")
    tasks = slot_pairs.shape[0]

    packed = density_source
    for other in (density_column, target_row, target_column):
        packed = packed * n_tile + other
    packed = lax.dynamic_index_in_dim(packed.reshape(n_tile, n_aux, tasks), aux, 1, False)
    target_cols = packed % n_tile
    targets = (packed // n_tile) % n_tile
    columns = (packed // n_tile ** 2) % n_tile
    sources = packed // n_tile ** 3
    own_source = lax.dynamic_index_in_dim(sources, me, 0, False)
    own_target = lax.dynamic_index_in_dim(targets, me, 0, False)
    send_cols = jnp.concatenate([slot_columns(sources, columns, me), slot_columns(sources, columns, opposite(me))])
    sources_k = served(me, jnp.arange(n_tile // 2, dtype=jnp.int32), n_tile)
    pick = sources_k[:, None] == jnp.arange(n_tile, dtype=jnp.int32)[None, :]

    def order_for(row):
        slot_cols = slot_columns(targets, target_cols, row)
        cols = jnp.sum(jnp.where(pick[:, :, None], slot_cols[None] + 1, 0), axis=1) - 1
        return column_order(cols.reshape(-1), n_tile)

    table = jnp.stack([
        own_source * CAP + ranks_of(own_source),
        slot_pairs[:, 0],
        slot_pairs[:, 1],
        own_target * CAP + ranks_of(own_target),
    ])
    slots = n_tile * CAP
    incoming = fetch_density(density, jnp.maximum(send_cols, 0), n_tile, n_aux)
    outbound = run_tasks(table, incoming.reshape(slots, TILE, TILE), factors, slots)
    own, mirror = return_partials(
        jnp.concatenate([order_for(opposite(me)), order_for(me)]), outbound.reshape(n_tile, CAP, TILE, TILE), n_tile, n_aux)
    return finish(jnp.stack([me, aux]).astype(jnp.int32), own, mirror, orthogonalizers)


def solution(mesh):
    return jax.shard_map(
        local,
        mesh=mesh,
        in_specs=(
            P("tile", "aux"),
            P(("tile", "aux"), None, None, None),
            P(),
            P(("tile", "aux"), None),
            P(),
            P(),
            P(),
            P(),
        ),
        out_specs=P("tile", "aux"),
        check_vma=False,
    )
```

```python
import functools
import jax
import jax.numpy as jnp
from jax import lax
from jax.experimental import pallas as pl
from jax.experimental.pallas import tpu as pltpu
from jax.sharding import PartitionSpec as P

MESH = pl.DeviceIdType.MESH
TILE = 128
CAP = 2
VMEM_BYTES = 56 * 1024 * 1024
RING = 8
CORES = 2
ORDER = 13
ROWS = (32, 48, 48)
SPANS = [(sum(ROWS[:r]), n) for r, n in enumerate(ROWS)]
BACK = (48, 40, 24, 16)
AHEAD = 2
BACK_SPANS = [(sum(BACK[:r]), n) for r, n in enumerate(BACK)]


def halves(x):
    top = x.astype(jnp.bfloat16)
    rest = (x - top.astype(jnp.float32)).astype(jnp.bfloat16)
    return top, rest


def ranks_of(keys):
    count = keys.shape[-1]
    spot = jnp.arange(count)
    earlier = spot[None, :] < spot[:, None]
    return jnp.sum((keys[..., :, None] == keys[..., None, :]) & earlier, axis=-1).astype(jnp.int32)


def slot_columns(keys, columns, wanted):
    ranking = ranks_of(keys)
    picked = []
    for level in range(CAP):
        chosen = (keys == wanted) & (ranking == level)
        picked.append(jnp.sum(jnp.where(chosen, columns + 1, 0), axis=-1) - 1)
    return jnp.stack(picked, axis=-1)


def spot_of(tile):
    return tile // (RING * CORES), lax.rem(tile // CORES, RING), lax.rem(tile, CORES)


def tile_of(x, z, core):
    return (x * RING + z) * CORES + core


def copy_at(tile):
    x, z, core = spot_of(tile)
    return tile_of(x, lax.rem(z + 3 + (RING - 6) * core, RING), core)


def copy_of(tile):
    x, z, core = spot_of(tile)
    return tile_of(x, lax.rem(z + RING - 3 - (RING - 6) * core, RING), core)


def reach(turn, core, copy):
    far = jnp.where(core == 0, RING - 2, 2)
    if copy:
        far = RING - far
    return jnp.where(turn == 3, far, jnp.where(turn == 2, RING - 1, turn))


def served(tile, k, n_tile, copy):
    x, z, core = spot_of(tile)
    across = n_tile // (RING * CORES)
    to_core = lax.rem(core + lax.rem(k, CORES), CORES)
    turn = lax.rem(k // CORES, 4)
    return tile_of(lax.rem(x + k // (4 * CORES), across), lax.rem(z + reach(turn, core, copy), RING), to_core)


def holder(tile, k, n_tile, copy):
    x, z, core = spot_of(tile)
    across = n_tile // (RING * CORES)
    from_core = lax.rem(core + CORES - lax.rem(k, CORES), CORES)
    turn = lax.rem(k // CORES, 4)
    z_from = lax.rem(z + RING - reach(turn, from_core, copy), RING)
    return tile_of(lax.rem(x + across - k // (4 * CORES), across), z_from, from_core)


def density_kernel(n_tile, n_aux, cols_ref, dens_ref, out_ref, *scratch):
    parts = len(ROWS)
    slabs, outgoing = scratch[:2 * parts], scratch[2 * parts:4 * parts]
    y_send, y_recv, z_send, z_recv, t_send, t_recv, own_sem = scratch[4 * parts:]
    me = lax.axis_index("tile")
    aux = lax.axis_index("aux")
    homes = [me] * parts + [copy_of(me)] * parts
    spans = SPANS * 2
    up, down = lax.rem(aux + 1, n_aux), lax.rem(aux + n_aux - 1, n_aux)
    across = lax.rem(aux + 2, n_aux)
    per = dens_ref.shape[1] // TILE
    half = per // 2
    peers = n_tile // 2
    barrier = pltpu.get_barrier_semaphore()

    @pl.loop(1, n_tile)
    def _(s):
        pl.semaphore_signal(barrier, inc=1, device_id={"tile": lax.rem(me + s, n_tile), "aux": aux}, device_id_type=MESH)

    for other in (up, down):
        pl.semaphore_signal(barrier, inc=1, device_id={"tile": me, "aux": other}, device_id_type=MESH)
    for r, (start, length) in enumerate(SPANS):
        for j in range(per):
            slabs[r][aux * per + j] = dens_ref[start:start + length, j * TILE:(j + 1) * TILE]
    pl.semaphore_wait(barrier, n_tile + 1)

    def near(r, owner, start, length, index, other):
        where = slabs[r].at[pl.ds(owner * per + start, length)]
        return pltpu.make_async_remote_copy(
            src_ref=where, dst_ref=where, send_sem=y_send.at[r, index], recv_sem=y_recv.at[r, index],
            device_id={"tile": me, "aux": other}, device_id_type=MESH)

    def swap(r):
        mine = pl.ds(aux * per, per)
        return pltpu.make_async_remote_copy(
            src_ref=slabs[r].at[mine], dst_ref=slabs[parts + r].at[mine], send_sem=z_send.at[r], recv_sem=z_recv.at[r],
            device_id={"tile": copy_at(me), "aux": aux}, device_id_type=MESH)

    def home_rows(tile, r):
        return out_ref.at[tile, :, pl.ds(*spans[r])]

    def ship(r, k):
        return pltpu.make_async_remote_copy(
            src_ref=outgoing[r].at[k], dst_ref=home_rows(homes[r], r),
            send_sem=t_send.at[r, k], recv_sem=t_recv.at[r, k],
            device_id={"tile": served(me, k, n_tile, r >= parts), "aux": aux}, device_id_type=MESH)

    def own(r):
        return pltpu.make_async_copy(outgoing[r].at[0], home_rows(homes[r], r), own_sem.at[r])

    def first(r):
        near(r, aux, 0, per, 0, up).start()
        near(r, aux, 0, per, 1, down).start()

    def second(r):
        near(r, down, 0, per, 0, up).wait_recv()
        near(r, down, 0, half, 2, up).start()
        near(r, up, 0, per, 1, down).wait_recv()
        near(r, up, half, half, 3, down).start()

    def gathered(r):
        near(r, across, 0, half, 2, up).wait_recv()
        near(r, across, half, half, 3, down).wait_recv()

    def send_all(r):
        base = 0 if r < parts else n_tile

        @pl.loop(0, peers)
        def _(s):
            k = lax.rem(s * ORDER, peers)
            dest = base + served(me, k, n_tile, r >= parts)
            for level in range(CAP):
                outgoing[r][k, level] = slabs[r][cols_ref[dest, level]]

            @pl.when(s > 0)
            def _():
                ship(r, k).start()

        own(r).start()

    def step_copy(r):
        swap(r).wait_recv()
        first(parts + r)

    for r in range(parts):
        first(r)
        swap(r).start()
    second(0)
    for r in range(2 * parts):
        gathered(r)
        if r + 1 < 2 * parts:
            second(r + 1)
        send_all(r)
        if r < parts:
            step_copy(r)

    for r in range(2 * parts):
        @pl.loop(1, peers)
        def _(k):
            source = holder(me, k, n_tile, r >= parts)
            home = source if r < parts else copy_of(source)
            pltpu.make_async_remote_copy(
                src_ref=outgoing[r].at[k], dst_ref=home_rows(home, r),
                send_sem=t_send.at[r, k], recv_sem=t_recv.at[r, k],
                device_id={"tile": source, "aux": aux}, device_id_type=MESH).wait_recv()
            ship(r, k).wait_send()

        own(r).wait()
        near(r, aux, 0, per, 0, up).wait_send()
        near(r, aux, 0, per, 1, down).wait_send()
        near(r, down, 0, half, 2, up).wait_send()
        near(r, up, half, half, 3, down).wait_send()
        if r < parts:
            swap(r).wait_send()


def fetch_density(density, cols, n_tile, n_aux):
    units = 2 * len(ROWS)
    return pl.pallas_call(
        functools.partial(density_kernel, n_tile, n_aux),
        out_shape=jax.ShapeDtypeStruct((n_tile, CAP, TILE, TILE), jnp.float32),
        in_specs=[pl.BlockSpec(memory_space=pltpu.SMEM), pl.BlockSpec(memory_space=pltpu.VMEM)],
        out_specs=pl.BlockSpec(memory_space=pl.ANY),
        scratch_shapes=[pltpu.VMEM((n_tile, n, TILE), jnp.float32) for n in ROWS * 2]
        + [pltpu.VMEM((n_tile // 2, CAP, n, TILE), jnp.float32) for n in ROWS * 2]
        + [
            pltpu.SemaphoreType.DMA((units, 4)),
            pltpu.SemaphoreType.DMA((units, 4)),
            pltpu.SemaphoreType.DMA((len(ROWS),)),
            pltpu.SemaphoreType.DMA((len(ROWS),)),
            pltpu.SemaphoreType.DMA((units, n_tile // 2)),
            pltpu.SemaphoreType.DMA((units, n_tile // 2)),
            pltpu.SemaphoreType.DMA((units,)),
        ],
        compiler_params=pltpu.CompilerParams(collective_id=0, has_side_effects=True, vmem_limit_bytes=VMEM_BYTES),
        name="fetch_density",
    )(cols, density)


def task_kernel(pair_count, table, dens_ref, fact_ref, out_ref, split, lhs):
    q = pl.program_id(0)
    last = pl.num_programs(0) - 2
    now = lax.rem(q, 2)

    @pl.when(q == 0)
    def _():
        lhs[1] = jnp.zeros(lhs.shape[1:], lhs.dtype)

        @pl.loop(0, fact_ref.shape[0])
        def _(slot):
            for p in range(pair_count):
                rows = slice(p * 2 * TILE, (p + 1) * 2 * TILE)
                top, rest = halves(fact_ref[slot, rows, :])
                split[slot, rows, 0:TILE] = top
                split[slot, rows, TILE:2 * TILE] = rest

    left, right = table[1, jnp.minimum(q, last)], table[2, jnp.maximum(q - 1, 0)]
    top, rest = halves(dens_ref[0])
    row = jnp.concatenate([top, rest], axis=1)
    weights = jnp.concatenate([row, row], axis=0)
    total = jnp.dot(lhs[1 - now], split[right], preferred_element_type=jnp.float32)
    for p in range(pair_count):
        rows = slice(p * 2 * TILE, (p + 1) * 2 * TILE)
        wide = jnp.dot(split[left, rows, :], weights, preferred_element_type=jnp.float32)
        top, rest = halves(wide[:, :TILE] + wide[:, TILE:])
        lhs[now, :, rows] = jnp.concatenate(
            [jnp.concatenate([top[:TILE], top[TILE:]], axis=1), jnp.concatenate([rest[:TILE], rest[TILE:]], axis=1)], axis=0)
    tall = total[:, :TILE] + total[:, TILE:]
    out_ref[0] = tall[:TILE] + tall[TILE:]


def run_tasks(table, incoming, factors, slots):
    slot_count, aux_funcs = factors.shape[:2]
    flat = factors.reshape(slot_count, aux_funcs * TILE, TILE)
    task_count = table.shape[1]
    return pl.pallas_call(
        functools.partial(task_kernel, aux_funcs // 2),
        out_shape=jax.ShapeDtypeStruct((slots, TILE, TILE), jnp.float32),
        grid_spec=pltpu.PrefetchScalarGridSpec(
            num_scalar_prefetch=1,
            grid=(task_count + 1,),
            in_specs=[
                pl.BlockSpec((1, TILE, TILE), lambda q, t: (t[0, jnp.minimum(q, task_count - 1)], 0, 0)),
                pl.BlockSpec(flat.shape, lambda q, t: (0, 0, 0), pipeline_mode=pl.Buffered(1)),
            ],
            out_specs=pl.BlockSpec((1, TILE, TILE), lambda q, t: (t[3, jnp.maximum(q - 1, 0)], 0, 0)),
            scratch_shapes=[
                pltpu.VMEM((slot_count, aux_funcs * TILE, 2 * TILE), jnp.bfloat16),
                pltpu.VMEM((2, 2 * TILE, aux_funcs * TILE), jnp.bfloat16),
            ],
        ),
        compiler_params=pltpu.CompilerParams(vmem_limit_bytes=VMEM_BYTES),
        name="run_tasks",
    )(table, incoming, flat)


def return_kernel(n_tile, n_aux, order_ref, src_ref, own_ref, mirror_ref, *scratch):
    parts = len(BACK)
    units = 2 * parts
    groups = [scratch[i * units:(i + 1) * units] for i in range(8)]
    arrived, rows, half_up, half_down, full_up, full_down, outgoing, summed = groups
    swapped = scratch[8 * units:8 * units + parts]
    (running, t_send, t_recv, y_send, y_recv, m_send, m_recv, z_send, z_recv, own_sem, out_sem) = scratch[8 * units + parts:]
    me = lax.axis_index("tile")
    aux = lax.axis_index("aux")
    up, down = lax.rem(aux + 1, n_aux), lax.rem(aux + n_aux - 1, n_aux)
    across = lax.rem(aux + 2, n_aux)
    per = n_tile // n_aux
    half = per // 2
    peers = n_tile // 2
    block = me // per
    slot = lax.rem(me, per)
    alike = block == aux
    barrier = pltpu.get_barrier_semaphore()

    @pl.loop(1, n_tile)
    def _(s):
        pl.semaphore_signal(barrier, inc=1, device_id={"tile": lax.rem(me + s, n_tile), "aux": aux}, device_id_type=MESH)

    for other in (up, down):
        pl.semaphore_signal(barrier, inc=1, device_id={"tile": me, "aux": other}, device_id_type=MESH)

    @pl.loop(0, per)
    def _(j):
        @pl.when(jnp.logical_not(alike & (j == slot)))
        def _():
            pl.semaphore_signal(barrier, inc=1, device_id={"tile": aux * per + j, "aux": block}, device_id_type=MESH)

    pl.semaphore_wait(barrier, n_tile + jnp.where(alike, per, per + 1))

    def span(u):
        return pl.ds(*BACK_SPANS[u // 2])

    def home_of(tile, u):
        return copy_of(tile) if u % 2 == 0 else tile

    def far(u, k):
        dest = holder(me, k, n_tile, u % 2 == 0)
        return pltpu.make_async_remote_copy(
            src_ref=src_ref.at[home_of(dest, u), :, span(u)], dst_ref=arrived[u].at[pl.ds(k * CAP, CAP)],
            send_sem=t_send.at[u, k], recv_sem=t_recv.at[u, k],
            device_id={"tile": dest, "aux": aux}, device_id_type=MESH)

    def own(u):
        return pltpu.make_async_copy(src_ref.at[home_of(me, u), :, span(u)], arrived[u].at[pl.ds(0, CAP)], own_sem.at[u])

    def begin(u):
        @pl.loop(1, peers)
        def _(s):
            far(u, lax.rem(s * ORDER, peers)).start()

        own(u).start()

    def near(src, dst, u, index, other):
        return pltpu.make_async_remote_copy(
            src_ref=src, dst_ref=dst, send_sem=y_send.at[u, index], recv_sem=y_recv.at[u, index],
            device_id={"tile": me, "aux": other}, device_id_type=MESH)

    def steps(u):
        return (
            near(rows[u].at[pl.ds(across * per, half)], half_up[u], u, 0, up),
            near(rows[u].at[pl.ds(across * per + half, half)], half_down[u], u, 1, down),
            near(outgoing[u].at[0], full_up[u], u, 2, up),
            near(outgoing[u].at[1], full_down[u], u, 3, down),
        )

    def swap(p):
        return pltpu.make_async_remote_copy(
            src_ref=summed[2 * p], dst_ref=swapped[p], send_sem=z_send.at[p], recv_sem=z_recv.at[p],
            device_id={"tile": copy_of(me), "aux": aux}, device_id_type=MESH)

    def send(u, j):
        return pltpu.make_async_remote_copy(
            src_ref=summed[u].at[j], dst_ref=mirror_ref.at[slot, span(u)],
            send_sem=m_send.at[u, j], recv_sem=m_recv.at[u, slot],
            device_id={"tile": aux * per + j, "aux": block}, device_id_type=MESH)

    def keep(u, j):
        return pltpu.make_async_copy(summed[u].at[j], mirror_ref.at[j, span(u)], m_send.at[u, j])

    def settle(u):
        return pltpu.make_async_copy(summed[u], own_ref.at[:, span(u)], out_sem.at[u // 2])

    def collect(u):
        length = BACK[u // 2]
        table = (u % 2) * 4

        @pl.loop(1, peers)
        def _(k):
            pltpu.make_async_remote_copy(
                src_ref=src_ref.at[me, :, span(u)], dst_ref=arrived[u].at[pl.ds(k * CAP, CAP)],
                send_sem=t_send.at[u, k], recv_sem=t_recv.at[u, k],
                device_id={"tile": served(me, k, n_tile, u % 2 == 0), "aux": aux}, device_id_type=MESH).wait_recv()

        own(u).wait()
        if u + AHEAD < units:
            begin(u + AHEAD)

        def add(i, carry):
            for v in range(4):
                k = i * 4 + v
                carry = jnp.where(order_ref[table + 1, k] > 0, 0.0, carry) + arrived[u][order_ref[table, k]]
                running[k, 0:length] = carry
            return carry

        lax.fori_loop(0, peers * CAP // 4, add, jnp.zeros((length, TILE), jnp.float32))

        @pl.loop(0, n_tile)
        def _(b):
            rows[u][b] = jnp.where(order_ref[table + 3, b] > 0, running[order_ref[table + 2, b], 0:length], 0.0)

        first_up, first_down, _, _ = steps(u)
        first_up.start()
        first_down.start()

        @pl.loop(0, half)
        def _(j):
            outgoing[u][0, half + j] = rows[u][up * per + half + j]
            outgoing[u][1, j] = rows[u][down * per + j]

    def pass_on(u):
        first_up, first_down, second_up, second_down = steps(u)
        first_up.wait_recv()

        @pl.loop(0, half)
        def _(j):
            outgoing[u][0, j] = rows[u][up * per + j] + half_up[u][j]

        second_up.start()
        first_down.wait_recv()

        @pl.loop(0, half)
        def _(j):
            outgoing[u][1, half + j] = rows[u][down * per + half + j] + half_down[u][j]

        second_down.start()

    def conclude(u):
        _, _, second_up, second_down = steps(u)
        second_up.wait_recv()
        second_down.wait_recv()
        if u % 2 == 0:
            @pl.loop(0, per)
            def _(j):
                summed[u][j] = rows[u][aux * per + j] + (full_up[u][j] + full_down[u][j])

            swap(u // 2).start()
        else:
            swap(u // 2).wait_recv()

            @pl.loop(0, per)
            def _(j):
                summed[u][j] = (rows[u][aux * per + j] + swapped[u // 2][j]) + (full_up[u][j] + full_down[u][j])
                mine = alike & (j == slot)

                @pl.when(jnp.logical_not(mine))
                def _():
                    send(u, j).start()

                @pl.when(mine)
                def _():
                    keep(u, j).start()

            settle(u).start()

    for u in range(AHEAD):
        begin(u)
    for u in range(units):
        collect(u)
        if u > 0:
            conclude(u - 1)
        pass_on(u)
    conclude(units - 1)

    for u in range(units):
        @pl.loop(1, peers)
        def _(k):
            far(u, k).wait_send()

        for copy in steps(u):
            copy.wait_send()
        if u % 2 == 0:
            swap(u // 2).wait_send()
        else:
            @pl.loop(0, per)
            def _(j):
                mine = alike & (j == slot)

                @pl.when(jnp.logical_not(mine))
                def _():
                    pltpu.make_async_remote_copy(
                        src_ref=summed[u].at[j], dst_ref=mirror_ref.at[j, span(u)],
                        send_sem=m_send.at[u, j], recv_sem=m_recv.at[u, j],
                        device_id={"tile": aux * per + j, "aux": block}, device_id_type=MESH).wait_recv()
                    send(u, j).wait_send()

                @pl.when(mine)
                def _():
                    keep(u, j).wait()

            settle(u).wait()


def return_partials(order, outbound, n_tile, n_aux):
    per = n_tile // n_aux
    peers = n_tile // 2
    parts = len(BACK)
    units = 2 * parts
    lengths = [n for n in BACK for _ in range(2)]
    shape = jax.ShapeDtypeStruct((per, TILE, TILE), jnp.float32)
    leads = [(peers * CAP,), (n_tile,), (per // 2,), (per // 2,), (per,), (per,), (2, per), (per,)]
    return pl.pallas_call(
        functools.partial(return_kernel, n_tile, n_aux),
        out_shape=(shape, shape),
        in_specs=[pl.BlockSpec(memory_space=pltpu.SMEM), pl.BlockSpec(memory_space=pl.ANY)],
        out_specs=(pl.BlockSpec(memory_space=pl.ANY), pl.BlockSpec(memory_space=pl.ANY)),
        scratch_shapes=[pltpu.VMEM(lead + (n, TILE), jnp.float32) for lead in leads for n in lengths]
        + [pltpu.VMEM((per, n, TILE), jnp.float32) for n in BACK]
        + [
            pltpu.VMEM((peers * CAP, max(BACK), TILE), jnp.float32),
            pltpu.SemaphoreType.DMA((units, peers)),
            pltpu.SemaphoreType.DMA((units, peers)),
            pltpu.SemaphoreType.DMA((units, 4)),
            pltpu.SemaphoreType.DMA((units, 4)),
            pltpu.SemaphoreType.DMA((units, per)),
            pltpu.SemaphoreType.DMA((units, per)),
            pltpu.SemaphoreType.DMA((parts,)),
            pltpu.SemaphoreType.DMA((parts,)),
            pltpu.SemaphoreType.DMA((units,)),
            pltpu.SemaphoreType.DMA((parts,)),
        ],
        compiler_params=pltpu.CompilerParams(collective_id=1, has_side_effects=True, vmem_limit_bytes=VMEM_BYTES),
        name="return_partials",
    )(order, outbound)


def stacked(x, axis):
    return jnp.concatenate(halves(x), axis=axis)


def folded(x):
    tall = x[:, :TILE] + x[:, TILE:]
    return tall[:TILE] + tall[TILE:]


def finish_kernel(group, place, own_ref, mirror_ref, left_ref, right_ref, out_ref):
    left = stacked(jnp.transpose(left_ref[...]), 0)
    for i in range(group):
        symmetric = own_ref[i] + jnp.transpose(mirror_ref[i])
        leftward = folded(jnp.dot(left, stacked(symmetric, 1), preferred_element_type=jnp.float32))
        right = stacked(right_ref[i * TILE:(i + 1) * TILE, :], 1)
        out_ref[:, i * TILE:(i + 1) * TILE] = folded(
            jnp.dot(stacked(leftward, 0), right, preferred_element_type=jnp.float32))


def finish(place, own, mirror, orthogonalizers):
    per = own.shape[0]
    group = 4
    steps = per // group
    tile = pl.BlockSpec((group, TILE, TILE), lambda j, t: (j, 0, 0))
    return pl.pallas_call(
        functools.partial(finish_kernel, group),
        out_shape=jax.ShapeDtypeStruct((TILE, per * TILE), jnp.float32),
        grid_spec=pltpu.PrefetchScalarGridSpec(
            num_scalar_prefetch=1,
            grid=(steps,),
            in_specs=[
                tile, tile,
                pl.BlockSpec((TILE, TILE), lambda j, t: (t[0], 0)),
                pl.BlockSpec((group * TILE, TILE), lambda j, t: (t[1] * steps + j, 0)),
            ],
            out_specs=pl.BlockSpec((TILE, group * TILE), lambda j, t: (0, j)),
        ),
        name="finish",
    )(place, own, mirror, orthogonalizers, orthogonalizers)


def column_order(cols, n_tile):
    count = cols.shape[0]
    spot = jnp.arange(count, dtype=jnp.int32)
    key = jnp.where(cols < 0, n_tile, cols)
    before = (key[None, :] < key[:, None]) | ((key[None, :] == key[:, None]) & (spot[None, :] < spot[:, None]))
    place = jnp.sum(before, axis=1)
    at = place[None, :] == spot[:, None]
    order = jnp.sum(jnp.where(at, spot[None, :], 0), axis=1)
    starts = jnp.any(at & (~jnp.any(before & (key[None, :] == key[:, None]), axis=1))[None, :], axis=1)
    ends = jnp.sum(key[None, :] <= spot[:, None], axis=1) - 1
    held = jnp.any(key[None, :] == spot[:, None], axis=1) & (spot < n_tile)
    return jnp.stack([order, starts.astype(jnp.int32), jnp.maximum(ends, 0), held.astype(jnp.int32)]).astype(jnp.int32)


def local(density, factors, orthogonalizers, slot_pairs, density_source, density_column, target_row, target_column):
    n_tile, n_aux = lax.axis_size("tile"), lax.axis_size("aux")
    me, aux = lax.axis_index("tile"), lax.axis_index("aux")
    tasks = slot_pairs.shape[0]

    packed = density_source
    for other in (density_column, target_row, target_column):
        packed = packed * n_tile + other
    packed = lax.dynamic_index_in_dim(packed.reshape(n_tile, n_aux, tasks), aux, 1, False)
    target_cols = packed % n_tile
    targets = (packed // n_tile) % n_tile
    columns = (packed // n_tile ** 2) % n_tile
    sources = packed // n_tile ** 3
    own_source = lax.dynamic_index_in_dim(sources, me, 0, False)
    own_target = lax.dynamic_index_in_dim(targets, me, 0, False)
    send_cols = jnp.concatenate([slot_columns(sources, columns, me), slot_columns(sources, columns, copy_of(me))])
    places = jnp.arange(n_tile, dtype=jnp.int32)

    def order_for(row, copy):
        slot_cols = slot_columns(targets, target_cols, row)
        pick = served(me, places[:n_tile // 2], n_tile, copy)[:, None] == places[None, :]
        cols = jnp.sum(jnp.where(pick[:, :, None], slot_cols[None] + 1, 0), axis=1) - 1
        return column_order(cols.reshape(-1), n_tile)

    table = jnp.stack([
        own_source * CAP + ranks_of(own_source),
        slot_pairs[:, 0],
        slot_pairs[:, 1],
        own_target * CAP + ranks_of(own_target),
    ])
    slots = n_tile * CAP
    incoming = fetch_density(density, jnp.maximum(send_cols, 0), n_tile, n_aux)
    outbound = run_tasks(table, incoming.reshape(slots, TILE, TILE), factors, slots)
    own, mirror = return_partials(
        jnp.concatenate([order_for(copy_of(me), True), order_for(me, False)]), outbound.reshape(n_tile, CAP, TILE, TILE), n_tile, n_aux)
    return finish(jnp.stack([me, aux]).astype(jnp.int32), own, mirror, orthogonalizers)


def solution(mesh):
    return jax.shard_map(
        local,
        mesh=mesh,
        in_specs=(
            P("tile", "aux"),
            P(("tile", "aux"), None, None, None),
            P(),
            P(("tile", "aux"), None),
            P(),
            P(),
            P(),
            P(),
        ),
        out_specs=P("tile", "aux"),
        check_vma=False,
    )
```

```python
import functools
import jax
import jax.numpy as jnp
from jax import lax
from jax.experimental import pallas as pl
from jax.experimental.pallas import tpu as pltpu
from jax.sharding import PartitionSpec as P

MESH = pl.DeviceIdType.MESH
TILE = 128
CAP = 2
VMEM_BYTES = 56 * 1024 * 1024
RING = 8
CORES = 2
ORDER = 13
ROWS = (32, 48, 48)
SPANS = [(sum(ROWS[:r]), n) for r, n in enumerate(ROWS)]
BACK = (48, 40, 24, 16)
AHEAD = 2
BACK_SPANS = [(sum(BACK[:r]), n) for r, n in enumerate(BACK)]


def halves(x):
    top = x.astype(jnp.bfloat16)
    rest = (x - top.astype(jnp.float32)).astype(jnp.bfloat16)
    return top, rest


def ranks_of(keys):
    count = keys.shape[-1]
    spot = jnp.arange(count)
    earlier = spot[None, :] < spot[:, None]
    return jnp.sum((keys[..., :, None] == keys[..., None, :]) & earlier, axis=-1).astype(jnp.int32)


def slot_columns(keys, columns, wanted):
    ranking = ranks_of(keys)
    picked = []
    for level in range(CAP):
        chosen = (keys == wanted) & (ranking == level)
        picked.append(jnp.sum(jnp.where(chosen, columns + 1, 0), axis=-1) - 1)
    return jnp.stack(picked, axis=-1)


def spot_of(tile):
    return tile // (RING * CORES), lax.rem(tile // CORES, RING), lax.rem(tile, CORES)


def tile_of(x, z, core):
    return (x * RING + z) * CORES + core


def copy_at(tile):
    x, z, core = spot_of(tile)
    return tile_of(x, lax.rem(z + 3 + (RING - 6) * core, RING), core)


def copy_of(tile):
    x, z, core = spot_of(tile)
    return tile_of(x, lax.rem(z + RING - 3 - (RING - 6) * core, RING), core)


def reach(turn, core, copy):
    far = jnp.where(core == 0, RING - 2, 2)
    if copy:
        far = RING - far
    return jnp.where(turn == 3, far, jnp.where(turn == 2, RING - 1, turn))


def served(tile, k, n_tile, copy):
    x, z, core = spot_of(tile)
    across = n_tile // (RING * CORES)
    to_core = lax.rem(core + lax.rem(k, CORES), CORES)
    turn = lax.rem(k // CORES, 4)
    return tile_of(lax.rem(x + k // (4 * CORES), across), lax.rem(z + reach(turn, core, copy), RING), to_core)


def holder(tile, k, n_tile, copy):
    x, z, core = spot_of(tile)
    across = n_tile // (RING * CORES)
    from_core = lax.rem(core + CORES - lax.rem(k, CORES), CORES)
    turn = lax.rem(k // CORES, 4)
    z_from = lax.rem(z + RING - reach(turn, from_core, copy), RING)
    return tile_of(lax.rem(x + across - k // (4 * CORES), across), z_from, from_core)


def density_kernel(n_tile, n_aux, cols_ref, dens_ref, out_ref, *scratch):
    parts = len(ROWS)
    slabs, outgoing = scratch[:2 * parts], scratch[2 * parts:4 * parts]
    y_send, y_recv, z_send, z_recv, t_send, t_recv, own_sem = scratch[4 * parts:]
    me = lax.axis_index("tile")
    aux = lax.axis_index("aux")
    homes = [me] * parts + [copy_of(me)] * parts
    spans = SPANS * 2
    up, down = lax.rem(aux + 1, n_aux), lax.rem(aux + n_aux - 1, n_aux)
    across = lax.rem(aux + 2, n_aux)
    per = dens_ref.shape[1] // TILE
    half = per // 2
    peers = n_tile // 2
    barrier = pltpu.get_barrier_semaphore()

    @pl.loop(1, n_tile)
    def _(s):
        pl.semaphore_signal(barrier, inc=1, device_id={"tile": lax.rem(me + s, n_tile), "aux": aux}, device_id_type=MESH)

    for other in (up, down):
        pl.semaphore_signal(barrier, inc=1, device_id={"tile": me, "aux": other}, device_id_type=MESH)
    for r, (start, length) in enumerate(SPANS):
        for j in range(per):
            slabs[r][aux * per + j] = dens_ref[start:start + length, j * TILE:(j + 1) * TILE]
    pl.semaphore_wait(barrier, n_tile + 1)

    def near(r, owner, start, length, index, other):
        where = slabs[r].at[pl.ds(owner * per + start, length)]
        return pltpu.make_async_remote_copy(
            src_ref=where, dst_ref=where, send_sem=y_send.at[r, index], recv_sem=y_recv.at[r, index],
            device_id={"tile": me, "aux": other}, device_id_type=MESH)

    def swap(r):
        mine = pl.ds(aux * per, per)
        return pltpu.make_async_remote_copy(
            src_ref=slabs[r].at[mine], dst_ref=slabs[parts + r].at[mine], send_sem=z_send.at[r], recv_sem=z_recv.at[r],
            device_id={"tile": copy_at(me), "aux": aux}, device_id_type=MESH)

    def home_rows(tile, r):
        return out_ref.at[tile, :, pl.ds(*spans[r])]

    def ship(r, k):
        return pltpu.make_async_remote_copy(
            src_ref=outgoing[r].at[k], dst_ref=home_rows(homes[r], r),
            send_sem=t_send.at[r, k], recv_sem=t_recv.at[r, k],
            device_id={"tile": served(me, k, n_tile, r >= parts), "aux": aux}, device_id_type=MESH)

    def own(r):
        return pltpu.make_async_copy(outgoing[r].at[0], home_rows(homes[r], r), own_sem.at[r])

    def first(r):
        near(r, aux, 0, per, 0, up).start()
        near(r, aux, 0, per, 1, down).start()

    def second(r):
        near(r, down, 0, per, 0, up).wait_recv()
        near(r, down, 0, half, 2, up).start()
        near(r, up, 0, per, 1, down).wait_recv()
        near(r, up, half, half, 3, down).start()

    def gathered(r):
        near(r, across, 0, half, 2, up).wait_recv()
        near(r, across, half, half, 3, down).wait_recv()

    def send_all(r):
        base = 0 if r < parts else n_tile

        @pl.loop(0, peers)
        def _(s):
            k = lax.rem(s * ORDER, peers)
            dest = base + served(me, k, n_tile, r >= parts)
            for level in range(CAP):
                outgoing[r][k, level] = slabs[r][cols_ref[dest, level]]

            @pl.when(s > 0)
            def _():
                ship(r, k).start()

        own(r).start()

    def step_copy(r):
        swap(r).wait_recv()
        first(parts + r)

    for r in range(parts):
        first(r)
        swap(r).start()
    second(0)
    for r in range(2 * parts):
        gathered(r)
        if r + 1 < 2 * parts:
            second(r + 1)
        send_all(r)
        if r < parts:
            step_copy(r)

    for r in range(2 * parts):
        @pl.loop(1, peers)
        def _(k):
            source = holder(me, k, n_tile, r >= parts)
            home = source if r < parts else copy_of(source)
            pltpu.make_async_remote_copy(
                src_ref=outgoing[r].at[k], dst_ref=home_rows(home, r),
                send_sem=t_send.at[r, k], recv_sem=t_recv.at[r, k],
                device_id={"tile": source, "aux": aux}, device_id_type=MESH).wait_recv()
            ship(r, k).wait_send()

        own(r).wait()
        near(r, aux, 0, per, 0, up).wait_send()
        near(r, aux, 0, per, 1, down).wait_send()
        near(r, down, 0, half, 2, up).wait_send()
        near(r, up, half, half, 3, down).wait_send()
        if r < parts:
            swap(r).wait_send()


def fetch_density(density, cols, n_tile, n_aux):
    units = 2 * len(ROWS)
    return pl.pallas_call(
        functools.partial(density_kernel, n_tile, n_aux),
        out_shape=jax.ShapeDtypeStruct((n_tile, CAP, TILE, TILE), jnp.float32),
        in_specs=[pl.BlockSpec(memory_space=pltpu.SMEM), pl.BlockSpec(memory_space=pltpu.VMEM)],
        out_specs=pl.BlockSpec(memory_space=pl.ANY),
        scratch_shapes=[pltpu.VMEM((n_tile, n, TILE), jnp.float32) for n in ROWS * 2]
        + [pltpu.VMEM((n_tile // 2, CAP, n, TILE), jnp.float32) for n in ROWS * 2]
        + [
            pltpu.SemaphoreType.DMA((units, 4)),
            pltpu.SemaphoreType.DMA((units, 4)),
            pltpu.SemaphoreType.DMA((len(ROWS),)),
            pltpu.SemaphoreType.DMA((len(ROWS),)),
            pltpu.SemaphoreType.DMA((units, n_tile // 2)),
            pltpu.SemaphoreType.DMA((units, n_tile // 2)),
            pltpu.SemaphoreType.DMA((units,)),
        ],
        compiler_params=pltpu.CompilerParams(collective_id=0, has_side_effects=True, vmem_limit_bytes=VMEM_BYTES),
        name="fetch_density",
    )(cols, density)


def task_kernel(pair_count, table, dens_ref, fact_ref, out_ref, split, lhs):
    q = pl.program_id(0)
    last = pl.num_programs(0) - 2
    now = lax.rem(q, 2)

    @pl.when(q == 0)
    def _():
        lhs[1] = jnp.zeros(lhs.shape[1:], lhs.dtype)

        @pl.loop(0, fact_ref.shape[0])
        def _(slot):
            for p in range(pair_count):
                rows = slice(p * 2 * TILE, (p + 1) * 2 * TILE)
                top, rest = halves(fact_ref[slot, rows, :])
                split[slot, rows, 0:TILE] = top
                split[slot, rows, TILE:2 * TILE] = rest

    left, right = table[1, jnp.minimum(q, last)], table[2, jnp.maximum(q - 1, 0)]
    top, rest = halves(dens_ref[0])
    row = jnp.concatenate([top, rest], axis=1)
    weights = jnp.concatenate([row, row], axis=0)
    total = jnp.dot(lhs[1 - now], split[right], preferred_element_type=jnp.float32)
    for p in range(pair_count):
        rows = slice(p * 2 * TILE, (p + 1) * 2 * TILE)
        wide = jnp.dot(split[left, rows, :], weights, preferred_element_type=jnp.float32)
        top, rest = halves(wide[:, :TILE] + wide[:, TILE:])
        lhs[now, :, rows] = jnp.concatenate(
            [jnp.concatenate([top[:TILE], top[TILE:]], axis=1), jnp.concatenate([rest[:TILE], rest[TILE:]], axis=1)], axis=0)
    tall = total[:, :TILE] + total[:, TILE:]
    out_ref[0] = tall[:TILE] + tall[TILE:]


def run_tasks(table, incoming, factors, slots):
    slot_count, aux_funcs = factors.shape[:2]
    flat = factors.reshape(slot_count, aux_funcs * TILE, TILE)
    task_count = table.shape[1]
    return pl.pallas_call(
        functools.partial(task_kernel, aux_funcs // 2),
        out_shape=jax.ShapeDtypeStruct((slots, TILE, TILE), jnp.float32),
        grid_spec=pltpu.PrefetchScalarGridSpec(
            num_scalar_prefetch=1,
            grid=(task_count + 1,),
            in_specs=[
                pl.BlockSpec((1, TILE, TILE), lambda q, t: (t[0, jnp.minimum(q, task_count - 1)], 0, 0)),
                pl.BlockSpec(flat.shape, lambda q, t: (0, 0, 0), pipeline_mode=pl.Buffered(1)),
            ],
            out_specs=pl.BlockSpec((1, TILE, TILE), lambda q, t: (t[3, jnp.maximum(q - 1, 0)], 0, 0)),
            scratch_shapes=[
                pltpu.VMEM((slot_count, aux_funcs * TILE, 2 * TILE), jnp.bfloat16),
                pltpu.VMEM((2, 2 * TILE, aux_funcs * TILE), jnp.bfloat16),
            ],
        ),
        compiler_params=pltpu.CompilerParams(vmem_limit_bytes=VMEM_BYTES),
        name="run_tasks",
    )(table, incoming, flat)


def return_kernel(n_tile, n_aux, order_ref, src_ref, own_ref, mirror_ref, *scratch):
    parts = len(BACK)
    units = 2 * parts
    groups = [scratch[i * units:(i + 1) * units] for i in range(8)]
    arrived, rows, half_up, half_down, full_up, full_down, outgoing, summed = groups
    swapped = scratch[8 * units:8 * units + parts]
    (running, t_send, t_recv, y_send, y_recv, m_send, m_recv, z_send, z_recv, own_sem, out_sem) = scratch[8 * units + parts:]
    me = lax.axis_index("tile")
    aux = lax.axis_index("aux")
    up, down = lax.rem(aux + 1, n_aux), lax.rem(aux + n_aux - 1, n_aux)
    across = lax.rem(aux + 2, n_aux)
    per = n_tile // n_aux
    half = per // 2
    peers = n_tile // 2
    block = me // per
    slot = lax.rem(me, per)
    alike = block == aux
    barrier = pltpu.get_barrier_semaphore()

    @pl.loop(1, n_tile)
    def _(s):
        pl.semaphore_signal(barrier, inc=1, device_id={"tile": lax.rem(me + s, n_tile), "aux": aux}, device_id_type=MESH)

    for other in (up, down):
        pl.semaphore_signal(barrier, inc=1, device_id={"tile": me, "aux": other}, device_id_type=MESH)

    @pl.loop(0, per)
    def _(j):
        @pl.when(jnp.logical_not(alike & (j == slot)))
        def _():
            pl.semaphore_signal(barrier, inc=1, device_id={"tile": aux * per + j, "aux": block}, device_id_type=MESH)

    pl.semaphore_wait(barrier, n_tile + jnp.where(alike, per, per + 1))

    def span(u):
        return pl.ds(*BACK_SPANS[u // 2])

    def home_of(tile, u):
        return copy_of(tile) if u % 2 == 0 else tile

    def far(u, k):
        dest = holder(me, k, n_tile, u % 2 == 0)
        return pltpu.make_async_remote_copy(
            src_ref=src_ref.at[home_of(dest, u), :, span(u)], dst_ref=arrived[u].at[pl.ds(k * CAP, CAP)],
            send_sem=t_send.at[u, k], recv_sem=t_recv.at[u, k],
            device_id={"tile": dest, "aux": aux}, device_id_type=MESH)

    def own(u):
        return pltpu.make_async_copy(src_ref.at[home_of(me, u), :, span(u)], arrived[u].at[pl.ds(0, CAP)], own_sem.at[u])

    def begin(u):
        @pl.loop(1, peers)
        def _(s):
            far(u, lax.rem(s * ORDER, peers)).start()

        own(u).start()

    def near(src, dst, u, index, other):
        return pltpu.make_async_remote_copy(
            src_ref=src, dst_ref=dst, send_sem=y_send.at[u, index], recv_sem=y_recv.at[u, index],
            device_id={"tile": me, "aux": other}, device_id_type=MESH)

    def steps(u):
        return (
            near(rows[u].at[pl.ds(across * per, half)], half_up[u], u, 0, up),
            near(rows[u].at[pl.ds(across * per + half, half)], half_down[u], u, 1, down),
            near(outgoing[u].at[0], full_up[u], u, 2, up),
            near(outgoing[u].at[1], full_down[u], u, 3, down),
        )

    def swap(p):
        return pltpu.make_async_remote_copy(
            src_ref=summed[2 * p], dst_ref=swapped[p], send_sem=z_send.at[p], recv_sem=z_recv.at[p],
            device_id={"tile": copy_of(me), "aux": aux}, device_id_type=MESH)

    def send(u, j):
        return pltpu.make_async_remote_copy(
            src_ref=summed[u].at[j], dst_ref=mirror_ref.at[slot, span(u)],
            send_sem=m_send.at[u, j], recv_sem=m_recv.at[u, slot],
            device_id={"tile": aux * per + j, "aux": block}, device_id_type=MESH)

    def keep(u, j):
        return pltpu.make_async_copy(summed[u].at[j], mirror_ref.at[j, span(u)], m_send.at[u, j])

    def settle(u):
        return pltpu.make_async_copy(summed[u], own_ref.at[:, span(u)], out_sem.at[u // 2])

    def collect(u):
        length = BACK[u // 2]
        table = (u % 2) * 4

        @pl.loop(1, peers)
        def _(k):
            pltpu.make_async_remote_copy(
                src_ref=src_ref.at[me, :, span(u)], dst_ref=arrived[u].at[pl.ds(k * CAP, CAP)],
                send_sem=t_send.at[u, k], recv_sem=t_recv.at[u, k],
                device_id={"tile": served(me, k, n_tile, u % 2 == 0), "aux": aux}, device_id_type=MESH).wait_recv()

        own(u).wait()
        if u + AHEAD < units:
            begin(u + AHEAD)

        def add(i, carry):
            for v in range(4):
                k = i * 4 + v
                carry = jnp.where(order_ref[table + 1, k] > 0, 0.0, carry) + arrived[u][order_ref[table, k]]
                running[k, 0:length] = carry
            return carry

        lax.fori_loop(0, peers * CAP // 4, add, jnp.zeros((length, TILE), jnp.float32))

        @pl.loop(0, n_tile)
        def _(b):
            rows[u][b] = jnp.where(order_ref[table + 3, b] > 0, running[order_ref[table + 2, b], 0:length], 0.0)

        first_up, first_down, _, _ = steps(u)
        first_up.start()
        first_down.start()

        @pl.loop(0, half)
        def _(j):
            outgoing[u][0, half + j] = rows[u][up * per + half + j]
            outgoing[u][1, j] = rows[u][down * per + j]

    def pass_on(u):
        first_up, first_down, second_up, second_down = steps(u)
        first_up.wait_recv()

        @pl.loop(0, half)
        def _(j):
            outgoing[u][0, j] = rows[u][up * per + j] + half_up[u][j]

        second_up.start()
        first_down.wait_recv()

        @pl.loop(0, half)
        def _(j):
            outgoing[u][1, half + j] = rows[u][down * per + half + j] + half_down[u][j]

        second_down.start()

    def conclude(u):
        _, _, second_up, second_down = steps(u)
        second_up.wait_recv()
        second_down.wait_recv()
        if u % 2 == 0:
            @pl.loop(0, per)
            def _(j):
                summed[u][j] = rows[u][aux * per + j] + (full_up[u][j] + full_down[u][j])

            swap(u // 2).start()
        else:
            swap(u // 2).wait_recv()

            @pl.loop(0, per)
            def _(turn):
                j = lax.rem(slot + turn, per)
                summed[u][j] = (rows[u][aux * per + j] + swapped[u // 2][j]) + (full_up[u][j] + full_down[u][j])
                mine = alike & (j == slot)

                @pl.when(jnp.logical_not(mine))
                def _():
                    send(u, j).start()

                @pl.when(mine)
                def _():
                    keep(u, j).start()

            settle(u).start()

    for u in range(AHEAD):
        begin(u)
    for u in range(units):
        collect(u)
        if u > 0:
            conclude(u - 1)
        pass_on(u)
    conclude(units - 1)

    for u in range(units):
        @pl.loop(1, peers)
        def _(k):
            far(u, k).wait_send()

        for copy in steps(u):
            copy.wait_send()
        if u % 2 == 0:
            swap(u // 2).wait_send()
        else:
            @pl.loop(0, per)
            def _(j):
                mine = alike & (j == slot)

                @pl.when(jnp.logical_not(mine))
                def _():
                    pltpu.make_async_remote_copy(
                        src_ref=summed[u].at[j], dst_ref=mirror_ref.at[j, span(u)],
                        send_sem=m_send.at[u, j], recv_sem=m_recv.at[u, j],
                        device_id={"tile": aux * per + j, "aux": block}, device_id_type=MESH).wait_recv()
                    send(u, j).wait_send()

                @pl.when(mine)
                def _():
                    keep(u, j).wait()

            settle(u).wait()


def return_partials(order, outbound, n_tile, n_aux):
    per = n_tile // n_aux
    peers = n_tile // 2
    parts = len(BACK)
    units = 2 * parts
    lengths = [n for n in BACK for _ in range(2)]
    shape = jax.ShapeDtypeStruct((per, TILE, TILE), jnp.float32)
    leads = [(peers * CAP,), (n_tile,), (per // 2,), (per // 2,), (per,), (per,), (2, per), (per,)]
    return pl.pallas_call(
        functools.partial(return_kernel, n_tile, n_aux),
        out_shape=(shape, shape),
        in_specs=[pl.BlockSpec(memory_space=pltpu.SMEM), pl.BlockSpec(memory_space=pl.ANY)],
        out_specs=(pl.BlockSpec(memory_space=pl.ANY), pl.BlockSpec(memory_space=pl.ANY)),
        scratch_shapes=[pltpu.VMEM(lead + (n, TILE), jnp.float32) for lead in leads for n in lengths]
        + [pltpu.VMEM((per, n, TILE), jnp.float32) for n in BACK]
        + [
            pltpu.VMEM((peers * CAP, max(BACK), TILE), jnp.float32),
            pltpu.SemaphoreType.DMA((units, peers)),
            pltpu.SemaphoreType.DMA((units, peers)),
            pltpu.SemaphoreType.DMA((units, 4)),
            pltpu.SemaphoreType.DMA((units, 4)),
            pltpu.SemaphoreType.DMA((units, per)),
            pltpu.SemaphoreType.DMA((units, per)),
            pltpu.SemaphoreType.DMA((parts,)),
            pltpu.SemaphoreType.DMA((parts,)),
            pltpu.SemaphoreType.DMA((units,)),
            pltpu.SemaphoreType.DMA((parts,)),
        ],
        compiler_params=pltpu.CompilerParams(collective_id=1, has_side_effects=True, vmem_limit_bytes=VMEM_BYTES),
        name="return_partials",
    )(order, outbound)


def stacked(x, axis):
    return jnp.concatenate(halves(x), axis=axis)


def folded(x):
    tall = x[:, :TILE] + x[:, TILE:]
    return tall[:TILE] + tall[TILE:]


def finish_kernel(group, place, own_ref, mirror_ref, left_ref, right_ref, out_ref):
    left = stacked(jnp.transpose(left_ref[...]), 0)
    for i in range(group):
        symmetric = own_ref[i] + jnp.transpose(mirror_ref[i])
        leftward = folded(jnp.dot(left, stacked(symmetric, 1), preferred_element_type=jnp.float32))
        right = stacked(right_ref[i * TILE:(i + 1) * TILE, :], 1)
        out_ref[:, i * TILE:(i + 1) * TILE] = folded(
            jnp.dot(stacked(leftward, 0), right, preferred_element_type=jnp.float32))


def finish(place, own, mirror, orthogonalizers):
    per = own.shape[0]
    group = 4
    steps = per // group
    tile = pl.BlockSpec((group, TILE, TILE), lambda j, t: (j, 0, 0))
    return pl.pallas_call(
        functools.partial(finish_kernel, group),
        out_shape=jax.ShapeDtypeStruct((TILE, per * TILE), jnp.float32),
        grid_spec=pltpu.PrefetchScalarGridSpec(
            num_scalar_prefetch=1,
            grid=(steps,),
            in_specs=[
                tile, tile,
                pl.BlockSpec((TILE, TILE), lambda j, t: (t[0], 0)),
                pl.BlockSpec((group * TILE, TILE), lambda j, t: (t[1] * steps + j, 0)),
            ],
            out_specs=pl.BlockSpec((TILE, group * TILE), lambda j, t: (0, j)),
        ),
        name="finish",
    )(place, own, mirror, orthogonalizers, orthogonalizers)


def column_order(cols, n_tile):
    count = cols.shape[0]
    spot = jnp.arange(count, dtype=jnp.int32)
    key = jnp.where(cols < 0, n_tile, cols)
    before = (key[None, :] < key[:, None]) | ((key[None, :] == key[:, None]) & (spot[None, :] < spot[:, None]))
    place = jnp.sum(before, axis=1)
    at = place[None, :] == spot[:, None]
    order = jnp.sum(jnp.where(at, spot[None, :], 0), axis=1)
    starts = jnp.any(at & (~jnp.any(before & (key[None, :] == key[:, None]), axis=1))[None, :], axis=1)
    ends = jnp.sum(key[None, :] <= spot[:, None], axis=1) - 1
    held = jnp.any(key[None, :] == spot[:, None], axis=1) & (spot < n_tile)
    return jnp.stack([order, starts.astype(jnp.int32), jnp.maximum(ends, 0), held.astype(jnp.int32)]).astype(jnp.int32)


def local(density, factors, orthogonalizers, slot_pairs, density_source, density_column, target_row, target_column):
    n_tile, n_aux = lax.axis_size("tile"), lax.axis_size("aux")
    me, aux = lax.axis_index("tile"), lax.axis_index("aux")
    tasks = slot_pairs.shape[0]

    packed = density_source
    for other in (density_column, target_row, target_column):
        packed = packed * n_tile + other
    packed = lax.dynamic_index_in_dim(packed.reshape(n_tile, n_aux, tasks), aux, 1, False)
    target_cols = packed % n_tile
    targets = (packed // n_tile) % n_tile
    columns = (packed // n_tile ** 2) % n_tile
    sources = packed // n_tile ** 3
    own_source = lax.dynamic_index_in_dim(sources, me, 0, False)
    own_target = lax.dynamic_index_in_dim(targets, me, 0, False)
    send_cols = jnp.concatenate([slot_columns(sources, columns, me), slot_columns(sources, columns, copy_of(me))])
    places = jnp.arange(n_tile, dtype=jnp.int32)

    def order_for(row, copy):
        slot_cols = slot_columns(targets, target_cols, row)
        pick = served(me, places[:n_tile // 2], n_tile, copy)[:, None] == places[None, :]
        cols = jnp.sum(jnp.where(pick[:, :, None], slot_cols[None] + 1, 0), axis=1) - 1
        return column_order(cols.reshape(-1), n_tile)

    table = jnp.stack([
        own_source * CAP + ranks_of(own_source),
        slot_pairs[:, 0],
        slot_pairs[:, 1],
        own_target * CAP + ranks_of(own_target),
    ])
    slots = n_tile * CAP
    incoming = fetch_density(density, jnp.maximum(send_cols, 0), n_tile, n_aux)
    outbound = run_tasks(table, incoming.reshape(slots, TILE, TILE), factors, slots)
    own, mirror = return_partials(
        jnp.concatenate([order_for(copy_of(me), True), order_for(me, False)]), outbound.reshape(n_tile, CAP, TILE, TILE), n_tile, n_aux)
    return finish(jnp.stack([me, aux]).astype(jnp.int32), own, mirror, orthogonalizers)


def solution(mesh):
    return jax.shard_map(
        local,
        mesh=mesh,
        in_specs=(
            P("tile", "aux"),
            P(("tile", "aux"), None, None, None),
            P(),
            P(("tile", "aux"), None),
            P(),
            P(),
            P(),
            P(),
        ),
        out_specs=P("tile", "aux"),
        check_vma=False,
    )
```

```python
import functools
import jax
import jax.numpy as jnp
from jax import lax
from jax.experimental import pallas as pl
from jax.experimental.pallas import tpu as pltpu
from jax.sharding import PartitionSpec as P

MESH = pl.DeviceIdType.MESH
TILE = 128
CAP = 2
VMEM_BYTES = 56 * 1024 * 1024
RING = 8
CORES = 2
ORDER = 13
KINDS = 3
ROWS = (56, 72)
SPANS = [(sum(ROWS[:r]), n) for r, n in enumerate(ROWS)]
BACK = (56, 40, 24, 8)
AHEAD = 2
BACK_SPANS = [(sum(BACK[:r]), n) for r, n in enumerate(BACK)]


def halves(x):
    top = x.astype(jnp.bfloat16)
    rest = (x - top.astype(jnp.float32)).astype(jnp.bfloat16)
    return top, rest


def ranks_of(keys):
    count = keys.shape[-1]
    spot = jnp.arange(count)
    earlier = spot[None, :] < spot[:, None]
    return jnp.sum((keys[..., :, None] == keys[..., None, :]) & earlier, axis=-1).astype(jnp.int32)


def slot_columns(keys, columns, wanted):
    ranking = ranks_of(keys)
    picked = []
    for level in range(CAP):
        chosen = (keys == wanted) & (ranking == level)
        picked.append(jnp.sum(jnp.where(chosen, columns + 1, 0), axis=-1) - 1)
    return jnp.stack(picked, axis=-1)


def spot_of(tile):
    return tile // (RING * CORES), lax.rem(tile // CORES, RING), lax.rem(tile, CORES)


def tile_of(x, z, core):
    return (x * RING + z) * CORES + core


def copy_at(tile):
    x, z, core = spot_of(tile)
    return tile_of(x, lax.rem(z + 3 + (RING - 6) * core, RING), core)


def copy_of(tile):
    x, z, core = spot_of(tile)
    return tile_of(x, lax.rem(z + RING - 3 - (RING - 6) * core, RING), core)


def reach(turn, core, copy):
    far = jnp.where(core == 0, RING - 2, 2)
    if copy:
        far = RING - far
    return jnp.where(turn == 3, far, jnp.where(turn == 2, RING - 1, turn))


def served(tile, k, n_tile, copy):
    x, z, core = spot_of(tile)
    across = n_tile // (RING * CORES)
    to_core = lax.rem(core + lax.rem(k, CORES), CORES)
    turn = lax.rem(k // CORES, 4)
    return tile_of(lax.rem(x + k // (4 * CORES), across), lax.rem(z + reach(turn, core, copy), RING), to_core)


def holder(tile, k, n_tile, copy):
    x, z, core = spot_of(tile)
    across = n_tile // (RING * CORES)
    from_core = lax.rem(core + CORES - lax.rem(k, CORES), CORES)
    turn = lax.rem(k // CORES, 4)
    z_from = lax.rem(z + RING - reach(turn, from_core, copy), RING)
    return tile_of(lax.rem(x + across - k // (4 * CORES), across), z_from, from_core)


def turned(z, steps, core):
    return lax.rem(z + steps * (1 - 2 * core) + RING, RING)


def held_at(tile, kind):
    x, z, core = spot_of(tile)
    return tile_of(x, turned(z, (0, 3, -2)[kind], core), core)


def held_by(tile, kind):
    x, z, core = spot_of(tile)
    return tile_of(x, turned(z, (0, -3, 2)[kind], core), core)


def fan(n_tile, kind):
    return n_tile // RING * (2 if kind == 0 else 3)


def fed(tile, k, n_tile, kind):
    x, z, core = spot_of(tile)
    across, turns = n_tile // (RING * CORES), 2 if kind == 0 else 3
    turn = lax.rem(k // CORES, turns)
    to_core = lax.rem(core + lax.rem(k, CORES), CORES)
    return tile_of(lax.rem(x + k // (turns * CORES), across), turned(z, turn - 3 * (turn // 2), core), to_core)


def feeder(tile, k, n_tile, kind):
    x, z, core = spot_of(tile)
    across, turns = n_tile // (RING * CORES), 2 if kind == 0 else 3
    turn = lax.rem(k // CORES, turns)
    from_core = lax.rem(core + CORES - lax.rem(k, CORES), CORES)
    z_from = turned(z, 3 * (turn // 2) - turn, from_core)
    return tile_of(lax.rem(x + across - k // (turns * CORES), across), z_from, from_core)


def density_kernel(n_tile, n_aux, cols_ref, dens_ref, out_ref, *scratch):
    parts = len(ROWS)
    units = KINDS * parts
    slabs, outgoing = scratch[:units], scratch[units:2 * units]
    y_send, y_recv, z_send, z_recv, t_send, t_recv, own_sem = scratch[2 * units:]
    me = lax.axis_index("tile")
    aux = lax.axis_index("aux")
    homes = [held_by(me, u // parts) for u in range(units)]
    spans = SPANS * KINDS
    up, down = lax.rem(aux + 1, n_aux), lax.rem(aux + n_aux - 1, n_aux)
    across = lax.rem(aux + 2, n_aux)
    per = dens_ref.shape[1] // TILE
    half = per // 2
    barrier = pltpu.get_barrier_semaphore()

    @pl.loop(1, n_tile)
    def _(s):
        pl.semaphore_signal(barrier, inc=1, device_id={"tile": lax.rem(me + s, n_tile), "aux": aux}, device_id_type=MESH)

    for other in (up, down):
        pl.semaphore_signal(barrier, inc=1, device_id={"tile": me, "aux": other}, device_id_type=MESH)
    for r, (start, length) in enumerate(SPANS):
        for j in range(per):
            slabs[r][aux * per + j] = dens_ref[start:start + length, j * TILE:(j + 1) * TILE]
    pl.semaphore_wait(barrier, n_tile + 1)

    def near(r, owner, start, length, index, other):
        where = slabs[r].at[pl.ds(owner * per + start, length)]
        return pltpu.make_async_remote_copy(
            src_ref=where, dst_ref=where, send_sem=y_send.at[r, index], recv_sem=y_recv.at[r, index],
            device_id={"tile": me, "aux": other}, device_id_type=MESH)

    def swap(u):
        mine = pl.ds(aux * per, per)
        return pltpu.make_async_remote_copy(
            src_ref=slabs[u % parts].at[mine], dst_ref=slabs[u].at[mine],
            send_sem=z_send.at[u], recv_sem=z_recv.at[u],
            device_id={"tile": held_at(me, u // parts), "aux": aux}, device_id_type=MESH)

    def home_rows(tile, r):
        return out_ref.at[tile, :, pl.ds(*spans[r])]

    def ship(r, k):
        return pltpu.make_async_remote_copy(
            src_ref=outgoing[r].at[k], dst_ref=home_rows(homes[r], r),
            send_sem=t_send.at[r, k], recv_sem=t_recv.at[r, k],
            device_id={"tile": fed(me, k, n_tile, r // parts), "aux": aux}, device_id_type=MESH)

    def own(r):
        return pltpu.make_async_copy(outgoing[r].at[0], home_rows(homes[r], r), own_sem.at[r])

    def first(r):
        near(r, aux, 0, per, 0, up).start()
        near(r, aux, 0, per, 1, down).start()

    def second(r):
        near(r, down, 0, per, 0, up).wait_recv()
        near(r, down, 0, half, 2, up).start()
        near(r, up, 0, per, 1, down).wait_recv()
        near(r, up, half, half, 3, down).start()

    def gathered(r):
        near(r, across, 0, half, 2, up).wait_recv()
        near(r, across, half, half, 3, down).wait_recv()

    def send_all(r):
        base = r // parts * n_tile
        peers = fan(n_tile, r // parts)

        @pl.loop(0, peers)
        def _(s):
            k = lax.rem(s * ORDER, peers)
            dest = base + fed(me, k, n_tile, r // parts)
            for level in range(CAP):
                outgoing[r][k, level] = slabs[r][cols_ref[dest, level]]

            @pl.when(s > 0)
            def _():
                ship(r, k).start()

        own(r).start()

    first(0)
    for u in range(parts, units):
        swap(u).start()
    for r in range(1, parts):
        first(r)
    second(0)
    for r in range(units):
        gathered(r)
        if r + 1 < units:
            second(r + 1)
        send_all(r)
        if parts <= r + 2 < units:
            swap(r + 2).wait_recv()
            first(r + 2)

    for r in range(units):
        @pl.loop(1, fan(n_tile, r // parts))
        def _(k):
            source = feeder(me, k, n_tile, r // parts)
            home = held_by(source, r // parts)
            pltpu.make_async_remote_copy(
                src_ref=outgoing[r].at[k], dst_ref=home_rows(home, r),
                send_sem=t_send.at[r, k], recv_sem=t_recv.at[r, k],
                device_id={"tile": source, "aux": aux}, device_id_type=MESH).wait_recv()
            ship(r, k).wait_send()

        own(r).wait()
        near(r, aux, 0, per, 0, up).wait_send()
        near(r, aux, 0, per, 1, down).wait_send()
        near(r, down, 0, half, 2, up).wait_send()
        near(r, up, half, half, 3, down).wait_send()
        if r >= parts:
            swap(r).wait_send()


def fetch_density(density, cols, n_tile, n_aux):
    parts = len(ROWS)
    units = KINDS * parts
    return pl.pallas_call(
        functools.partial(density_kernel, n_tile, n_aux),
        out_shape=jax.ShapeDtypeStruct((n_tile, CAP, TILE, TILE), jnp.float32),
        in_specs=[pl.BlockSpec(memory_space=pltpu.SMEM), pl.BlockSpec(memory_space=pltpu.VMEM)],
        out_specs=pl.BlockSpec(memory_space=pl.ANY),
        scratch_shapes=[pltpu.VMEM((n_tile, n, TILE), jnp.float32) for n in ROWS * KINDS]
        + [pltpu.VMEM((fan(n_tile, u // parts), CAP, ROWS[u % parts], TILE), jnp.float32) for u in range(units)]
        + [
            pltpu.SemaphoreType.DMA((units, 4)),
            pltpu.SemaphoreType.DMA((units, 4)),
            pltpu.SemaphoreType.DMA((units,)),
            pltpu.SemaphoreType.DMA((units,)),
            pltpu.SemaphoreType.DMA((units, fan(n_tile, 1))),
            pltpu.SemaphoreType.DMA((units, fan(n_tile, 1))),
            pltpu.SemaphoreType.DMA((units,)),
        ],
        compiler_params=pltpu.CompilerParams(collective_id=0, has_side_effects=True, vmem_limit_bytes=VMEM_BYTES),
        name="fetch_density",
    )(cols, density)


def task_kernel(pair_count, table, dens_ref, fact_ref, out_ref, split, lhs):
    q = pl.program_id(0)
    last = pl.num_programs(0) - 2
    now = lax.rem(q, 2)

    @pl.when(q == 0)
    def _():
        lhs[1] = jnp.zeros(lhs.shape[1:], lhs.dtype)

        @pl.loop(0, fact_ref.shape[0])
        def _(slot):
            for p in range(pair_count):
                rows = slice(p * 2 * TILE, (p + 1) * 2 * TILE)
                top, rest = halves(fact_ref[slot, rows, :])
                split[slot, rows, 0:TILE] = top
                split[slot, rows, TILE:2 * TILE] = rest

    left, right = table[1, jnp.minimum(q, last)], table[2, jnp.maximum(q - 1, 0)]
    top, rest = halves(dens_ref[0])
    row = jnp.concatenate([top, rest], axis=1)
    weights = jnp.concatenate([row, row], axis=0)
    total = jnp.dot(lhs[1 - now], split[right], preferred_element_type=jnp.float32)
    for p in range(pair_count):
        rows = slice(p * 2 * TILE, (p + 1) * 2 * TILE)
        wide = jnp.dot(split[left, rows, :], weights, preferred_element_type=jnp.float32)
        top, rest = halves(wide[:, :TILE] + wide[:, TILE:])
        lhs[now, :, rows] = jnp.concatenate(
            [jnp.concatenate([top[:TILE], top[TILE:]], axis=1), jnp.concatenate([rest[:TILE], rest[TILE:]], axis=1)], axis=0)
    tall = total[:, :TILE] + total[:, TILE:]
    out_ref[0] = tall[:TILE] + tall[TILE:]


def run_tasks(table, incoming, factors, slots):
    slot_count, aux_funcs = factors.shape[:2]
    flat = factors.reshape(slot_count, aux_funcs * TILE, TILE)
    task_count = table.shape[1]
    return pl.pallas_call(
        functools.partial(task_kernel, aux_funcs // 2),
        out_shape=jax.ShapeDtypeStruct((slots, TILE, TILE), jnp.float32),
        grid_spec=pltpu.PrefetchScalarGridSpec(
            num_scalar_prefetch=1,
            grid=(task_count + 1,),
            in_specs=[
                pl.BlockSpec((1, TILE, TILE), lambda q, t: (t[0, jnp.minimum(q, task_count - 1)], 0, 0)),
                pl.BlockSpec(flat.shape, lambda q, t: (0, 0, 0), pipeline_mode=pl.Buffered(1)),
            ],
            out_specs=pl.BlockSpec((1, TILE, TILE), lambda q, t: (t[3, jnp.maximum(q - 1, 0)], 0, 0)),
            scratch_shapes=[
                pltpu.VMEM((slot_count, aux_funcs * TILE, 2 * TILE), jnp.bfloat16),
                pltpu.VMEM((2, 2 * TILE, aux_funcs * TILE), jnp.bfloat16),
            ],
        ),
        compiler_params=pltpu.CompilerParams(vmem_limit_bytes=VMEM_BYTES),
        name="run_tasks",
    )(table, incoming, flat)


def return_kernel(n_tile, n_aux, order_ref, src_ref, own_ref, mirror_ref, *scratch):
    parts = len(BACK)
    units = 2 * parts
    groups = [scratch[i * units:(i + 1) * units] for i in range(8)]
    arrived, rows, half_up, half_down, full_up, full_down, outgoing, summed = groups
    swapped = scratch[8 * units:8 * units + parts]
    (running, t_send, t_recv, y_send, y_recv, m_send, m_recv, z_send, z_recv, own_sem, out_sem) = scratch[8 * units + parts:]
    me = lax.axis_index("tile")
    aux = lax.axis_index("aux")
    up, down = lax.rem(aux + 1, n_aux), lax.rem(aux + n_aux - 1, n_aux)
    across = lax.rem(aux + 2, n_aux)
    per = n_tile // n_aux
    half = per // 2
    peers = n_tile // 2
    block = me // per
    slot = lax.rem(me, per)
    alike = block == aux
    barrier = pltpu.get_barrier_semaphore()

    @pl.loop(1, n_tile)
    def _(s):
        pl.semaphore_signal(barrier, inc=1, device_id={"tile": lax.rem(me + s, n_tile), "aux": aux}, device_id_type=MESH)

    for other in (up, down):
        pl.semaphore_signal(barrier, inc=1, device_id={"tile": me, "aux": other}, device_id_type=MESH)

    @pl.loop(0, per)
    def _(j):
        @pl.when(jnp.logical_not(alike & (j == slot)))
        def _():
            pl.semaphore_signal(barrier, inc=1, device_id={"tile": aux * per + j, "aux": block}, device_id_type=MESH)

    pl.semaphore_wait(barrier, n_tile + jnp.where(alike, per, per + 1))

    def span(u):
        return pl.ds(*BACK_SPANS[u // 2])

    def home_of(tile, u):
        return copy_of(tile) if u % 2 == 0 else tile

    def far(u, k):
        dest = holder(me, k, n_tile, u % 2 == 0)
        return pltpu.make_async_remote_copy(
            src_ref=src_ref.at[home_of(dest, u), :, span(u)], dst_ref=arrived[u].at[pl.ds(k * CAP, CAP)],
            send_sem=t_send.at[u, k], recv_sem=t_recv.at[u, k],
            device_id={"tile": dest, "aux": aux}, device_id_type=MESH)

    def own(u):
        return pltpu.make_async_copy(src_ref.at[home_of(me, u), :, span(u)], arrived[u].at[pl.ds(0, CAP)], own_sem.at[u])

    def begin(u):
        @pl.loop(1, peers)
        def _(s):
            far(u, lax.rem(s * ORDER, peers)).start()

        own(u).start()

    def near(src, dst, u, index, other):
        return pltpu.make_async_remote_copy(
            src_ref=src, dst_ref=dst, send_sem=y_send.at[u, index], recv_sem=y_recv.at[u, index],
            device_id={"tile": me, "aux": other}, device_id_type=MESH)

    def steps(u):
        return (
            near(rows[u].at[pl.ds(across * per, half)], half_up[u], u, 0, up),
            near(rows[u].at[pl.ds(across * per + half, half)], half_down[u], u, 1, down),
            near(outgoing[u].at[0], full_up[u], u, 2, up),
            near(outgoing[u].at[1], full_down[u], u, 3, down),
        )

    def swap(p):
        return pltpu.make_async_remote_copy(
            src_ref=summed[2 * p], dst_ref=swapped[p], send_sem=z_send.at[p], recv_sem=z_recv.at[p],
            device_id={"tile": copy_of(me), "aux": aux}, device_id_type=MESH)

    def send(u, j):
        return pltpu.make_async_remote_copy(
            src_ref=summed[u].at[j], dst_ref=mirror_ref.at[slot, span(u)],
            send_sem=m_send.at[u, j], recv_sem=m_recv.at[u, slot],
            device_id={"tile": aux * per + j, "aux": block}, device_id_type=MESH)

    def keep(u, j):
        return pltpu.make_async_copy(summed[u].at[j], mirror_ref.at[j, span(u)], m_send.at[u, j])

    def settle(u):
        return pltpu.make_async_copy(summed[u], own_ref.at[:, span(u)], out_sem.at[u // 2])

    def collect(u):
        length = BACK[u // 2]
        table = (u % 2) * 4

        @pl.loop(1, peers)
        def _(k):
            pltpu.make_async_remote_copy(
                src_ref=src_ref.at[me, :, span(u)], dst_ref=arrived[u].at[pl.ds(k * CAP, CAP)],
                send_sem=t_send.at[u, k], recv_sem=t_recv.at[u, k],
                device_id={"tile": served(me, k, n_tile, u % 2 == 0), "aux": aux}, device_id_type=MESH).wait_recv()

        own(u).wait()
        if u + AHEAD < units:
            begin(u + AHEAD)

        def add(i, carry):
            for v in range(4):
                k = i * 4 + v
                carry = jnp.where(order_ref[table + 1, k] > 0, 0.0, carry) + arrived[u][order_ref[table, k]]
                running[k, 0:length] = carry
            return carry

        lax.fori_loop(0, peers * CAP // 4, add, jnp.zeros((length, TILE), jnp.float32))

        @pl.loop(0, n_tile)
        def _(b):
            rows[u][b] = jnp.where(order_ref[table + 3, b] > 0, running[order_ref[table + 2, b], 0:length], 0.0)

        first_up, first_down, _, _ = steps(u)
        first_up.start()
        first_down.start()

        @pl.loop(0, half)
        def _(j):
            outgoing[u][0, half + j] = rows[u][up * per + half + j]
            outgoing[u][1, j] = rows[u][down * per + j]

    def pass_on(u):
        first_up, first_down, second_up, second_down = steps(u)
        first_up.wait_recv()

        @pl.loop(0, half)
        def _(j):
            outgoing[u][0, j] = rows[u][up * per + j] + half_up[u][j]

        second_up.start()
        first_down.wait_recv()

        @pl.loop(0, half)
        def _(j):
            outgoing[u][1, half + j] = rows[u][down * per + half + j] + half_down[u][j]

        second_down.start()

    def conclude(u):
        _, _, second_up, second_down = steps(u)
        second_up.wait_recv()
        second_down.wait_recv()
        if u % 2 == 0:
            @pl.loop(0, per)
            def _(j):
                summed[u][j] = rows[u][aux * per + j] + (full_up[u][j] + full_down[u][j])

            swap(u // 2).start()
        else:
            swap(u // 2).wait_recv()

            @pl.loop(0, per)
            def _(turn):
                j = lax.rem(slot + turn, per)
                summed[u][j] = (rows[u][aux * per + j] + swapped[u // 2][j]) + (full_up[u][j] + full_down[u][j])
                mine = alike & (j == slot)

                @pl.when(jnp.logical_not(mine))
                def _():
                    send(u, j).start()

                @pl.when(mine)
                def _():
                    keep(u, j).start()

            settle(u).start()

    for u in range(AHEAD):
        begin(u)
    for u in range(units):
        collect(u)
        if u > 0:
            conclude(u - 1)
        pass_on(u)
    conclude(units - 1)

    for u in range(units):
        @pl.loop(1, peers)
        def _(k):
            far(u, k).wait_send()

        for copy in steps(u):
            copy.wait_send()
        if u % 2 == 0:
            swap(u // 2).wait_send()
        else:
            @pl.loop(0, per)
            def _(j):
                mine = alike & (j == slot)

                @pl.when(jnp.logical_not(mine))
                def _():
                    pltpu.make_async_remote_copy(
                        src_ref=summed[u].at[j], dst_ref=mirror_ref.at[j, span(u)],
                        send_sem=m_send.at[u, j], recv_sem=m_recv.at[u, j],
                        device_id={"tile": aux * per + j, "aux": block}, device_id_type=MESH).wait_recv()
                    send(u, j).wait_send()

                @pl.when(mine)
                def _():
                    keep(u, j).wait()

            settle(u).wait()


def return_partials(order, outbound, n_tile, n_aux):
    per = n_tile // n_aux
    peers = n_tile // 2
    parts = len(BACK)
    units = 2 * parts
    lengths = [n for n in BACK for _ in range(2)]
    shape = jax.ShapeDtypeStruct((per, TILE, TILE), jnp.float32)
    leads = [(peers * CAP,), (n_tile,), (per // 2,), (per // 2,), (per,), (per,), (2, per), (per,)]
    return pl.pallas_call(
        functools.partial(return_kernel, n_tile, n_aux),
        out_shape=(shape, shape),
        in_specs=[pl.BlockSpec(memory_space=pltpu.SMEM), pl.BlockSpec(memory_space=pl.ANY)],
        out_specs=(pl.BlockSpec(memory_space=pl.ANY), pl.BlockSpec(memory_space=pl.ANY)),
        scratch_shapes=[pltpu.VMEM(lead + (n, TILE), jnp.float32) for lead in leads for n in lengths]
        + [pltpu.VMEM((per, n, TILE), jnp.float32) for n in BACK]
        + [
            pltpu.VMEM((peers * CAP, max(BACK), TILE), jnp.float32),
            pltpu.SemaphoreType.DMA((units, peers)),
            pltpu.SemaphoreType.DMA((units, peers)),
            pltpu.SemaphoreType.DMA((units, 4)),
            pltpu.SemaphoreType.DMA((units, 4)),
            pltpu.SemaphoreType.DMA((units, per)),
            pltpu.SemaphoreType.DMA((units, per)),
            pltpu.SemaphoreType.DMA((parts,)),
            pltpu.SemaphoreType.DMA((parts,)),
            pltpu.SemaphoreType.DMA((units,)),
            pltpu.SemaphoreType.DMA((parts,)),
        ],
        compiler_params=pltpu.CompilerParams(collective_id=1, has_side_effects=True, vmem_limit_bytes=VMEM_BYTES),
        name="return_partials",
    )(order, outbound)


def stacked(x, axis):
    return jnp.concatenate(halves(x), axis=axis)


def folded(x):
    tall = x[:, :TILE] + x[:, TILE:]
    return tall[:TILE] + tall[TILE:]


def finish_kernel(group, place, own_ref, mirror_ref, left_ref, right_ref, out_ref):
    left = stacked(jnp.transpose(left_ref[...]), 0)
    for i in range(group):
        symmetric = own_ref[i] + jnp.transpose(mirror_ref[i])
        leftward = folded(jnp.dot(left, stacked(symmetric, 1), preferred_element_type=jnp.float32))
        right = stacked(right_ref[i * TILE:(i + 1) * TILE, :], 1)
        out_ref[:, i * TILE:(i + 1) * TILE] = folded(
            jnp.dot(stacked(leftward, 0), right, preferred_element_type=jnp.float32))


def finish(place, own, mirror, orthogonalizers):
    per = own.shape[0]
    group = 4
    steps = per // group
    tile = pl.BlockSpec((group, TILE, TILE), lambda j, t: (j, 0, 0))
    return pl.pallas_call(
        functools.partial(finish_kernel, group),
        out_shape=jax.ShapeDtypeStruct((TILE, per * TILE), jnp.float32),
        grid_spec=pltpu.PrefetchScalarGridSpec(
            num_scalar_prefetch=1,
            grid=(steps,),
            in_specs=[
                tile, tile,
                pl.BlockSpec((TILE, TILE), lambda j, t: (t[0], 0)),
                pl.BlockSpec((group * TILE, TILE), lambda j, t: (t[1] * steps + j, 0)),
            ],
            out_specs=pl.BlockSpec((TILE, group * TILE), lambda j, t: (0, j)),
        ),
        name="finish",
    )(place, own, mirror, orthogonalizers, orthogonalizers)


def column_order(cols, n_tile):
    count = cols.shape[0]
    spot = jnp.arange(count, dtype=jnp.int32)
    key = jnp.where(cols < 0, n_tile, cols)
    before = (key[None, :] < key[:, None]) | ((key[None, :] == key[:, None]) & (spot[None, :] < spot[:, None]))
    place = jnp.sum(before, axis=1)
    at = place[None, :] == spot[:, None]
    order = jnp.sum(jnp.where(at, spot[None, :], 0), axis=1)
    starts = jnp.any(at & (~jnp.any(before & (key[None, :] == key[:, None]), axis=1))[None, :], axis=1)
    ends = jnp.sum(key[None, :] <= spot[:, None], axis=1) - 1
    held = jnp.any(key[None, :] == spot[:, None], axis=1) & (spot < n_tile)
    return jnp.stack([order, starts.astype(jnp.int32), jnp.maximum(ends, 0), held.astype(jnp.int32)]).astype(jnp.int32)


def local(density, factors, orthogonalizers, slot_pairs, density_source, density_column, target_row, target_column):
    n_tile, n_aux = lax.axis_size("tile"), lax.axis_size("aux")
    me, aux = lax.axis_index("tile"), lax.axis_index("aux")
    tasks = slot_pairs.shape[0]

    packed = density_source
    for other in (density_column, target_row, target_column):
        packed = packed * n_tile + other
    packed = lax.dynamic_index_in_dim(packed.reshape(n_tile, n_aux, tasks), aux, 1, False)
    target_cols = packed % n_tile
    targets = (packed // n_tile) % n_tile
    columns = (packed // n_tile ** 2) % n_tile
    sources = packed // n_tile ** 3
    own_source = lax.dynamic_index_in_dim(sources, me, 0, False)
    own_target = lax.dynamic_index_in_dim(targets, me, 0, False)
    send_cols = jnp.concatenate([slot_columns(sources, columns, held_by(me, kind)) for kind in range(KINDS)])
    places = jnp.arange(n_tile, dtype=jnp.int32)

    def order_for(row, copy):
        slot_cols = slot_columns(targets, target_cols, row)
        pick = served(me, places[:n_tile // 2], n_tile, copy)[:, None] == places[None, :]
        cols = jnp.sum(jnp.where(pick[:, :, None], slot_cols[None] + 1, 0), axis=1) - 1
        return column_order(cols.reshape(-1), n_tile)

    table = jnp.stack([
        own_source * CAP + ranks_of(own_source),
        slot_pairs[:, 0],
        slot_pairs[:, 1],
        own_target * CAP + ranks_of(own_target),
    ])
    slots = n_tile * CAP
    incoming = fetch_density(density, jnp.maximum(send_cols, 0), n_tile, n_aux)
    outbound = run_tasks(table, incoming.reshape(slots, TILE, TILE), factors, slots)
    own, mirror = return_partials(
        jnp.concatenate([order_for(copy_of(me), True), order_for(me, False)]), outbound.reshape(n_tile, CAP, TILE, TILE), n_tile, n_aux)
    return finish(jnp.stack([me, aux]).astype(jnp.int32), own, mirror, orthogonalizers)


def solution(mesh):
    return jax.shard_map(
        local,
        mesh=mesh,
        in_specs=(
            P("tile", "aux"),
            P(("tile", "aux"), None, None, None),
            P(),
            P(("tile", "aux"), None),
            P(),
            P(),
            P(),
            P(),
        ),
        out_specs=P("tile", "aux"),
        check_vma=False,
    )
```

```python
import functools
import jax
import jax.numpy as jnp
from jax import lax
from jax.experimental import pallas as pl
from jax.experimental.pallas import tpu as pltpu
from jax.sharding import PartitionSpec as P

MESH = pl.DeviceIdType.MESH
TILE = 128
CAP = 2
VMEM_BYTES = 56 * 1024 * 1024
RING = 8
CORES = 2
ORDER = 13
ROWS = (32, 48, 48)
SPANS = [(sum(ROWS[:r]), n) for r, n in enumerate(ROWS)]
BACK = (48, 40, 24, 16)
AHEAD = 3
BACK_SPANS = [(sum(BACK[:r]), n) for r, n in enumerate(BACK)]


def halves(x):
    top = x.astype(jnp.bfloat16)
    rest = (x - top.astype(jnp.float32)).astype(jnp.bfloat16)
    return top, rest


def ranks_of(keys):
    count = keys.shape[-1]
    spot = jnp.arange(count)
    earlier = spot[None, :] < spot[:, None]
    return jnp.sum((keys[..., :, None] == keys[..., None, :]) & earlier, axis=-1).astype(jnp.int32)


def slot_columns(keys, columns, wanted):
    ranking = ranks_of(keys)
    picked = []
    for level in range(CAP):
        chosen = (keys == wanted) & (ranking == level)
        picked.append(jnp.sum(jnp.where(chosen, columns + 1, 0), axis=-1) - 1)
    return jnp.stack(picked, axis=-1)


def spot_of(tile):
    return tile // (RING * CORES), lax.rem(tile // CORES, RING), lax.rem(tile, CORES)


def tile_of(x, z, core):
    return (x * RING + z) * CORES + core


def copy_at(tile):
    x, z, core = spot_of(tile)
    return tile_of(x, lax.rem(z + 3 + (RING - 6) * core, RING), core)


def copy_of(tile):
    x, z, core = spot_of(tile)
    return tile_of(x, lax.rem(z + RING - 3 - (RING - 6) * core, RING), core)


def reach(turn, core, copy):
    far = jnp.where(core == 0, RING - 2, 2)
    if copy:
        far = RING - far
    return jnp.where(turn == 3, far, jnp.where(turn == 2, RING - 1, turn))


def served(tile, k, n_tile, copy):
    x, z, core = spot_of(tile)
    across = n_tile // (RING * CORES)
    to_core = lax.rem(core + lax.rem(k, CORES), CORES)
    turn = lax.rem(k // CORES, 4)
    return tile_of(lax.rem(x + k // (4 * CORES), across), lax.rem(z + reach(turn, core, copy), RING), to_core)


def holder(tile, k, n_tile, copy):
    x, z, core = spot_of(tile)
    across = n_tile // (RING * CORES)
    from_core = lax.rem(core + CORES - lax.rem(k, CORES), CORES)
    turn = lax.rem(k // CORES, 4)
    z_from = lax.rem(z + RING - reach(turn, from_core, copy), RING)
    return tile_of(lax.rem(x + across - k // (4 * CORES), across), z_from, from_core)


def density_kernel(n_tile, n_aux, cols_ref, dens_ref, out_ref, *scratch):
    parts = len(ROWS)
    slabs, outgoing = scratch[:2 * parts], scratch[2 * parts:4 * parts]
    y_send, y_recv, z_send, z_recv, t_send, t_recv, own_sem = scratch[4 * parts:]
    me = lax.axis_index("tile")
    aux = lax.axis_index("aux")
    homes = [me] * parts + [copy_of(me)] * parts
    spans = SPANS * 2
    up, down = lax.rem(aux + 1, n_aux), lax.rem(aux + n_aux - 1, n_aux)
    across = lax.rem(aux + 2, n_aux)
    per = dens_ref.shape[1] // TILE
    half = per // 2
    peers = n_tile // 2
    barrier = pltpu.get_barrier_semaphore()

    @pl.loop(1, n_tile)
    def _(s):
        pl.semaphore_signal(barrier, inc=1, device_id={"tile": lax.rem(me + s, n_tile), "aux": aux}, device_id_type=MESH)

    for other in (up, down):
        pl.semaphore_signal(barrier, inc=1, device_id={"tile": me, "aux": other}, device_id_type=MESH)
    for r, (start, length) in enumerate(SPANS):
        for j in range(per):
            slabs[r][aux * per + j] = dens_ref[start:start + length, j * TILE:(j + 1) * TILE]
    pl.semaphore_wait(barrier, n_tile + 1)

    def near(r, owner, start, length, index, other):
        where = slabs[r].at[pl.ds(owner * per + start, length)]
        return pltpu.make_async_remote_copy(
            src_ref=where, dst_ref=where, send_sem=y_send.at[r, index], recv_sem=y_recv.at[r, index],
            device_id={"tile": me, "aux": other}, device_id_type=MESH)

    def swap(r):
        mine = pl.ds(aux * per, per)
        return pltpu.make_async_remote_copy(
            src_ref=slabs[r].at[mine], dst_ref=slabs[parts + r].at[mine], send_sem=z_send.at[r], recv_sem=z_recv.at[r],
            device_id={"tile": copy_at(me), "aux": aux}, device_id_type=MESH)

    def home_rows(tile, r):
        return out_ref.at[tile, :, pl.ds(*spans[r])]

    def ship(r, k):
        return pltpu.make_async_remote_copy(
            src_ref=outgoing[r].at[k], dst_ref=home_rows(homes[r], r),
            send_sem=t_send.at[r, k], recv_sem=t_recv.at[r, k],
            device_id={"tile": served(me, k, n_tile, r >= parts), "aux": aux}, device_id_type=MESH)

    def own(r):
        return pltpu.make_async_copy(outgoing[r].at[0], home_rows(homes[r], r), own_sem.at[r])

    def first(r):
        near(r, aux, 0, per, 0, up).start()
        near(r, aux, 0, per, 1, down).start()

    def second(r):
        near(r, down, 0, per, 0, up).wait_recv()
        near(r, down, 0, half, 2, up).start()
        near(r, up, 0, per, 1, down).wait_recv()
        near(r, up, half, half, 3, down).start()

    def gathered(r):
        near(r, across, 0, half, 2, up).wait_recv()
        near(r, across, half, half, 3, down).wait_recv()

    def send_all(r):
        base = 0 if r < parts else n_tile

        @pl.loop(0, peers)
        def _(s):
            k = lax.rem(s * ORDER, peers)
            dest = base + served(me, k, n_tile, r >= parts)
            for level in range(CAP):
                outgoing[r][k, level] = slabs[r][cols_ref[dest, level]]

            @pl.when(s > 0)
            def _():
                ship(r, k).start()

        own(r).start()

    def step_copy(r):
        swap(r).wait_recv()
        first(parts + r)

    for r in range(parts):
        first(r)
        swap(r).start()
    second(0)
    for r in range(2 * parts):
        gathered(r)
        if r + 1 < 2 * parts:
            second(r + 1)
        send_all(r)
        if r < parts:
            step_copy(r)

    for r in range(2 * parts):
        @pl.loop(1, peers)
        def _(k):
            source = holder(me, k, n_tile, r >= parts)
            home = source if r < parts else copy_of(source)
            pltpu.make_async_remote_copy(
                src_ref=outgoing[r].at[k], dst_ref=home_rows(home, r),
                send_sem=t_send.at[r, k], recv_sem=t_recv.at[r, k],
                device_id={"tile": source, "aux": aux}, device_id_type=MESH).wait_recv()
            ship(r, k).wait_send()

        own(r).wait()
        near(r, aux, 0, per, 0, up).wait_send()
        near(r, aux, 0, per, 1, down).wait_send()
        near(r, down, 0, half, 2, up).wait_send()
        near(r, up, half, half, 3, down).wait_send()
        if r < parts:
            swap(r).wait_send()


def fetch_density(density, cols, n_tile, n_aux):
    units = 2 * len(ROWS)
    return pl.pallas_call(
        functools.partial(density_kernel, n_tile, n_aux),
        out_shape=jax.ShapeDtypeStruct((n_tile, CAP, TILE, TILE), jnp.float32),
        in_specs=[pl.BlockSpec(memory_space=pltpu.SMEM), pl.BlockSpec(memory_space=pltpu.VMEM)],
        out_specs=pl.BlockSpec(memory_space=pl.ANY),
        scratch_shapes=[pltpu.VMEM((n_tile, n, TILE), jnp.float32) for n in ROWS * 2]
        + [pltpu.VMEM((n_tile // 2, CAP, n, TILE), jnp.float32) for n in ROWS * 2]
        + [
            pltpu.SemaphoreType.DMA((units, 4)),
            pltpu.SemaphoreType.DMA((units, 4)),
            pltpu.SemaphoreType.DMA((len(ROWS),)),
            pltpu.SemaphoreType.DMA((len(ROWS),)),
            pltpu.SemaphoreType.DMA((units, n_tile // 2)),
            pltpu.SemaphoreType.DMA((units, n_tile // 2)),
            pltpu.SemaphoreType.DMA((units,)),
        ],
        compiler_params=pltpu.CompilerParams(collective_id=0, has_side_effects=True, vmem_limit_bytes=VMEM_BYTES),
        name="fetch_density",
    )(cols, density)


def task_kernel(pair_count, table, dens_ref, fact_ref, out_ref, split, lhs):
    q = pl.program_id(0)
    last = pl.num_programs(0) - 2
    now = lax.rem(q, 2)

    @pl.when(q == 0)
    def _():
        lhs[1] = jnp.zeros(lhs.shape[1:], lhs.dtype)

        @pl.loop(0, fact_ref.shape[0])
        def _(slot):
            for p in range(pair_count):
                rows = slice(p * 2 * TILE, (p + 1) * 2 * TILE)
                top, rest = halves(fact_ref[slot, rows, :])
                split[slot, rows, 0:TILE] = top
                split[slot, rows, TILE:2 * TILE] = rest

    left, right = table[1, jnp.minimum(q, last)], table[2, jnp.maximum(q - 1, 0)]
    top, rest = halves(dens_ref[0])
    row = jnp.concatenate([top, rest], axis=1)
    weights = jnp.concatenate([row, row], axis=0)
    total = jnp.dot(lhs[1 - now], split[right], preferred_element_type=jnp.float32)
    for p in range(pair_count):
        rows = slice(p * 2 * TILE, (p + 1) * 2 * TILE)
        wide = jnp.dot(split[left, rows, :], weights, preferred_element_type=jnp.float32)
        top, rest = halves(wide[:, :TILE] + wide[:, TILE:])
        lhs[now, :, rows] = jnp.concatenate(
            [jnp.concatenate([top[:TILE], top[TILE:]], axis=1), jnp.concatenate([rest[:TILE], rest[TILE:]], axis=1)], axis=0)
    tall = total[:, :TILE] + total[:, TILE:]
    out_ref[0] = tall[:TILE] + tall[TILE:]


def run_tasks(table, incoming, factors, slots):
    slot_count, aux_funcs = factors.shape[:2]
    flat = factors.reshape(slot_count, aux_funcs * TILE, TILE)
    task_count = table.shape[1]
    return pl.pallas_call(
        functools.partial(task_kernel, aux_funcs // 2),
        out_shape=jax.ShapeDtypeStruct((slots, TILE, TILE), jnp.float32),
        grid_spec=pltpu.PrefetchScalarGridSpec(
            num_scalar_prefetch=1,
            grid=(task_count + 1,),
            in_specs=[
                pl.BlockSpec((1, TILE, TILE), lambda q, t: (t[0, jnp.minimum(q, task_count - 1)], 0, 0)),
                pl.BlockSpec(flat.shape, lambda q, t: (0, 0, 0), pipeline_mode=pl.Buffered(1)),
            ],
            out_specs=pl.BlockSpec((1, TILE, TILE), lambda q, t: (t[3, jnp.maximum(q - 1, 0)], 0, 0)),
            scratch_shapes=[
                pltpu.VMEM((slot_count, aux_funcs * TILE, 2 * TILE), jnp.bfloat16),
                pltpu.VMEM((2, 2 * TILE, aux_funcs * TILE), jnp.bfloat16),
            ],
        ),
        compiler_params=pltpu.CompilerParams(vmem_limit_bytes=VMEM_BYTES),
        name="run_tasks",
    )(table, incoming, flat)


def return_kernel(n_tile, n_aux, order_ref, src_ref, own_ref, mirror_ref, *scratch):
    parts = len(BACK)
    units = 2 * parts
    groups = [scratch[i * units:(i + 1) * units] for i in range(8)]
    arrived, rows, half_up, half_down, full_up, full_down, outgoing, summed = groups
    swapped = scratch[8 * units:8 * units + parts]
    (running, t_send, t_recv, y_send, y_recv, m_send, m_recv, z_send, z_recv, own_sem, out_sem) = scratch[8 * units + parts:]
    me = lax.axis_index("tile")
    aux = lax.axis_index("aux")
    up, down = lax.rem(aux + 1, n_aux), lax.rem(aux + n_aux - 1, n_aux)
    across = lax.rem(aux + 2, n_aux)
    per = n_tile // n_aux
    half = per // 2
    peers = n_tile // 2
    block = me // per
    slot = lax.rem(me, per)
    alike = block == aux
    barrier = pltpu.get_barrier_semaphore()

    @pl.loop(1, n_tile)
    def _(s):
        pl.semaphore_signal(barrier, inc=1, device_id={"tile": lax.rem(me + s, n_tile), "aux": aux}, device_id_type=MESH)

    for other in (up, down):
        pl.semaphore_signal(barrier, inc=1, device_id={"tile": me, "aux": other}, device_id_type=MESH)

    @pl.loop(0, per)
    def _(j):
        @pl.when(jnp.logical_not(alike & (j == slot)))
        def _():
            pl.semaphore_signal(barrier, inc=1, device_id={"tile": aux * per + j, "aux": block}, device_id_type=MESH)

    pl.semaphore_wait(barrier, n_tile + jnp.where(alike, per, per + 1))

    def span(u):
        return pl.ds(*BACK_SPANS[u // 2])

    def home_of(tile, u):
        return copy_of(tile) if u % 2 == 0 else tile

    def far(u, k):
        dest = holder(me, k, n_tile, u % 2 == 0)
        return pltpu.make_async_remote_copy(
            src_ref=src_ref.at[home_of(dest, u), :, span(u)], dst_ref=arrived[u].at[pl.ds(k * CAP, CAP)],
            send_sem=t_send.at[u, k], recv_sem=t_recv.at[u, k],
            device_id={"tile": dest, "aux": aux}, device_id_type=MESH)

    def own(u):
        return pltpu.make_async_copy(src_ref.at[home_of(me, u), :, span(u)], arrived[u].at[pl.ds(0, CAP)], own_sem.at[u])

    def begin(u):
        @pl.loop(1, peers)
        def _(s):
            far(u, lax.rem(s * ORDER, peers)).start()

        own(u).start()

    def near(src, dst, u, index, other):
        return pltpu.make_async_remote_copy(
            src_ref=src, dst_ref=dst, send_sem=y_send.at[u, index], recv_sem=y_recv.at[u, index],
            device_id={"tile": me, "aux": other}, device_id_type=MESH)

    def steps(u):
        return (
            near(rows[u].at[pl.ds(across * per, half)], half_up[u], u, 0, up),
            near(rows[u].at[pl.ds(across * per + half, half)], half_down[u], u, 1, down),
            near(outgoing[u].at[0], full_up[u], u, 2, up),
            near(outgoing[u].at[1], full_down[u], u, 3, down),
        )

    def swap(p):
        return pltpu.make_async_remote_copy(
            src_ref=summed[2 * p], dst_ref=swapped[p], send_sem=z_send.at[p], recv_sem=z_recv.at[p],
            device_id={"tile": copy_of(me), "aux": aux}, device_id_type=MESH)

    def send(u, j):
        return pltpu.make_async_remote_copy(
            src_ref=summed[u].at[j], dst_ref=mirror_ref.at[slot, span(u)],
            send_sem=m_send.at[u, j], recv_sem=m_recv.at[u, slot],
            device_id={"tile": aux * per + j, "aux": block}, device_id_type=MESH)

    def keep(u, j):
        return pltpu.make_async_copy(summed[u].at[j], mirror_ref.at[j, span(u)], m_send.at[u, j])

    def settle(u):
        return pltpu.make_async_copy(summed[u], own_ref.at[:, span(u)], out_sem.at[u // 2])

    def collect(u):
        length = BACK[u // 2]
        table = (u % 2) * 4

        @pl.loop(1, peers)
        def _(k):
            pltpu.make_async_remote_copy(
                src_ref=src_ref.at[me, :, span(u)], dst_ref=arrived[u].at[pl.ds(k * CAP, CAP)],
                send_sem=t_send.at[u, k], recv_sem=t_recv.at[u, k],
                device_id={"tile": served(me, k, n_tile, u % 2 == 0), "aux": aux}, device_id_type=MESH).wait_recv()

        own(u).wait()

        def add(i, carry):
            for v in range(4):
                k = i * 4 + v
                carry = jnp.where(order_ref[table + 1, k] > 0, 0.0, carry) + arrived[u][order_ref[table, k]]
                running[k, 0:length] = carry
            return carry

        lax.fori_loop(0, peers * CAP // 4, add, jnp.zeros((length, TILE), jnp.float32))

        @pl.loop(0, n_tile)
        def _(b):
            rows[u][b] = jnp.where(order_ref[table + 3, b] > 0, running[order_ref[table + 2, b], 0:length], 0.0)

        first_up, first_down, _, _ = steps(u)
        first_up.start()
        first_down.start()

        @pl.loop(0, half)
        def _(j):
            outgoing[u][0, half + j] = rows[u][up * per + half + j]
            outgoing[u][1, j] = rows[u][down * per + j]

    def pass_on(u):
        first_up, first_down, second_up, second_down = steps(u)
        first_up.wait_recv()

        @pl.loop(0, half)
        def _(j):
            outgoing[u][0, j] = rows[u][up * per + j] + half_up[u][j]

        second_up.start()
        first_down.wait_recv()

        @pl.loop(0, half)
        def _(j):
            outgoing[u][1, half + j] = rows[u][down * per + half + j] + half_down[u][j]

        second_down.start()

    def conclude(u):
        _, _, second_up, second_down = steps(u)
        second_up.wait_recv()
        second_down.wait_recv()
        if u % 2 == 0:
            @pl.loop(0, per)
            def _(j):
                summed[u][j] = rows[u][aux * per + j] + (full_up[u][j] + full_down[u][j])

            swap(u // 2).start()
        else:
            swap(u // 2).wait_recv()

            @pl.loop(0, per)
            def _(turn):
                j = lax.rem(slot + turn, per)
                summed[u][j] = (rows[u][aux * per + j] + swapped[u // 2][j]) + (full_up[u][j] + full_down[u][j])
                mine = alike & (j == slot)

                @pl.when(jnp.logical_not(mine))
                def _():
                    send(u, j).start()

                @pl.when(mine)
                def _():
                    keep(u, j).start()

            settle(u).start()

    for u in range(AHEAD):
        begin(u)
    for u in range(units):
        collect(u)
        if u > 0:
            conclude(u - 1)
        pass_on(u)
        if u + AHEAD < units:
            begin(u + AHEAD)
    conclude(units - 1)

    for u in range(units):
        @pl.loop(1, peers)
        def _(k):
            far(u, k).wait_send()

        for copy in steps(u):
            copy.wait_send()
        if u % 2 == 0:
            swap(u // 2).wait_send()
        else:
            @pl.loop(0, per)
            def _(j):
                mine = alike & (j == slot)

                @pl.when(jnp.logical_not(mine))
                def _():
                    pltpu.make_async_remote_copy(
                        src_ref=summed[u].at[j], dst_ref=mirror_ref.at[j, span(u)],
                        send_sem=m_send.at[u, j], recv_sem=m_recv.at[u, j],
                        device_id={"tile": aux * per + j, "aux": block}, device_id_type=MESH).wait_recv()
                    send(u, j).wait_send()

                @pl.when(mine)
                def _():
                    keep(u, j).wait()

            settle(u).wait()


def return_partials(order, outbound, n_tile, n_aux):
    per = n_tile // n_aux
    peers = n_tile // 2
    parts = len(BACK)
    units = 2 * parts
    lengths = [n for n in BACK for _ in range(2)]
    shape = jax.ShapeDtypeStruct((per, TILE, TILE), jnp.float32)
    leads = [(peers * CAP,), (n_tile,), (per // 2,), (per // 2,), (per,), (per,), (2, per), (per,)]
    return pl.pallas_call(
        functools.partial(return_kernel, n_tile, n_aux),
        out_shape=(shape, shape),
        in_specs=[pl.BlockSpec(memory_space=pltpu.SMEM), pl.BlockSpec(memory_space=pl.ANY)],
        out_specs=(pl.BlockSpec(memory_space=pl.ANY), pl.BlockSpec(memory_space=pl.ANY)),
        scratch_shapes=[pltpu.VMEM(lead + (n, TILE), jnp.float32) for lead in leads for n in lengths]
        + [pltpu.VMEM((per, n, TILE), jnp.float32) for n in BACK]
        + [
            pltpu.VMEM((peers * CAP, max(BACK), TILE), jnp.float32),
            pltpu.SemaphoreType.DMA((units, peers)),
            pltpu.SemaphoreType.DMA((units, peers)),
            pltpu.SemaphoreType.DMA((units, 4)),
            pltpu.SemaphoreType.DMA((units, 4)),
            pltpu.SemaphoreType.DMA((units, per)),
            pltpu.SemaphoreType.DMA((units, per)),
            pltpu.SemaphoreType.DMA((parts,)),
            pltpu.SemaphoreType.DMA((parts,)),
            pltpu.SemaphoreType.DMA((units,)),
            pltpu.SemaphoreType.DMA((parts,)),
        ],
        compiler_params=pltpu.CompilerParams(collective_id=1, has_side_effects=True, vmem_limit_bytes=VMEM_BYTES),
        name="return_partials",
    )(order, outbound)


def stacked(x, axis):
    return jnp.concatenate(halves(x), axis=axis)


def folded(x):
    tall = x[:, :TILE] + x[:, TILE:]
    return tall[:TILE] + tall[TILE:]


def finish_kernel(group, place, own_ref, mirror_ref, left_ref, right_ref, out_ref):
    left = stacked(jnp.transpose(left_ref[...]), 0)
    for i in range(group):
        symmetric = own_ref[i] + jnp.transpose(mirror_ref[i])
        leftward = folded(jnp.dot(left, stacked(symmetric, 1), preferred_element_type=jnp.float32))
        right = stacked(right_ref[i * TILE:(i + 1) * TILE, :], 1)
        out_ref[:, i * TILE:(i + 1) * TILE] = folded(
            jnp.dot(stacked(leftward, 0), right, preferred_element_type=jnp.float32))


def finish(place, own, mirror, orthogonalizers):
    per = own.shape[0]
    group = 4
    steps = per // group
    tile = pl.BlockSpec((group, TILE, TILE), lambda j, t: (j, 0, 0))
    return pl.pallas_call(
        functools.partial(finish_kernel, group),
        out_shape=jax.ShapeDtypeStruct((TILE, per * TILE), jnp.float32),
        grid_spec=pltpu.PrefetchScalarGridSpec(
            num_scalar_prefetch=1,
            grid=(steps,),
            in_specs=[
                tile, tile,
                pl.BlockSpec((TILE, TILE), lambda j, t: (t[0], 0)),
                pl.BlockSpec((group * TILE, TILE), lambda j, t: (t[1] * steps + j, 0)),
            ],
            out_specs=pl.BlockSpec((TILE, group * TILE), lambda j, t: (0, j)),
        ),
        name="finish",
    )(place, own, mirror, orthogonalizers, orthogonalizers)


def column_order(cols, n_tile):
    count = cols.shape[0]
    spot = jnp.arange(count, dtype=jnp.int32)
    key = jnp.where(cols < 0, n_tile, cols)
    before = (key[None, :] < key[:, None]) | ((key[None, :] == key[:, None]) & (spot[None, :] < spot[:, None]))
    place = jnp.sum(before, axis=1)
    at = place[None, :] == spot[:, None]
    order = jnp.sum(jnp.where(at, spot[None, :], 0), axis=1)
    starts = jnp.any(at & (~jnp.any(before & (key[None, :] == key[:, None]), axis=1))[None, :], axis=1)
    ends = jnp.sum(key[None, :] <= spot[:, None], axis=1) - 1
    held = jnp.any(key[None, :] == spot[:, None], axis=1) & (spot < n_tile)
    return jnp.stack([order, starts.astype(jnp.int32), jnp.maximum(ends, 0), held.astype(jnp.int32)]).astype(jnp.int32)


def local(density, factors, orthogonalizers, slot_pairs, density_source, density_column, target_row, target_column):
    n_tile, n_aux = lax.axis_size("tile"), lax.axis_size("aux")
    me, aux = lax.axis_index("tile"), lax.axis_index("aux")
    tasks = slot_pairs.shape[0]

    packed = density_source
    for other in (density_column, target_row, target_column):
        packed = packed * n_tile + other
    packed = lax.dynamic_index_in_dim(packed.reshape(n_tile, n_aux, tasks), aux, 1, False)
    target_cols = packed % n_tile
    targets = (packed // n_tile) % n_tile
    columns = (packed // n_tile ** 2) % n_tile
    sources = packed // n_tile ** 3
    own_source = lax.dynamic_index_in_dim(sources, me, 0, False)
    own_target = lax.dynamic_index_in_dim(targets, me, 0, False)
    send_cols = jnp.concatenate([slot_columns(sources, columns, me), slot_columns(sources, columns, copy_of(me))])
    places = jnp.arange(n_tile, dtype=jnp.int32)

    def order_for(row, copy):
        slot_cols = slot_columns(targets, target_cols, row)
        pick = served(me, places[:n_tile // 2], n_tile, copy)[:, None] == places[None, :]
        cols = jnp.sum(jnp.where(pick[:, :, None], slot_cols[None] + 1, 0), axis=1) - 1
        return column_order(cols.reshape(-1), n_tile)

    table = jnp.stack([
        own_source * CAP + ranks_of(own_source),
        slot_pairs[:, 0],
        slot_pairs[:, 1],
        own_target * CAP + ranks_of(own_target),
    ])
    slots = n_tile * CAP
    incoming = fetch_density(density, jnp.maximum(send_cols, 0), n_tile, n_aux)
    outbound = run_tasks(table, incoming.reshape(slots, TILE, TILE), factors, slots)
    own, mirror = return_partials(
        jnp.concatenate([order_for(copy_of(me), True), order_for(me, False)]), outbound.reshape(n_tile, CAP, TILE, TILE), n_tile, n_aux)
    return finish(jnp.stack([me, aux]).astype(jnp.int32), own, mirror, orthogonalizers)


def solution(mesh):
    return jax.shard_map(
        local,
        mesh=mesh,
        in_specs=(
            P("tile", "aux"),
            P(("tile", "aux"), None, None, None),
            P(),
            P(("tile", "aux"), None),
            P(),
            P(),
            P(),
            P(),
        ),
        out_specs=P("tile", "aux"),
        check_vma=False,
    )
```

```python
import functools
import jax
import jax.numpy as jnp
from jax import lax
from jax.experimental import pallas as pl
from jax.experimental.pallas import tpu as pltpu
from jax.sharding import PartitionSpec as P

MESH = pl.DeviceIdType.MESH
TILE = 128
CAP = 2
VMEM_BYTES = 56 * 1024 * 1024
RING = 8
CORES = 2
ORDER = 13
ROWS = (48, 80)
SPANS = [(sum(ROWS[:r]), n) for r, n in enumerate(ROWS)]
BACK = (48, 40, 24, 16)
AHEAD = 2
BACK_SPANS = [(sum(BACK[:r]), n) for r, n in enumerate(BACK)]


def halves(x):
    top = x.astype(jnp.bfloat16)
    rest = (x - top.astype(jnp.float32)).astype(jnp.bfloat16)
    return top, rest


def ranks_of(keys):
    count = keys.shape[-1]
    spot = jnp.arange(count)
    earlier = spot[None, :] < spot[:, None]
    return jnp.sum((keys[..., :, None] == keys[..., None, :]) & earlier, axis=-1).astype(jnp.int32)


def slot_columns(keys, columns, wanted):
    ranking = ranks_of(keys)
    picked = []
    for level in range(CAP):
        chosen = (keys == wanted) & (ranking == level)
        picked.append(jnp.sum(jnp.where(chosen, columns + 1, 0), axis=-1) - 1)
    return jnp.stack(picked, axis=-1)


def spot_of(tile):
    return tile // (RING * CORES), lax.rem(tile // CORES, RING), lax.rem(tile, CORES)


def tile_of(x, z, core):
    return (x * RING + z) * CORES + core


def copy_at(tile):
    x, z, core = spot_of(tile)
    return tile_of(x, lax.rem(z + 3 + (RING - 6) * core, RING), core)


def copy_of(tile):
    x, z, core = spot_of(tile)
    return tile_of(x, lax.rem(z + RING - 3 - (RING - 6) * core, RING), core)


def reach(turn, core, copy):
    far = jnp.where(core == 0, RING - 2, 2)
    if copy:
        far = RING - far
    return jnp.where(turn == 3, far, jnp.where(turn == 2, RING - 1, turn))


def served(tile, k, n_tile, copy):
    x, z, core = spot_of(tile)
    across = n_tile // (RING * CORES)
    to_core = lax.rem(core + lax.rem(k, CORES), CORES)
    turn = lax.rem(k // CORES, 4)
    return tile_of(lax.rem(x + k // (4 * CORES), across), lax.rem(z + reach(turn, core, copy), RING), to_core)


def holder(tile, k, n_tile, copy):
    x, z, core = spot_of(tile)
    across = n_tile // (RING * CORES)
    from_core = lax.rem(core + CORES - lax.rem(k, CORES), CORES)
    turn = lax.rem(k // CORES, 4)
    z_from = lax.rem(z + RING - reach(turn, from_core, copy), RING)
    return tile_of(lax.rem(x + across - k // (4 * CORES), across), z_from, from_core)


def density_kernel(n_tile, n_aux, cols_ref, dens_ref, out_ref, *scratch):
    parts = len(ROWS)
    slabs, outgoing = scratch[:2 * parts], scratch[2 * parts:4 * parts]
    y_send, y_recv, z_send, z_recv, t_send, t_recv, own_sem = scratch[4 * parts:]
    me = lax.axis_index("tile")
    aux = lax.axis_index("aux")
    homes = [me] * parts + [copy_of(me)] * parts
    spans = SPANS * 2
    up, down = lax.rem(aux + 1, n_aux), lax.rem(aux + n_aux - 1, n_aux)
    across = lax.rem(aux + 2, n_aux)
    per = dens_ref.shape[1] // TILE
    half = per // 2
    peers = n_tile // 2
    barrier = pltpu.get_barrier_semaphore()

    @pl.loop(1, n_tile)
    def _(s):
        pl.semaphore_signal(barrier, inc=1, device_id={"tile": lax.rem(me + s, n_tile), "aux": aux}, device_id_type=MESH)

    for other in (up, down):
        pl.semaphore_signal(barrier, inc=1, device_id={"tile": me, "aux": other}, device_id_type=MESH)
    for r, (start, length) in enumerate(SPANS):
        for j in range(per):
            slabs[r][aux * per + j] = dens_ref[start:start + length, j * TILE:(j + 1) * TILE]
    pl.semaphore_wait(barrier, n_tile + 1)

    def near(r, owner, start, length, index, other):
        where = slabs[r].at[pl.ds(owner * per + start, length)]
        return pltpu.make_async_remote_copy(
            src_ref=where, dst_ref=where, send_sem=y_send.at[r, index], recv_sem=y_recv.at[r, index],
            device_id={"tile": me, "aux": other}, device_id_type=MESH)

    def swap(r):
        mine = pl.ds(aux * per, per)
        return pltpu.make_async_remote_copy(
            src_ref=slabs[r].at[mine], dst_ref=slabs[parts + r].at[mine], send_sem=z_send.at[r], recv_sem=z_recv.at[r],
            device_id={"tile": copy_at(me), "aux": aux}, device_id_type=MESH)

    def home_rows(tile, r):
        return out_ref.at[tile, :, pl.ds(*spans[r])]

    def ship(r, k):
        return pltpu.make_async_remote_copy(
            src_ref=outgoing[r].at[k], dst_ref=home_rows(homes[r], r),
            send_sem=t_send.at[r, k], recv_sem=t_recv.at[r, k],
            device_id={"tile": served(me, k, n_tile, r >= parts), "aux": aux}, device_id_type=MESH)

    def own(r):
        return pltpu.make_async_copy(outgoing[r].at[0], home_rows(homes[r], r), own_sem.at[r])

    def first(r):
        near(r, aux, 0, per, 0, up).start()
        near(r, aux, 0, per, 1, down).start()

    def second(r):
        near(r, down, 0, per, 0, up).wait_recv()
        near(r, down, 0, half, 2, up).start()
        near(r, up, 0, per, 1, down).wait_recv()
        near(r, up, half, half, 3, down).start()

    def gathered(r):
        near(r, across, 0, half, 2, up).wait_recv()
        near(r, across, half, half, 3, down).wait_recv()

    def send_all(r):
        base = 0 if r < parts else n_tile

        @pl.loop(0, peers)
        def _(s):
            k = lax.rem(s * ORDER, peers)
            dest = base + served(me, k, n_tile, r >= parts)
            for level in range(CAP):
                outgoing[r][k, level] = slabs[r][cols_ref[dest, level]]

            @pl.when(s > 0)
            def _():
                ship(r, k).start()

        own(r).start()

    def step_copy(r):
        swap(r).wait_recv()
        first(parts + r)

    for r in range(parts):
        first(r)
        swap(r).start()
    second(0)
    for r in range(2 * parts):
        gathered(r)
        if r + 1 < 2 * parts:
            second(r + 1)
        send_all(r)
        if r < parts:
            step_copy(r)

    for r in range(2 * parts):
        @pl.loop(1, peers)
        def _(k):
            source = holder(me, k, n_tile, r >= parts)
            home = source if r < parts else copy_of(source)
            pltpu.make_async_remote_copy(
                src_ref=outgoing[r].at[k], dst_ref=home_rows(home, r),
                send_sem=t_send.at[r, k], recv_sem=t_recv.at[r, k],
                device_id={"tile": source, "aux": aux}, device_id_type=MESH).wait_recv()
            ship(r, k).wait_send()

        own(r).wait()
        near(r, aux, 0, per, 0, up).wait_send()
        near(r, aux, 0, per, 1, down).wait_send()
        near(r, down, 0, half, 2, up).wait_send()
        near(r, up, half, half, 3, down).wait_send()
        if r < parts:
            swap(r).wait_send()


def fetch_density(density, cols, n_tile, n_aux):
    units = 2 * len(ROWS)
    return pl.pallas_call(
        functools.partial(density_kernel, n_tile, n_aux),
        out_shape=jax.ShapeDtypeStruct((n_tile, CAP, TILE, TILE), jnp.float32),
        in_specs=[pl.BlockSpec(memory_space=pltpu.SMEM), pl.BlockSpec(memory_space=pltpu.VMEM)],
        out_specs=pl.BlockSpec(memory_space=pl.ANY),
        scratch_shapes=[pltpu.VMEM((n_tile, n, TILE), jnp.float32) for n in ROWS * 2]
        + [pltpu.VMEM((n_tile // 2, CAP, n, TILE), jnp.float32) for n in ROWS * 2]
        + [
            pltpu.SemaphoreType.DMA((units, 4)),
            pltpu.SemaphoreType.DMA((units, 4)),
            pltpu.SemaphoreType.DMA((len(ROWS),)),
            pltpu.SemaphoreType.DMA((len(ROWS),)),
            pltpu.SemaphoreType.DMA((units, n_tile // 2)),
            pltpu.SemaphoreType.DMA((units, n_tile // 2)),
            pltpu.SemaphoreType.DMA((units,)),
        ],
        compiler_params=pltpu.CompilerParams(collective_id=0, has_side_effects=True, vmem_limit_bytes=VMEM_BYTES),
        name="fetch_density",
    )(cols, density)


def task_kernel(pair_count, table, dens_ref, fact_ref, out_ref, split, lhs):
    q = pl.program_id(0)
    last = pl.num_programs(0) - 2
    now = lax.rem(q, 2)

    @pl.when(q == 0)
    def _():
        lhs[1] = jnp.zeros(lhs.shape[1:], lhs.dtype)

        @pl.loop(0, fact_ref.shape[0])
        def _(slot):
            for p in range(pair_count):
                rows = slice(p * 2 * TILE, (p + 1) * 2 * TILE)
                top, rest = halves(fact_ref[slot, rows, :])
                split[slot, rows, 0:TILE] = top
                split[slot, rows, TILE:2 * TILE] = rest

    left, right = table[1, jnp.minimum(q, last)], table[2, jnp.maximum(q - 1, 0)]
    top, rest = halves(dens_ref[0])
    row = jnp.concatenate([top, rest], axis=1)
    weights = jnp.concatenate([row, row], axis=0)
    total = jnp.dot(lhs[1 - now], split[right], preferred_element_type=jnp.float32)
    for p in range(pair_count):
        rows = slice(p * 2 * TILE, (p + 1) * 2 * TILE)
        wide = jnp.dot(split[left, rows, :], weights, preferred_element_type=jnp.float32)
        top, rest = halves(wide[:, :TILE] + wide[:, TILE:])
        lhs[now, :, rows] = jnp.concatenate(
            [jnp.concatenate([top[:TILE], top[TILE:]], axis=1), jnp.concatenate([rest[:TILE], rest[TILE:]], axis=1)], axis=0)
    tall = total[:, :TILE] + total[:, TILE:]
    out_ref[0] = tall[:TILE] + tall[TILE:]


def run_tasks(table, incoming, factors, slots):
    slot_count, aux_funcs = factors.shape[:2]
    flat = factors.reshape(slot_count, aux_funcs * TILE, TILE)
    task_count = table.shape[1]
    return pl.pallas_call(
        functools.partial(task_kernel, aux_funcs // 2),
        out_shape=jax.ShapeDtypeStruct((slots, TILE, TILE), jnp.float32),
        grid_spec=pltpu.PrefetchScalarGridSpec(
            num_scalar_prefetch=1,
            grid=(task_count + 1,),
            in_specs=[
                pl.BlockSpec((1, TILE, TILE), lambda q, t: (t[0, jnp.minimum(q, task_count - 1)], 0, 0)),
                pl.BlockSpec(flat.shape, lambda q, t: (0, 0, 0), pipeline_mode=pl.Buffered(1)),
            ],
            out_specs=pl.BlockSpec((1, TILE, TILE), lambda q, t: (t[3, jnp.maximum(q - 1, 0)], 0, 0)),
            scratch_shapes=[
                pltpu.VMEM((slot_count, aux_funcs * TILE, 2 * TILE), jnp.bfloat16),
                pltpu.VMEM((2, 2 * TILE, aux_funcs * TILE), jnp.bfloat16),
            ],
        ),
        compiler_params=pltpu.CompilerParams(vmem_limit_bytes=VMEM_BYTES),
        name="run_tasks",
    )(table, incoming, flat)


def return_kernel(n_tile, n_aux, order_ref, src_ref, own_ref, mirror_ref, *scratch):
    parts = len(BACK)
    units = 2 * parts
    groups = [scratch[i * units:(i + 1) * units] for i in range(8)]
    arrived, rows, half_up, half_down, full_up, full_down, outgoing, summed = groups
    swapped = scratch[8 * units:8 * units + parts]
    (running, t_send, t_recv, y_send, y_recv, m_send, m_recv, z_send, z_recv, own_sem, out_sem) = scratch[8 * units + parts:]
    me = lax.axis_index("tile")
    aux = lax.axis_index("aux")
    up, down = lax.rem(aux + 1, n_aux), lax.rem(aux + n_aux - 1, n_aux)
    across = lax.rem(aux + 2, n_aux)
    per = n_tile // n_aux
    half = per // 2
    peers = n_tile // 2
    block = me // per
    slot = lax.rem(me, per)
    alike = block == aux
    barrier = pltpu.get_barrier_semaphore()

    @pl.loop(1, n_tile)
    def _(s):
        pl.semaphore_signal(barrier, inc=1, device_id={"tile": lax.rem(me + s, n_tile), "aux": aux}, device_id_type=MESH)

    for other in (up, down):
        pl.semaphore_signal(barrier, inc=1, device_id={"tile": me, "aux": other}, device_id_type=MESH)

    @pl.loop(0, per)
    def _(j):
        @pl.when(jnp.logical_not(alike & (j == slot)))
        def _():
            pl.semaphore_signal(barrier, inc=1, device_id={"tile": aux * per + j, "aux": block}, device_id_type=MESH)

    pl.semaphore_wait(barrier, n_tile + jnp.where(alike, per, per + 1))

    def span(u):
        return pl.ds(*BACK_SPANS[u // 2])

    def home_of(tile, u):
        return copy_of(tile) if u % 2 == 0 else tile

    def far(u, k):
        dest = holder(me, k, n_tile, u % 2 == 0)
        return pltpu.make_async_remote_copy(
            src_ref=src_ref.at[home_of(dest, u), :, span(u)], dst_ref=arrived[u].at[pl.ds(k * CAP, CAP)],
            send_sem=t_send.at[u, k], recv_sem=t_recv.at[u, k],
            device_id={"tile": dest, "aux": aux}, device_id_type=MESH)

    def own(u):
        return pltpu.make_async_copy(src_ref.at[home_of(me, u), :, span(u)], arrived[u].at[pl.ds(0, CAP)], own_sem.at[u])

    def begin(u):
        @pl.loop(1, peers)
        def _(s):
            far(u, lax.rem(s * ORDER, peers)).start()

        own(u).start()

    def near(src, dst, u, index, other):
        return pltpu.make_async_remote_copy(
            src_ref=src, dst_ref=dst, send_sem=y_send.at[u, index], recv_sem=y_recv.at[u, index],
            device_id={"tile": me, "aux": other}, device_id_type=MESH)

    def steps(u):
        return (
            near(rows[u].at[pl.ds(across * per, half)], half_up[u], u, 0, up),
            near(rows[u].at[pl.ds(across * per + half, half)], half_down[u], u, 1, down),
            near(outgoing[u].at[0], full_up[u], u, 2, up),
            near(outgoing[u].at[1], full_down[u], u, 3, down),
        )

    def swap(p):
        return pltpu.make_async_remote_copy(
            src_ref=summed[2 * p], dst_ref=swapped[p], send_sem=z_send.at[p], recv_sem=z_recv.at[p],
            device_id={"tile": copy_of(me), "aux": aux}, device_id_type=MESH)

    def send(u, j):
        return pltpu.make_async_remote_copy(
            src_ref=summed[u].at[j], dst_ref=mirror_ref.at[slot, span(u)],
            send_sem=m_send.at[u, j], recv_sem=m_recv.at[u, slot],
            device_id={"tile": aux * per + j, "aux": block}, device_id_type=MESH)

    def keep(u, j):
        return pltpu.make_async_copy(summed[u].at[j], mirror_ref.at[j, span(u)], m_send.at[u, j])

    def settle(u):
        return pltpu.make_async_copy(summed[u], own_ref.at[:, span(u)], out_sem.at[u // 2])

    def collect(u):
        length = BACK[u // 2]
        table = (u % 2) * 4

        @pl.loop(1, peers)
        def _(k):
            pltpu.make_async_remote_copy(
                src_ref=src_ref.at[me, :, span(u)], dst_ref=arrived[u].at[pl.ds(k * CAP, CAP)],
                send_sem=t_send.at[u, k], recv_sem=t_recv.at[u, k],
                device_id={"tile": served(me, k, n_tile, u % 2 == 0), "aux": aux}, device_id_type=MESH).wait_recv()

        own(u).wait()
        if u + AHEAD < units:
            begin(u + AHEAD)

        def add(i, carry):
            for v in range(4):
                k = i * 4 + v
                carry = jnp.where(order_ref[table + 1, k] > 0, 0.0, carry) + arrived[u][order_ref[table, k]]
                running[k, 0:length] = carry
            return carry

        lax.fori_loop(0, peers * CAP // 4, add, jnp.zeros((length, TILE), jnp.float32))

        @pl.loop(0, n_tile)
        def _(b):
            rows[u][b] = jnp.where(order_ref[table + 3, b] > 0, running[order_ref[table + 2, b], 0:length], 0.0)

        first_up, first_down, _, _ = steps(u)
        first_up.start()
        first_down.start()

        @pl.loop(0, half)
        def _(j):
            outgoing[u][0, half + j] = rows[u][up * per + half + j]
            outgoing[u][1, j] = rows[u][down * per + j]

    def pass_on(u):
        first_up, first_down, second_up, second_down = steps(u)
        first_up.wait_recv()

        @pl.loop(0, half)
        def _(j):
            outgoing[u][0, j] = rows[u][up * per + j] + half_up[u][j]

        second_up.start()
        first_down.wait_recv()

        @pl.loop(0, half)
        def _(j):
            outgoing[u][1, half + j] = rows[u][down * per + half + j] + half_down[u][j]

        second_down.start()

    def conclude(u):
        _, _, second_up, second_down = steps(u)
        second_up.wait_recv()
        second_down.wait_recv()
        if u % 2 == 0:
            @pl.loop(0, per)
            def _(j):
                summed[u][j] = rows[u][aux * per + j] + (full_up[u][j] + full_down[u][j])

            swap(u // 2).start()
        else:
            swap(u // 2).wait_recv()

            @pl.loop(0, per)
            def _(turn):
                j = lax.rem(slot + turn, per)
                summed[u][j] = (rows[u][aux * per + j] + swapped[u // 2][j]) + (full_up[u][j] + full_down[u][j])
                mine = alike & (j == slot)

                @pl.when(jnp.logical_not(mine))
                def _():
                    send(u, j).start()

                @pl.when(mine)
                def _():
                    keep(u, j).start()

            settle(u).start()

    for u in range(AHEAD):
        begin(u)
    for u in range(units):
        collect(u)
        if u > 0:
            conclude(u - 1)
        pass_on(u)
    conclude(units - 1)

    for u in range(units):
        @pl.loop(1, peers)
        def _(k):
            far(u, k).wait_send()

        for copy in steps(u):
            copy.wait_send()
        if u % 2 == 0:
            swap(u // 2).wait_send()
        else:
            @pl.loop(0, per)
            def _(j):
                mine = alike & (j == slot)

                @pl.when(jnp.logical_not(mine))
                def _():
                    pltpu.make_async_remote_copy(
                        src_ref=summed[u].at[j], dst_ref=mirror_ref.at[j, span(u)],
                        send_sem=m_send.at[u, j], recv_sem=m_recv.at[u, j],
                        device_id={"tile": aux * per + j, "aux": block}, device_id_type=MESH).wait_recv()
                    send(u, j).wait_send()

                @pl.when(mine)
                def _():
                    keep(u, j).wait()

            settle(u).wait()


def return_partials(order, outbound, n_tile, n_aux):
    per = n_tile // n_aux
    peers = n_tile // 2
    parts = len(BACK)
    units = 2 * parts
    lengths = [n for n in BACK for _ in range(2)]
    shape = jax.ShapeDtypeStruct((per, TILE, TILE), jnp.float32)
    leads = [(peers * CAP,), (n_tile,), (per // 2,), (per // 2,), (per,), (per,), (2, per), (per,)]
    return pl.pallas_call(
        functools.partial(return_kernel, n_tile, n_aux),
        out_shape=(shape, shape),
        in_specs=[pl.BlockSpec(memory_space=pltpu.SMEM), pl.BlockSpec(memory_space=pl.ANY)],
        out_specs=(pl.BlockSpec(memory_space=pl.ANY), pl.BlockSpec(memory_space=pl.ANY)),
        scratch_shapes=[pltpu.VMEM(lead + (n, TILE), jnp.float32) for lead in leads for n in lengths]
        + [pltpu.VMEM((per, n, TILE), jnp.float32) for n in BACK]
        + [
            pltpu.VMEM((peers * CAP, max(BACK), TILE), jnp.float32),
            pltpu.SemaphoreType.DMA((units, peers)),
            pltpu.SemaphoreType.DMA((units, peers)),
            pltpu.SemaphoreType.DMA((units, 4)),
            pltpu.SemaphoreType.DMA((units, 4)),
            pltpu.SemaphoreType.DMA((units, per)),
            pltpu.SemaphoreType.DMA((units, per)),
            pltpu.SemaphoreType.DMA((parts,)),
            pltpu.SemaphoreType.DMA((parts,)),
            pltpu.SemaphoreType.DMA((units,)),
            pltpu.SemaphoreType.DMA((parts,)),
        ],
        compiler_params=pltpu.CompilerParams(collective_id=1, has_side_effects=True, vmem_limit_bytes=VMEM_BYTES),
        name="return_partials",
    )(order, outbound)


def stacked(x, axis):
    return jnp.concatenate(halves(x), axis=axis)


def folded(x):
    tall = x[:, :TILE] + x[:, TILE:]
    return tall[:TILE] + tall[TILE:]


def finish_kernel(group, place, own_ref, mirror_ref, left_ref, right_ref, out_ref):
    left = stacked(jnp.transpose(left_ref[...]), 0)
    for i in range(group):
        symmetric = own_ref[i] + jnp.transpose(mirror_ref[i])
        leftward = folded(jnp.dot(left, stacked(symmetric, 1), preferred_element_type=jnp.float32))
        right = stacked(right_ref[i * TILE:(i + 1) * TILE, :], 1)
        out_ref[:, i * TILE:(i + 1) * TILE] = folded(
            jnp.dot(stacked(leftward, 0), right, preferred_element_type=jnp.float32))


def finish(place, own, mirror, orthogonalizers):
    per = own.shape[0]
    group = 8
    steps = per // group
    tile = pl.BlockSpec((group, TILE, TILE), lambda j, t: (j, 0, 0))
    return pl.pallas_call(
        functools.partial(finish_kernel, group),
        out_shape=jax.ShapeDtypeStruct((TILE, per * TILE), jnp.float32),
        grid_spec=pltpu.PrefetchScalarGridSpec(
            num_scalar_prefetch=1,
            grid=(steps,),
            in_specs=[
                tile, tile,
                pl.BlockSpec((TILE, TILE), lambda j, t: (t[0], 0)),
                pl.BlockSpec((group * TILE, TILE), lambda j, t: (t[1] * steps + j, 0)),
            ],
            out_specs=pl.BlockSpec((TILE, group * TILE), lambda j, t: (0, j)),
        ),
        name="finish",
    )(place, own, mirror, orthogonalizers, orthogonalizers)


def column_order(cols, n_tile):
    count = cols.shape[0]
    spot = jnp.arange(count, dtype=jnp.int32)
    key = jnp.where(cols < 0, n_tile, cols)
    before = (key[None, :] < key[:, None]) | ((key[None, :] == key[:, None]) & (spot[None, :] < spot[:, None]))
    place = jnp.sum(before, axis=1)
    at = place[None, :] == spot[:, None]
    order = jnp.sum(jnp.where(at, spot[None, :], 0), axis=1)
    starts = jnp.any(at & (~jnp.any(before & (key[None, :] == key[:, None]), axis=1))[None, :], axis=1)
    ends = jnp.sum(key[None, :] <= spot[:, None], axis=1) - 1
    held = jnp.any(key[None, :] == spot[:, None], axis=1) & (spot < n_tile)
    return jnp.stack([order, starts.astype(jnp.int32), jnp.maximum(ends, 0), held.astype(jnp.int32)]).astype(jnp.int32)


def local(density, factors, orthogonalizers, slot_pairs, density_source, density_column, target_row, target_column):
    n_tile, n_aux = lax.axis_size("tile"), lax.axis_size("aux")
    me, aux = lax.axis_index("tile"), lax.axis_index("aux")
    tasks = slot_pairs.shape[0]

    packed = density_source
    for other in (density_column, target_row, target_column):
        packed = packed * n_tile + other
    packed = lax.dynamic_index_in_dim(packed.reshape(n_tile, n_aux, tasks), aux, 1, False)
    target_cols = packed % n_tile
    targets = (packed // n_tile) % n_tile
    columns = (packed // n_tile ** 2) % n_tile
    sources = packed // n_tile ** 3
    own_source = lax.dynamic_index_in_dim(sources, me, 0, False)
    own_target = lax.dynamic_index_in_dim(targets, me, 0, False)
    send_cols = jnp.concatenate([slot_columns(sources, columns, me), slot_columns(sources, columns, copy_of(me))])
    places = jnp.arange(n_tile, dtype=jnp.int32)

    def order_for(row, copy):
        slot_cols = slot_columns(targets, target_cols, row)
        pick = served(me, places[:n_tile // 2], n_tile, copy)[:, None] == places[None, :]
        cols = jnp.sum(jnp.where(pick[:, :, None], slot_cols[None] + 1, 0), axis=1) - 1
        return column_order(cols.reshape(-1), n_tile)

    table = jnp.stack([
        own_source * CAP + ranks_of(own_source),
        slot_pairs[:, 0],
        slot_pairs[:, 1],
        own_target * CAP + ranks_of(own_target),
    ])
    slots = n_tile * CAP
    incoming = fetch_density(density, jnp.maximum(send_cols, 0), n_tile, n_aux)
    outbound = run_tasks(table, incoming.reshape(slots, TILE, TILE), factors, slots)
    own, mirror = return_partials(
        jnp.concatenate([order_for(copy_of(me), True), order_for(me, False)]), outbound.reshape(n_tile, CAP, TILE, TILE), n_tile, n_aux)
    return finish(jnp.stack([me, aux]).astype(jnp.int32), own, mirror, orthogonalizers)


def solution(mesh):
    return jax.shard_map(
        local,
        mesh=mesh,
        in_specs=(
            P("tile", "aux"),
            P(("tile", "aux"), None, None, None),
            P(),
            P(("tile", "aux"), None),
            P(),
            P(),
            P(),
            P(),
        ),
        out_specs=P("tile", "aux"),
        check_vma=False,
    )
```
